32 devices in a mesh: groups: 2 (over x), utt: 16 (over z, y, core).
Axes of the slice: x: 2, y: 2, z: 4, core: 2. Of those that a mesh axis runs over, the one named last changes fastest.
Arguments:
- waveforms: float32 [64, 90], P(('groups', 'utt')), parts along dimension 0, may hold values from -6 to 6
- lengths: int32 [64], P(('groups', 'utt')), parts along dimension 0, may hold values from 1 to 7, as said below
- take_list: int32 [64], P(('groups', 'utt')), parts along dimension 0, may hold values from 0 to 31, as said below
- conv_first: float32 [3, 10, 512], replicated, may hold values from -2 to 2
- conv_second: bfloat16 [3, 1536, 512], replicated, may hold values from -0.15625 to 0.15625
- norm_gain: float32 [3, 2, 512], replicated, may hold values from 0.5 to 1.5
- norm_shift: float32 [3, 2, 512], replicated, may hold values from -2 to 2
- enc_weight: bfloat16 [1536, 8192], P(None, 'utt'), may hold values from -0.15625 to 0.15625
- enc_bias: float32 [8192], P('utt'), may hold values from -2 to 2
- dec_weight: bfloat16 [8192, 1536], P('utt'), may hold values from -0.0625 to 0.0625
- dec_bias: float32 [1536], replicated, may hold values from -2 to 2
Outputs:
- enc_grad: bfloat16 [3072, 8192], P('groups', 'utt'), parts along dimension 0
- dec_grad: bfloat16 [16384, 1536], P(('groups', 'utt')), parts along dimension 0
- enc_bias_grad: float32 [16384], P(('groups', 'utt')), parts along dimension 0
- dec_bias_grad: float32 [3072], P('groups'), parts along dimension 0
- mean_loss: float32 [2], P('groups'), parts along dimension 0
- errors_out: bfloat16 [256, 1536], P(('groups', 'utt')), parts along dimension 0
The draws below stay inside these ranges and needn't reach their ends.
There are 2 independent parts, one for each index of `groups`. The reference program is written for one: setup_inputs(seed, part) draws one part's arguments, and reference() takes and returns one part's arrays. A program takes and returns all parts, laid end to end along the dimension named above; an argument that names none is the same for every part. Nothing has to cross between parts.
Inputs may be any that keep to these rules, and one draw needn't show every extreme that they name: Valid frames of each utterance; the 32 lengths sum to 128, and some utterance has exactly 7. `take_list`: a permutation of the utterances: entry d * 2 + k names the utterance that slot k of device d takes; the utterances taken by the slots of one device have 8 valid frames together.
All inputs are finite; a program needn't handle non-finite values.
Results may differ from the reference program's by a relative error of at most 0.0095.
Values may be sent and summed in bfloat16 or wider, within the bound.
No kernel may reach another device: no remote copies, remote signals or barrier semaphores. Data moves between devices by JAX's collectives and lax.ppermute only.
A program may use at most 128 MiB of HBM per device.

```python
import jax
import jax.numpy as jnp
from jax import lax

CH = 512
CKPT = 3
UTT_DEV = 2
FRAMES_UTT = 8
SAMPLES = 90
FEAT = 1536
LAT = 8192
TOKENS = 128
UTTS = 32


def layout(key):
    inner = jax.random.fold_in(key, 7)
    first_key, second_key = jax.random.split(inner)
    halves = UTTS // 2
    first = jax.random.randint(first_key, (halves,), 1, FRAMES_UTT)
    first = first.at[0].set(FRAMES_UTT - 1)
    paired = jnp.concatenate([first, FRAMES_UTT - first])
    order = jax.random.permutation(second_key, UTTS)
    return paired[order].astype(jnp.int32)


def draw_lengths(key, part):
    return layout(key)


def draw_take_list(key, part):
    lengths = layout(key)
    labels = jnp.arange(UTTS, dtype=jnp.int32)
    scores = lengths * UTTS + labels
    ranked = jnp.argsort(-scores)
    devices = UTTS // UTT_DEV
    device_of = labels // UTT_DEV
    slot_of = labels % UTT_DEV
    within = jnp.where(slot_of % 2 == 0, device_of, devices - 1 - device_of)
    return ranked[slot_of * devices + within].astype(jnp.int32)


def steps_of(key, shape, shards, least, high):
    level, own = 1.0, jax.random.fold_in(key, 6)
    for position, blocks in shards:
        heights = jnp.exp(jax.random.uniform(jax.random.fold_in(own, position), (blocks,), jnp.float32, least / len(shards), high / len(shards)))
        level = level * jnp.repeat(heights, shape[position] // blocks).reshape([-1 if axis == position else 1 for axis in range(len(shape))])
    return level


def bell_draw(own_key, dims, scale, limit, cuts=(), kind=jnp.bfloat16):
    result = jax.random.normal(own_key, dims, jnp.float32) * scale
    if len(cuts) > 0:
        result = steps_of(own_key, dims, cuts, -0.22, 0.18) * result
    return jnp.clip(result, min=-limit, max=limit).astype(kind)


def setup_inputs(seed: int = 0, part: int = 0) -> dict:
    splits = jax.random.split(jax.random.key(seed), 12)
    own_keys = jax.random.split(jax.random.fold_in(splits[11], part), 12)
    return {
        "waveforms": bell_draw(own_keys[0], (UTTS, SAMPLES), 1.0, 6.0, ((0, 16),), jnp.float32),
        "lengths": draw_lengths(jax.random.fold_in(jax.random.fold_in(splits[11], part), 71), part),
        "take_list": draw_take_list(jax.random.fold_in(jax.random.fold_in(splits[11], part), 71), part),
        "conv_first": bell_draw(splits[3], (CKPT, 10, CH), 10 ** -0.5, 2.0, (), jnp.float32),
        "conv_second": bell_draw(splits[4], (CKPT, 3 * CH, CH), (3 * CH) ** -0.5, 0.15625),
        "norm_gain": jnp.clip(1.0 + 0.1 * jax.random.normal(splits[5], (CKPT, 2, CH), jnp.float32), 0.5, 1.5),
        "norm_shift": bell_draw(splits[6], (CKPT, 2, CH), 0.3, 2.0, (), jnp.float32),
        "enc_weight": bell_draw(splits[7], (FEAT, LAT), FEAT ** -0.5, 0.15625, ((1, 16),)),
        "enc_bias": bell_draw(splits[8], (LAT,), 0.3, 2.0, ((0, 16),), jnp.float32),
        "dec_weight": bell_draw(splits[9], (LAT, FEAT), LAT ** -0.5, 0.0625, ((0, 16),)),
        "dec_bias": bell_draw(splits[10], (FEAT,), 0.3, 2.0, (), jnp.float32),
    }


sparsity = 0.5
epsilon = 1e-05

def normalize(values, gain, shift):
    center = values - lax.optimization_barrier(jnp.mean(values, axis=-1, keepdims=True))
    spread = lax.optimization_barrier(jnp.mean(center * center, axis=-1, keepdims=True))
    return center * lax.rsqrt(spread + epsilon) * gain + shift

def extract(chosen, conv_first, conv_second, norm_gain, norm_shift):
    count = chosen.shape[0]
    frames = (chosen.shape[1] - 10) // 10
    blocks = chosen.reshape(count, 2 * frames + 2, 5)
    windows = jnp.concatenate([blocks[:, :-1], blocks[:, 1:]], axis=-1)
    first = jnp.einsum('ntk,ckd->cntd', windows, conv_first, precision=lax.Precision.HIGHEST)
    first = normalize(first, norm_gain[:, 0][:, None, None, :], norm_shift[:, 0][:, None, None, :])
    first = jax.nn.gelu(first, approximate=False).astype(jnp.bfloat16)
    paired = first[:, :, :-1].reshape(CKPT, count, frames, 2 * CH)
    columns = jnp.concatenate([paired, first[:, :, 2::2]], axis=-1)
    second = jnp.einsum('cntk,ckd->cntd', columns.astype(jnp.float32), conv_second.astype(jnp.float32))
    second = normalize(second, norm_gain[:, 1][:, None, None, :], norm_shift[:, 1][:, None, None, :])
    second = jax.nn.gelu(second, approximate=False).astype(jnp.bfloat16)
    return second.transpose(1, 2, 0, 3).reshape(count, frames, CKPT * CH)

def reference(waveforms, lengths, take_list, conv_first, conv_second, norm_gain, norm_shift, enc_weight, enc_bias, dec_weight, dec_bias):
    chosen = waveforms[take_list]
    chosen_len = lengths[take_list].astype(jnp.int32)
    frames = extract(chosen, conv_first, conv_second, norm_gain, norm_shift)
    frame_index = jnp.arange(FRAMES_UTT, dtype=jnp.int32)
    starts = (jnp.cumsum(chosen_len) - chosen_len).astype(jnp.int32)
    rows = jnp.where(frame_index[None, :] < chosen_len[:, None], starts[:, None] + frame_index[None, :], TOKENS).astype(jnp.int32)
    inputs = jnp.zeros((TOKENS + 1, FEAT), jnp.bfloat16).at[rows.reshape(-1)].set(frames.reshape(-1, FEAT))[:TOKENS]
    preact = jnp.dot(inputs, enc_weight, preferred_element_type=jnp.float32) + enc_bias
    latent = jnp.maximum(preact, 0.0)
    latent_b = latent.astype(jnp.bfloat16)
    decoder = dec_weight.astype(jnp.float32).reshape(LAT, CKPT, CH)
    norms = jnp.sqrt(lax.optimization_barrier(jnp.sum(decoder * decoder, axis=-1)) + 1e-06)
    weights_sum = lax.optimization_barrier(jnp.sum(norms, axis=-1))
    errors = jnp.dot(latent_b, dec_weight, preferred_element_type=jnp.float32) + dec_bias - inputs.astype(jnp.float32)
    errors_b = errors.astype(jnp.bfloat16)
    total = jnp.sum(errors * errors) + sparsity * jnp.sum(latent * weights_sum)
    mean_loss = (total / (TOKENS * FEAT)).reshape(1)
    activity = lax.optimization_barrier(jnp.sum(latent, axis=0))
    dec_grad = 2.0 * jnp.dot(latent_b.T, errors_b, preferred_element_type=jnp.float32)
    dec_grad = dec_grad + sparsity * (activity[:, None, None] * decoder / norms[:, :, None]).reshape(LAT, FEAT)
    upstream = 2.0 * jnp.dot(errors_b, dec_weight.T, preferred_element_type=jnp.float32) + sparsity * weights_sum
    through = jnp.where(preact > 0.0, upstream, 0.0)
    enc_grad = jnp.dot(inputs.T, through.astype(jnp.bfloat16), preferred_element_type=jnp.float32)
    return (enc_grad.astype(jnp.bfloat16), dec_grad.astype(jnp.bfloat16), lax.optimization_barrier(jnp.sum(through, axis=0)), lax.optimization_barrier(jnp.sum(2.0 * errors, axis=0)), mean_loss, errors_b)
```

```python
import jax
import jax.numpy as jnp
from jax import lax
from jax.sharding import PartitionSpec as P

ROWS_DEV = 8
EXTRA = 128

sparsity = 0.5
epsilon = 1e-05


def normalize(values, gain, shift):
    center = values - jnp.mean(values, axis=-1, keepdims=True)
    spread = jnp.mean(center * center, axis=-1, keepdims=True)
    return center * lax.rsqrt(spread + epsilon) * gain + shift


def extract(chosen, conv_first, conv_second, norm_gain, norm_shift):
    count = chosen.shape[0]
    frames = (chosen.shape[1] - 10) // 10
    checkpoints = conv_first.shape[0]
    channels = conv_first.shape[2]
    blocks = chosen.reshape(count, 2 * frames + 2, 5)
    windows = jnp.concatenate([blocks[:, :-1], blocks[:, 1:]], axis=-1)
    first = jnp.einsum("ntk,ckd->cntd", windows, conv_first, precision=lax.Precision.HIGHEST)
    first = normalize(first, norm_gain[:, 0][:, None, None, :], norm_shift[:, 0][:, None, None, :])
    first = jax.nn.gelu(first, approximate=False).astype(jnp.bfloat16)
    paired = first[:, :, :-1].reshape(checkpoints, count, frames, 2 * channels)
    columns = jnp.concatenate([paired, first[:, :, 2::2]], axis=-1)
    second = jnp.einsum("cntk,ckd->cntd", columns, conv_second, preferred_element_type=jnp.float32)
    second = normalize(
        second, norm_gain[:, 1][:, None, None, :], norm_shift[:, 1][:, None, None, :]
    )
    second = jax.nn.gelu(second, approximate=False).astype(jnp.bfloat16)
    return second.transpose(1, 2, 0, 3).reshape(count, frames, checkpoints * channels)


def levels(devices):
    chips = devices // 2
    outer = 1
    while outer * outer < chips:
        outer *= 2
    return outer, chips // outer


def exchange(value, bit):
    devices = lax.axis_size("utt")
    return lax.ppermute(value, "utt", [(i, i ^ bit) for i in range(devices)])


def tree(parts):
    while len(parts) > 1:
        parts = [parts[i] + parts[i + 1] for i in range(0, len(parts), 2)]
    return parts[0]


def gather_frames(own, outer, inner):
    step = 2 * inner
    held = jnp.concatenate([own] + [exchange(own, step * k) for k in range(1, outer)], axis=0)
    bit = 2
    while bit < step:
        held = jnp.concatenate([held, exchange(held, bit)], axis=0)
        bit *= 2
    return jnp.concatenate([held, exchange(held, 1)], axis=0)


def shards(
    waveforms,
    lengths,
    take_list,
    conv_first,
    conv_second,
    norm_gain,
    norm_shift,
    enc_weight,
    enc_bias,
    dec_weight,
    dec_bias,
):
    slots = take_list.shape[0]
    devices = lax.axis_size("utt")
    outer, inner = levels(devices)
    step = 2 * inner
    tokens = ROWS_DEV * devices
    position = lax.axis_index("utt")
    latents_dev = enc_weight.shape[1]
    checkpoints = conv_first.shape[0]
    channels = conv_first.shape[2]

    frames = extract(waveforms, conv_first, conv_second, norm_gain, norm_shift)
    frame_count = frames.shape[1]
    feature = frames.shape[2]
    lane = lax.broadcasted_iota(jnp.int32, (slots, frame_count, feature), 2)
    row = lax.broadcasted_iota(jnp.int32, (slots, frame_count, feature), 1)
    notes = jnp.where(lane == 0, lengths[:, None, None], take_list[:, None, None])
    packed = jnp.where(row == frame_count - 1, notes.astype(jnp.bfloat16), frames)
    every = gather_frames(packed.reshape(slots * frame_count, feature), outer, inner)

    place = jnp.arange(devices, dtype=jnp.int32)
    core_rel = place // (devices // 2)
    inner_rel = (place // outer) % inner
    outer_rel = place % outer
    owner = position ^ (outer_rel * step + inner_rel * 2 + core_rel)
    notes = every.reshape(devices, slots, frame_count, feature)[:, :, frame_count - 1, :2]
    notes = notes.astype(jnp.float32).astype(jnp.int32)
    size_of = notes[:, :, 0].reshape(-1)
    takes = notes[:, :, 1].reshape(-1)
    kinds = jnp.arange(slots, dtype=jnp.int32)
    label = (owner[:, None] * slots + kinds[None, :]).reshape(-1)
    match = takes[:, None] == label[None, :]
    device_start = jnp.sum(jnp.where(match, ROWS_DEV * (label // slots)[:, None], 0), axis=0)
    second_slot = jnp.sum(jnp.where(match, (label % slots)[:, None], 0), axis=0)
    begin = device_start + second_slot * (ROWS_DEV - size_of)
    frame_index = jnp.arange(frame_count, dtype=jnp.int32)
    target = jnp.where(frame_index[None, :] < size_of[:, None], begin[:, None] + frame_index[None, :], -1)
    target = target.reshape(-1)

    core_of = place // (devices // 2)
    outer_of = (place // inner) % outer
    inner_of = place % inner
    holder = position ^ (outer_of * step + inner_of * 2 + core_of)
    token = (holder[:, None] * ROWS_DEV + jnp.arange(ROWS_DEV, dtype=jnp.int32)[None, :]).reshape(-1)
    pick = (token[:, None] == target[None, :]).astype(jnp.bfloat16)
    inputs = jnp.dot(pick, every, preferred_element_type=jnp.float32).astype(jnp.bfloat16)

    preact = jnp.dot(inputs, enc_weight, preferred_element_type=jnp.float32) + enc_bias
    latent = jnp.maximum(preact, 0.0)
    latent_b = latent.astype(jnp.bfloat16)
    decoder = dec_weight.astype(jnp.float32).reshape(latents_dev, checkpoints, channels)
    norms = jnp.sqrt(jnp.sum(decoder * decoder, axis=-1) + 1e-06)
    weights_sum = jnp.sum(norms, axis=-1)
    part = jnp.dot(latent_b, dec_weight, preferred_element_type=jnp.float32)
    weight_part = jnp.sum(latent * weights_sum, axis=1, keepdims=True)
    part = jnp.concatenate([part, jnp.broadcast_to(weight_part, (tokens, EXTRA))], axis=1)

    half = tokens // 2
    part = part[:half] + exchange(part[half:], 1)
    chunk = half // outer
    small = part.astype(jnp.bfloat16)
    pieces = [part[:chunk]]
    for k in range(1, outer):
        pieces.append(exchange(small[k * chunk : (k + 1) * chunk], step * k).astype(jnp.float32))
    part = sum(pieces[1:], pieces[0])
    rows = chunk // inner
    bit = 2
    while bit < step:
        other = exchange(part, bit)
        width = (bit // 2) * rows
        other = other.reshape(-1, 2, width, feature + EXTRA)[:, ::-1].reshape(chunk, feature + EXTRA)
        part = part + other
        bit *= 2
    errors = part[:, :feature] + dec_bias - inputs[:chunk].astype(jnp.float32)
    coarse = part[:, feature:].astype(jnp.bfloat16)
    fine = (part[:, feature:] - coarse.astype(jnp.float32)).astype(jnp.bfloat16)
    spot = lax.broadcasted_iota(jnp.int32, (chunk, EXTRA), 1)
    payload = jnp.concatenate([errors.astype(jnp.bfloat16), jnp.where(spot == 0, coarse, fine)], axis=1)
    held = jnp.concatenate([payload] + [exchange(payload, step * k) for k in range(1, outer)], axis=0)
    held = jnp.concatenate([held, exchange(held, 1)], axis=0)
    errors_b = held[:, :feature]

    wide = errors_b.astype(jnp.float32).reshape(devices, ROWS_DEV, feature)
    extra = held[:, feature:].astype(jnp.float32).reshape(devices, ROWS_DEV, EXTRA)
    totals = jnp.sum(wide, axis=1)
    squares = jnp.sum(wide * wide, axis=1)
    extras = jnp.sum(extra, axis=1)
    totals = tree([totals[i] for i in range(devices)])
    squares = tree([squares[i] for i in range(devices)])
    extras = tree([extras[i] for i in range(devices)])
    dec_bias_grad = 2.0 * totals
    loss_total = jnp.sum(squares) + sparsity * (extras[0] + extras[1])
    mean_loss = (loss_total / (tokens * feature)).reshape(1)

    activity = jnp.sum(latent, axis=0)
    dec_grad = 2.0 * jnp.dot(latent_b.T, errors_b, preferred_element_type=jnp.float32)
    dec_grad = dec_grad + sparsity * (
        activity[:, None, None] * decoder / norms[:, :, None]
    ).reshape(latents_dev, feature)
    upstream = (
        2.0 * jnp.dot(errors_b, dec_weight.T, preferred_element_type=jnp.float32)
        + sparsity * weights_sum
    )
    through = jnp.where(preact > 0.0, upstream, 0.0)
    enc_grad = jnp.dot(inputs.T, through.astype(jnp.bfloat16), preferred_element_type=jnp.float32)
    return (
        enc_grad.astype(jnp.bfloat16),
        dec_grad.astype(jnp.bfloat16),
        jnp.sum(through, axis=0),
        dec_bias_grad,
        mean_loss,
        errors_b[:ROWS_DEV],
    )


def solution(mesh):
    return jax.shard_map(
        shards,
        mesh=mesh,
        in_specs=(
            P(("groups", "utt"), None),
            P(("groups", "utt")),
            P(("groups", "utt")),
            P(),
            P(),
            P(),
            P(),
            P(None, "utt"),
            P("utt"),
            P("utt", None),
            P(),
        ),
        out_specs=(
            P("groups", "utt"),
            P(("groups", "utt"), None),
            P(("groups", "utt")),
            P("groups"),
            P("groups"),
            P(("groups", "utt"), None),
        ),
        check_vma=False,
    )
```

```python
import jax
import jax.numpy as jnp
from jax import lax
from jax.experimental import pallas as pl
from jax.experimental.pallas import tpu as pltpu
from jax.sharding import PartitionSpec as P

ROWS_DEV = 8
EXTRA = 128
LANES = 128
VMEM_BYTES = 56 << 20

sparsity = 0.5
epsilon = 1e-05

F32 = jnp.float32
BF16 = jnp.bfloat16

ERF_LIMIT = 3.7439211627767994
ERF_TOP = (
    0.00022905065861350646,
    0.0034082910107109506,
    0.050955695062380861,
    0.18520832239976145,
    1.128379143519084,
)
ERF_BOTTOM = (
    -1.1791602954361697e-7,
    0.000023547966471313185,
    0.0010179625278914885,
    0.014070470171167667,
    0.11098505178285362,
    0.49746925110067538,
    1.0,
)


def polynomial(x, terms):
    total = jnp.full_like(x, terms[0])
    for term in terms[1:]:
        total = total * x + term
    return total


def gelu(x):
    z = jnp.clip(x * 0.7071067811865476, -ERF_LIMIT, ERF_LIMIT)
    square = z * z
    erf = z * polynomial(square, ERF_TOP) / polynomial(square, ERF_BOTTOM)
    return 0.5 * x * (1.0 + erf)


def normalize(values, gain, shift):
    center = values - jnp.mean(values, axis=-1, keepdims=True)
    spread = jnp.mean(center * center, axis=-1, keepdims=True)
    return center * lax.rsqrt(spread + epsilon) * gain + shift


def levels(devices):
    chips = devices // 2
    outer = 1
    while outer * outer < chips:
        outer *= 2
    return outer, chips // outer


def exchange(value, bit):
    devices = lax.axis_size("utt")
    return lax.ppermute(value, "utt", [(i, i ^ bit) for i in range(devices)])


def tree(parts):
    while len(parts) > 1:
        parts = [parts[i] + parts[i + 1] for i in range(0, len(parts), 2)]
    return parts[0]


def iota(shape, dim):
    return lax.broadcasted_iota(jnp.int32, shape, dim)


def log2(n):
    return n.bit_length() - 1


def vmem():
    return pl.BlockSpec(memory_space=pltpu.VMEM)


def smem():
    return pl.BlockSpec(memory_space=pltpu.SMEM)


def call(kernel, name, out_shape, in_specs, out_specs, scratch=(), flops=0, moved=0):
    return pl.pallas_call(
        kernel,
        name=name,
        out_shape=out_shape,
        in_specs=in_specs,
        out_specs=out_specs,
        scratch_shapes=list(scratch),
        compiler_params=pltpu.CompilerParams(vmem_limit_bytes=VMEM_BYTES),
        cost_estimate=pl.CostEstimate(flops=flops, bytes_accessed=moved, transcendentals=0),
    )


def shape(dims, kind):
    return jax.ShapeDtypeStruct(dims, kind)


def features_kernel(length, take, wave, first_w, gain, shift, second_hbm, out, second_w, sems):
    checkpoints, taps_first, channels = first_w.shape
    slots, samples = wave.shape
    frames = out.shape[0] // slots
    copies = []
    for c in range(checkpoints):
        copies.append(pltpu.make_async_copy(second_hbm.at[c], second_w.at[c], sems.at[c]))
        copies[-1].start()
    lane = iota((frames, samples), 1)
    start = iota((frames, samples), 0) * 10
    columns = []
    for s in range(slots):
        row = jnp.broadcast_to(wave[s : s + 1, :], (frames, samples))
        columns.append(
            [
                jnp.sum(jnp.where(lane == start + o, row, 0.0), axis=1, keepdims=True)
                for o in range(taps_first + 10)
            ]
        )
    taps = [
        jnp.concatenate(
            [columns[s][5 * tap + k] for tap in range(3) for s in range(slots)], axis=0
        )
        for k in range(taps_first)
    ]
    hidden = []
    for c in range(checkpoints):
        total = taps[0] * first_w[c, 0:1, :]
        for k in range(1, taps_first):
            total = total + taps[k] * first_w[c, k : k + 1, :]
        total = normalize(total, gain[c, 0:1, :], shift[c, 0:1, :])
        hidden.append(gelu(total).astype(BF16))
    rows = slots * frames
    for c in range(checkpoints):
        copies[c].wait()
        total = jnp.zeros((rows, channels), F32)
        for tap in range(3):
            total = total + jnp.dot(
                hidden[c][tap * rows : (tap + 1) * rows],
                second_w[c, tap * channels : (tap + 1) * channels, :],
                preferred_element_type=F32,
            )
        total = gelu(normalize(total, gain[c, 1:2, :], shift[c, 1:2, :]))
        if c == 0:
            spot = iota((rows, channels), 1)
            line = iota((rows, channels), 0)
            for s in range(slots):
                note = jnp.where(
                    spot == 0, length[s].astype(F32), take[s].astype(F32)
                )
                total = jnp.where(line == (s + 1) * frames - 1, note, total)
        out[:, c * channels : (c + 1) * channels] = total.astype(BF16)


def join_kernel(*refs):
    out = refs[-1]
    at = 0
    for ref in refs[:-1]:
        out[at : at + ref.shape[0], :] = ref[...]
        at += ref.shape[0]


def norms_kernel(dec, norms, row):
    latents, feature = dec.shape
    channels = 512
    spot = iota((latents, LANES), 1)
    packed = jnp.zeros((latents, LANES), F32)
    total = jnp.zeros((latents, 1), F32)
    for c in range(feature // channels):
        block = dec[:, c * channels : (c + 1) * channels].astype(F32)
        norm = jnp.sqrt(jnp.sum(block * block, axis=1, keepdims=True) + 1e-06)
        total = total + norm
        packed = jnp.where(spot == c, norm, packed)
    norms[...] = packed
    row[...] = jnp.broadcast_to(total, (latents, LANES)).T[:8]


def encode_kernel(count, outer, inner, slots, frames, rel, *refs):
    me_ref = refs[0]
    pieces = refs[1 : 1 + count]
    enc, bias, dec, weights_sum, dec_bias = refs[1 + count : 6 + count]
    own, send, shift, inputs_out, latent_out = refs[6 + count :]
    me = me_ref[0]
    step = 2 * inner
    tokens, feature = inputs_out.shape
    rows = pieces[0].shape[0]
    held = rows // frames
    shift_frames, shift_slots = log2(frames), log2(slots)
    choose = (iota((held, rows), 1) == iota((held, rows), 0) * frames + frames - 1).astype(BF16)
    takes, starts = [], []
    for piece, bits in zip(pieces, rel):
        notes = jnp.dot(choose, piece[:, :LANES], preferred_element_type=F32)
        takes.append(notes[:, 1:2].astype(jnp.int32))
        device = me ^ ((iota((held, 1), 0) >> shift_slots) * step + bits)
        starts.append(device * ROWS_DEV)
    takes = jnp.concatenate(takes, axis=0)
    starts = jnp.concatenate(starts, axis=0)
    kinds = iota(takes.shape, 0) & (slots - 1)
    r = iota((tokens, 1), 0) >> log2(ROWS_DEV)
    holder = (
        ((r >> log2(inner)) & (outer - 1)) * step + (r & (inner - 1)) * 2 + (r >> log2(outer * inner))
    )
    token = (me ^ holder) * ROWS_DEV + (iota((tokens, 1), 0) & (ROWS_DEV - 1))
    lane = iota((1, rows), 1)
    frame = lane & (frames - 1)
    last = (iota((rows, rows), 0) == (iota((rows, rows), 1) | (frames - 1))).astype(BF16)
    ident = (iota((16, LANES), 0) == iota((16, LANES), 1)).astype(BF16)
    total = jnp.zeros((tokens, feature), F32)
    for piece, bits in zip(pieces, rel):
        turned = lax.dot_general(
            ident, piece[:, :LANES], (((1,), (1,)), ((), ())), preferred_element_type=F32
        )
        turned = jnp.dot(turned.astype(BF16), last, preferred_element_type=F32)
        size = turned[0:1, :].astype(jnp.int32)
        device = me ^ ((lane >> (shift_frames + shift_slots)) * step + bits)
        label = device * slots + ((lane >> shift_frames) & (slots - 1))
        match = takes == label
        begin = jnp.sum(jnp.where(match, starts, 0), axis=0, keepdims=True)
        second = jnp.sum(jnp.where(match, kinds, 0), axis=0, keepdims=True)
        target = begin + second * (ROWS_DEV - size) + frame
        target = jnp.where(frame < size, target, -1)
        pick = jnp.where(token == target, 1.0, 0.0).astype(BF16)
        total = total + jnp.dot(pick, piece[...], preferred_element_type=F32)
    inputs = total.astype(BF16)
    inputs_out[...] = inputs
    latent = jnp.maximum(jnp.dot(inputs, enc[...], preferred_element_type=F32) + bias[...], 0.0)
    latent_out[...] = latent
    part = jnp.dot(latent.astype(BF16), dec[...], preferred_element_type=F32)
    weighted = latent * weights_sum[0:1, :]
    extra = weighted[:, :LANES]
    for q in range(1, weighted.shape[1] // LANES):
        extra = extra + weighted[:, q * LANES : (q + 1) * LANES]
    half = tokens // 2
    own[:, :feature] = part[:half]
    own[:, feature:] = extra[:half]
    send[:, :feature] = part[half:]
    send[:, feature:] = extra[half:]
    chunk = shift.shape[0]
    shift[:, :feature] = dec_bias[...] - inputs[:chunk].astype(F32)
    shift[:, feature:] = jnp.zeros((chunk, EXTRA), F32)


def turn_kernel(inputs, latent, norms, inputs_t, latent_t, scale):
    inputs_t[...] = inputs[...].astype(F32).T.astype(BF16)
    turned = latent[...].T
    latent_t[...] = turned.astype(BF16)
    activity = jnp.sum(turned, axis=1, keepdims=True)
    scale[...] = (sparsity * activity) / jnp.maximum(norms[...], 1e-30)


def gradients_kernel(count, inner, cells, *refs):
    pieces = refs[:count]
    dec, weights_sum, inputs_t, latent_t, latent, scale = refs[count : count + 6]
    enc_out, dec_out, enc_bias_out, dec_bias_out, loss_out, errors_out = refs[count + 6 : count + 12]
    enc_buf, dec_buf, sems = refs[count + 12 :]
    latents, feature = dec.shape
    channels = 512
    errors = jnp.concatenate([piece[:, :feature] for piece in pieces], axis=0)
    copies = []
    parts = 4
    size = latents // parts
    for i in range(parts):
        at = slice(i * size, (i + 1) * size)
        grad = 2.0 * jnp.dot(latent_t[at], errors, preferred_element_type=F32)
        for c in range(feature // channels):
            lanes = slice(c * channels, (c + 1) * channels)
            term = scale[at, c : c + 1] * dec[at, lanes].astype(F32)
            dec_buf[at, lanes] = (grad[:, lanes] + term).astype(BF16)
        copies.append(pltpu.make_async_copy(dec_buf.at[at], dec_out.at[at], sems.at[i]))
        copies[-1].start()
    upstream = lax.dot_general(
        errors, dec[...], (((1,), (1,)), ((), ())), preferred_element_type=F32
    )
    upstream = 2.0 * upstream + sparsity * weights_sum[0:1, :]
    through = jnp.where(latent[...] > 0.0, upstream, 0.0)
    enc_bias_out[...] = jnp.sum(through, axis=0, keepdims=True)
    through = through.astype(BF16)
    size = feature // parts
    for i in range(parts):
        at = slice(i * size, (i + 1) * size)
        grad = jnp.dot(inputs_t[at], through, preferred_element_type=F32)
        enc_buf[at] = grad.astype(BF16)
        copies.append(pltpu.make_async_copy(enc_buf.at[at], enc_out.at[at], sems.at[parts + i]))
        copies[-1].start()
    errors_out[...] = pieces[0][:ROWS_DEV, :feature]
    wide = [piece[...].astype(F32) for piece in pieces]
    plain = tree(wide)
    squares = tree([w[:, :feature] * w[:, :feature] for w in wide])
    plain = tree([plain[i * ROWS_DEV : (i + 1) * ROWS_DEV] for i in range(inner)])
    squares = tree([squares[i * ROWS_DEV : (i + 1) * ROWS_DEV] for i in range(inner)])
    dec_bias_out[...] = 2.0 * jnp.sum(plain[:, :feature], axis=0, keepdims=True)
    loss = jnp.sum(squares) + sparsity * jnp.sum(plain[:, feature:])
    loss_out[0] = loss / cells
    for copy in copies:
        copy.wait()


def shards(
    waveforms,
    lengths,
    take_list,
    conv_first,
    conv_second,
    norm_gain,
    norm_shift,
    enc_weight,
    enc_bias,
    dec_weight,
    dec_bias,
):
    slots = take_list.shape[0]
    devices = lax.axis_size("utt")
    outer, inner = levels(devices)
    step = 2 * inner
    tokens = ROWS_DEV * devices
    position = lax.axis_index("utt").astype(jnp.int32).reshape(1)
    feature, latents = enc_weight.shape
    checkpoints, _, channels = conv_first.shape
    frames = (waveforms.shape[1] - 10) // 10
    wide = feature + EXTRA

    packed = call(
        features_kernel,
        "features",
        shape((slots * frames, feature), BF16),
        [smem(), smem(), vmem(), vmem(), vmem(), vmem(), pl.BlockSpec(memory_space=pl.ANY)],
        vmem(),
        [pltpu.VMEM(conv_second.shape, BF16), pltpu.SemaphoreType.DMA((checkpoints,))],
        flops=2 * slots * frames * feature * 3 * channels,
        moved=2 * conv_second.size,
    )(lengths, take_list, waveforms, conv_first, norm_gain, norm_shift, conv_second)

    norms, weights_sum = call(
        norms_kernel,
        "norms",
        (shape((latents, LANES), F32), shape((8, latents), F32)),
        [vmem()],
        (vmem(), vmem()),
        flops=4 * dec_weight.size,
        moved=2 * dec_weight.size,
    )(dec_weight)

    blocks = [packed] + [exchange(packed, step * k) for k in range(1, outer)]
    pieces = [
        call(
            join_kernel,
            "join",
            shape((outer * slots * frames, feature), BF16),
            [vmem()] * outer,
            vmem(),
            moved=4 * outer * slots * frames * feature,
        )(*blocks)
    ]
    rel = [0]
    bit = 2
    while bit < step:
        pieces += [exchange(piece, bit) for piece in pieces]
        rel += [r ^ bit for r in rel]
        bit *= 2
    pieces += [exchange(piece, 1) for piece in pieces]
    rel += [r ^ 1 for r in rel]

    half = tokens // 2
    chunk = half // outer

    def encode(*refs):
        encode_kernel(len(pieces), outer, inner, slots, frames, rel, *refs)

    own, send, shift, inputs, latent = call(
        encode,
        "encode",
        (
            shape((half, wide), F32),
            shape((half, wide), F32),
            shape((chunk, wide), F32),
            shape((tokens, feature), BF16),
            shape((tokens, latents), F32),
        ),
        [smem()] + [vmem()] * (len(pieces) + 5),
        (vmem(),) * 5,
        flops=4 * tokens * feature * latents,
        moved=4 * dec_weight.size,
    )(
        position,
        *pieces,
        enc_weight,
        enc_bias.reshape(1, latents),
        dec_weight,
        weights_sum,
        dec_bias.reshape(1, feature),
    )

    inputs_t, latent_t, scale = call(
        turn_kernel,
        "turn",
        (shape((feature, tokens), BF16), shape((latents, tokens), BF16), shape((latents, LANES), F32)),
        [vmem()] * 3,
        (vmem(),) * 3,
        flops=2 * tokens * feature,
        moved=4 * tokens * feature,
    )(inputs, latent, norms)

    part = own + exchange(send, 1)
    small = part.astype(BF16)
    blocks = [part[:chunk]]
    for k in range(1, outer):
        blocks.append(exchange(small[k * chunk : (k + 1) * chunk], step * k).astype(F32))
    part = sum(blocks[1:], blocks[0])
    rows = chunk // inner
    bit = 2
    while bit < step:
        width = (bit // 2) * rows
        other = exchange(part, bit).reshape(-1, 2, width, wide)
        part = part + other[:, ::-1].reshape(chunk, wide)
        bit *= 2
    errors = (part + shift).astype(BF16)
    blocks = [errors] + [exchange(errors, step * k) for k in range(1, outer)]
    blocks += [exchange(block, 1) for block in blocks]

    def gradients(*refs):
        gradients_kernel(len(blocks), inner, float(tokens * feature), *refs)

    any_space = pl.BlockSpec(memory_space=pl.ANY)
    enc_grad, dec_grad, enc_bias_grad, dec_bias_grad, mean_loss, errors_own = call(
        gradients,
        "gradients",
        (
            shape((feature, latents), BF16),
            shape((latents, feature), BF16),
            shape((1, latents), F32),
            shape((1, feature), F32),
            shape((1,), F32),
            shape((ROWS_DEV, feature), BF16),
        ),
        [vmem()] * (len(blocks) + 6),
        (any_space, any_space, vmem(), vmem(), smem(), vmem()),
        [
            pltpu.VMEM((feature, latents), BF16),
            pltpu.VMEM((latents, feature), BF16),
            pltpu.SemaphoreType.DMA((8,)),
        ],
        flops=6 * tokens * feature * latents,
        moved=8 * dec_weight.size,
    )(*blocks, dec_weight, weights_sum, inputs_t, latent_t, latent, scale)
    return (
        enc_grad,
        dec_grad,
        enc_bias_grad.reshape(latents),
        dec_bias_grad.reshape(feature),
        mean_loss,
        errors_own,
    )


def solution(mesh):
    return jax.shard_map(
        shards,
        mesh=mesh,
        in_specs=(
            P(("groups", "utt"), None),
            P(("groups", "utt")),
            P(("groups", "utt")),
            P(),
            P(),
            P(),
            P(),
            P(None, "utt"),
            P("utt"),
            P("utt", None),
            P(),
        ),
        out_specs=(
            P("groups", "utt"),
            P(("groups", "utt"), None),
            P(("groups", "utt")),
            P("groups"),
            P("groups"),
            P(("groups", "utt"), None),
        ),
        check_vma=False,
    )
```

```python
import functools

import jax
import jax.numpy as jnp
from jax import lax
from jax.experimental import pallas as pl
from jax.experimental.pallas import tpu as pltpu
from jax.sharding import PartitionSpec as P

ROWS_DEV = 8
EXTRA = 128
LANES = 128
VMEM_BYTES = 56 << 20
PINNED_BYTES = 24 << 20
PINNED_TOKENS = 256

sparsity = 0.5
epsilon = 1e-05

F32 = jnp.float32
BF16 = jnp.bfloat16

ERF_LIMIT = 3.7439211627767994
ERF_TOP = (
    0.00022905065861350646,
    0.0034082910107109506,
    0.050955695062380861,
    0.18520832239976145,
    1.128379143519084,
)
ERF_BOTTOM = (
    -1.1791602954361697e-7,
    0.000023547966471313185,
    0.0010179625278914885,
    0.014070470171167667,
    0.11098505178285362,
    0.49746925110067538,
    1.0,
)


def polynomial(x, terms):
    total = jnp.full_like(x, terms[0])
    for term in terms[1:]:
        total = total * x + term
    return total


def gelu(x):
    z = jnp.clip(x * 0.7071067811865476, -ERF_LIMIT, ERF_LIMIT)
    square = z * z
    erf = z * polynomial(square, ERF_TOP) / polynomial(square, ERF_BOTTOM)
    return 0.5 * x * (1.0 + erf)


def normalize(values, gain, shift):
    center = values - jnp.mean(values, axis=-1, keepdims=True)
    spread = jnp.mean(center * center, axis=-1, keepdims=True)
    return center * lax.rsqrt(spread + epsilon) * gain + shift


def levels(devices):
    chips = devices // 2
    outer = 1
    while outer * outer < chips:
        outer *= 2
    return outer, chips // outer


def exchange(value, bit):
    devices = lax.axis_size("utt")
    return lax.ppermute(value, "utt", [(i, i ^ bit) for i in range(devices)])


def tree(parts):
    while len(parts) > 1:
        parts = [parts[i] + parts[i + 1] for i in range(0, len(parts), 2)]
    return parts[0]


def iota(shape, dim):
    return lax.broadcasted_iota(jnp.int32, shape, dim)


def log2(n):
    return n.bit_length() - 1


def vmem():
    return pl.BlockSpec(memory_space=pltpu.VMEM)


def smem():
    return pl.BlockSpec(memory_space=pltpu.SMEM)


def launch(limit, kernel, name, out_shape, in_specs, out_specs, scratch=(), flops=0, moved=0):
    return pl.pallas_call(
        kernel,
        name=name,
        out_shape=out_shape,
        in_specs=in_specs,
        out_specs=out_specs,
        scratch_shapes=list(scratch),
        compiler_params=pltpu.CompilerParams(vmem_limit_bytes=limit),
        cost_estimate=pl.CostEstimate(flops=flops, bytes_accessed=moved, transcendentals=0),
    )


def shape(dims, kind):
    return jax.ShapeDtypeStruct(dims, kind)


def features_kernel(length, take, wave, first_w, gain, shift, second_hbm, out, second_w, sems):
    taps_first, checkpoints, channels = first_w.shape
    slots, samples = wave.shape
    frames = out.shape[0] // slots
    copies = []
    for c in range(checkpoints):
        copies.append(pltpu.make_async_copy(second_hbm.at[c], second_w.at[c], sems.at[c]))
        copies[-1].start()
    lane = iota((frames, samples), 1)
    start = iota((frames, samples), 0) * 10
    columns = []
    for s in range(slots):
        row = jnp.broadcast_to(wave[s : s + 1, :], (frames, samples))
        columns.append(
            [
                jnp.sum(jnp.where(lane == start + o, row, 0.0), axis=1, keepdims=True)
                for o in range(taps_first + 10)
            ]
        )
    taps = [
        jnp.concatenate(
            [columns[s][5 * tap + k] for tap in range(3) for s in range(slots)], axis=0
        )
        for k in range(taps_first)
    ]
    hidden = []
    for c in range(checkpoints):
        total = taps[0] * first_w[0, c : c + 1, :]
        for k in range(1, taps_first):
            total = total + taps[k] * first_w[k, c : c + 1, :]
        total = normalize(total, gain[c, 0:1, :], shift[c, 0:1, :])
        hidden.append(gelu(total).astype(BF16))
    rows = slots * frames
    for c in range(checkpoints):
        copies[c].wait()
        total = jnp.zeros((rows, channels), F32)
        for tap in range(3):
            total = total + jnp.dot(
                hidden[c][tap * rows : (tap + 1) * rows],
                second_w[c, tap * channels : (tap + 1) * channels, :],
                preferred_element_type=F32,
            )
        total = gelu(normalize(total, gain[c, 1:2, :], shift[c, 1:2, :]))
        if c == 0:
            spot = iota((rows, channels), 1)
            line = iota((rows, channels), 0)
            for s in range(slots):
                note = jnp.where(
                    spot == 0, length[s].astype(F32), take[s].astype(F32)
                )
                total = jnp.where(line == (s + 1) * frames - 1, note, total)
        out[:, c * channels : (c + 1) * channels] = total.astype(BF16)


def join_kernel(*refs):
    out = refs[-1]
    at = 0
    for ref in refs[2:-1]:
        out[at : at + ref.shape[0], :] = ref[...]
        at += ref.shape[0]


def norms_kernel(dec, norms, row):
    latents, feature = dec.shape
    channels = 512
    spot = iota((latents, LANES), 1)
    packed = jnp.zeros((latents, LANES), F32)
    total = jnp.zeros((latents, 1), F32)
    for c in range(feature // channels):
        block = dec[:, c * channels : (c + 1) * channels].astype(F32)
        norm = jnp.sqrt(jnp.sum(block * block, axis=1, keepdims=True) + 1e-06)
        total = total + norm
        packed = jnp.where(spot == c, norm, packed)
    norms[...] = packed
    row[...] = jnp.broadcast_to(total, (latents, LANES)).T[:8]


def encode_kernel(count, outer, inner, slots, frames, rel, *refs):
    me_ref = refs[0]
    pieces = refs[1 : 1 + count]
    enc, bias, dec, weights_sum, dec_bias = refs[1 + count : 6 + count]
    own, send, shift, inputs_out, latent_out = refs[6 + count :]
    me = me_ref[0]
    step = 2 * inner
    tokens, feature = inputs_out.shape
    rows = pieces[0].shape[0]
    held = rows // frames
    shift_frames, shift_slots = log2(frames), log2(slots)
    choose = (iota((held, rows), 1) == iota((held, rows), 0) * frames + frames - 1).astype(BF16)
    takes, starts = [], []
    for piece, bits in zip(pieces, rel):
        notes = jnp.dot(choose, piece[:, :LANES], preferred_element_type=F32)
        takes.append(notes[:, 1:2].astype(jnp.int32))
        device = me ^ ((iota((held, 1), 0) >> shift_slots) * step + bits)
        starts.append(device * ROWS_DEV)
    takes = jnp.concatenate(takes, axis=0)
    starts = jnp.concatenate(starts, axis=0)
    kinds = iota(takes.shape, 0) & (slots - 1)
    r = iota((tokens, 1), 0) >> log2(ROWS_DEV)
    holder = (
        ((r >> log2(inner)) & (outer - 1)) * step + (r & (inner - 1)) * 2 + (r >> log2(outer * inner))
    )
    token = (me ^ holder) * ROWS_DEV + (iota((tokens, 1), 0) & (ROWS_DEV - 1))
    lane = iota((1, rows), 1)
    frame = lane & (frames - 1)
    last = (iota((rows, rows), 0) == (iota((rows, rows), 1) | (frames - 1))).astype(BF16)
    ident = (iota((16, LANES), 0) == iota((16, LANES), 1)).astype(BF16)
    total = jnp.zeros((tokens, feature), F32)
    for piece, bits in zip(pieces, rel):
        turned = lax.dot_general(
            ident, piece[:, :LANES], (((1,), (1,)), ((), ())), preferred_element_type=F32
        )
        turned = jnp.dot(turned.astype(BF16), last, preferred_element_type=F32)
        size = turned[0:1, :].astype(jnp.int32)
        device = me ^ ((lane >> (shift_frames + shift_slots)) * step + bits)
        label = device * slots + ((lane >> shift_frames) & (slots - 1))
        match = takes == label
        begin = jnp.sum(jnp.where(match, starts, 0), axis=0, keepdims=True)
        second = jnp.sum(jnp.where(match, kinds, 0), axis=0, keepdims=True)
        target = begin + second * (ROWS_DEV - size) + frame
        target = jnp.where(frame < size, target, -1)
        pick = jnp.where(token == target, 1.0, 0.0).astype(BF16)
        total = total + jnp.dot(pick, piece[...], preferred_element_type=F32)
    inputs = total.astype(BF16)
    inputs_out[...] = inputs
    latent = jnp.maximum(jnp.dot(inputs, enc[...], preferred_element_type=F32) + bias[...], 0.0)
    latent_out[...] = latent
    part = jnp.dot(latent.astype(BF16), dec[...], preferred_element_type=F32)
    weighted = latent * weights_sum[0:1, :]
    extra = weighted[:, :LANES]
    for q in range(1, weighted.shape[1] // LANES):
        extra = extra + weighted[:, q * LANES : (q + 1) * LANES]
    half = tokens // 2
    own[:, :feature] = part[:half]
    own[:, feature:] = extra[:half]
    send[:, :feature] = part[half:]
    send[:, feature:] = extra[half:]
    chunk = shift.shape[0]
    shift[:, :feature] = dec_bias[...].reshape(1, feature) - inputs[:chunk].astype(F32)
    shift[:, feature:] = jnp.zeros((chunk, EXTRA), F32)


def turn_kernel(inputs, latent, norms, inputs_t, latent_t, scale):
    inputs_t[...] = inputs[...].astype(F32).T.astype(BF16)
    turned = latent[...].T
    latent_t[...] = turned.astype(BF16)
    activity = jnp.sum(turned, axis=1, keepdims=True)
    scale[...] = (sparsity * activity) / jnp.maximum(norms[...], 1e-30)


def sum_kernel(*refs):
    total = refs[1][...]
    for ref in refs[2:-1]:
        total = total + ref[...].astype(F32)
    refs[-1][...] = total


def gradients_kernel(count, inner, cells, *refs):
    pieces = refs[:count]
    dec, weights_sum, inputs_t, latent_t, latent, scale = refs[count : count + 6]
    enc_out, dec_out, enc_bias_out, dec_bias_out, loss_out, errors_out = refs[count + 6 : count + 12]
    enc_buf, dec_buf, sems = refs[count + 12 :]
    latents, feature = dec.shape
    channels = 512
    errors = jnp.concatenate([piece[:, :feature] for piece in pieces], axis=0)
    copies = []
    parts = 4
    size = latents // parts
    for i in range(parts):
        at = slice(i * size, (i + 1) * size)
        grad = 2.0 * jnp.dot(latent_t[at], errors, preferred_element_type=F32)
        for c in range(feature // channels):
            lanes = slice(c * channels, (c + 1) * channels)
            term = scale[at, c : c + 1] * dec[at, lanes].astype(F32)
            dec_buf[at, lanes] = (grad[:, lanes] + term).astype(BF16)
        copies.append(pltpu.make_async_copy(dec_buf.at[at], dec_out.at[at], sems.at[i]))
        copies[-1].start()
    upstream = lax.dot_general(
        errors, dec[...], (((1,), (1,)), ((), ())), preferred_element_type=F32
    )
    upstream = 2.0 * upstream + sparsity * weights_sum[0:1, :]
    through = jnp.where(latent[...] > 0.0, upstream, 0.0)
    enc_bias_out[...] = jnp.sum(through, axis=0, keepdims=True)
    through = through.astype(BF16)
    size = feature // parts
    for i in range(parts):
        at = slice(i * size, (i + 1) * size)
        grad = jnp.dot(inputs_t[at], through, preferred_element_type=F32)
        enc_buf[at] = grad.astype(BF16)
        copies.append(pltpu.make_async_copy(enc_buf.at[at], enc_out.at[at], sems.at[parts + i]))
        copies[-1].start()
    errors_out[...] = pieces[0][:ROWS_DEV, :feature]
    wide = [piece[...].astype(F32) for piece in pieces]
    plain = tree(wide)
    squares = tree([w[:, :feature] * w[:, :feature] for w in wide])
    plain = tree([plain[i * ROWS_DEV : (i + 1) * ROWS_DEV] for i in range(inner)])
    squares = tree([squares[i * ROWS_DEV : (i + 1) * ROWS_DEV] for i in range(inner)])
    dec_bias_out[...] = 2.0 * jnp.sum(plain[:, :feature], axis=0)
    loss = jnp.sum(squares) + sparsity * jnp.sum(plain[:, feature:])
    loss_out[0] = loss / cells
    for copy in copies:
        copy.wait()


def shards(
    waveforms,
    lengths,
    take_list,
    conv_first,
    conv_second,
    norm_gain,
    norm_shift,
    enc_weight,
    enc_bias,
    dec_weight,
    dec_bias,
):
    slots = take_list.shape[0]
    devices = lax.axis_size("utt")
    outer, inner = levels(devices)
    step = 2 * inner
    tokens = ROWS_DEV * devices
    position = lax.axis_index("utt").astype(jnp.int32).reshape(1)
    feature, latents = enc_weight.shape
    checkpoints, _, channels = conv_first.shape
    frames = (waveforms.shape[1] - 10) // 10
    wide = feature + EXTRA

    pinned = tokens <= PINNED_TOKENS
    call = functools.partial(launch, PINNED_BYTES if pinned else VMEM_BYTES)

    def fast(dims, kind):
        return pltpu.VMEM(dims, kind) if pinned else shape(dims, kind)

    def near(value):
        return pltpu.with_memory_space_constraint(value, pltpu.VMEM) if pinned else value

    encoder = near(enc_weight)
    decoder = near(dec_weight)

    packed = call(
        features_kernel,
        "features",
        fast((slots * frames, feature), BF16),
        [smem(), smem(), vmem(), vmem(), vmem(), vmem(), pl.BlockSpec(memory_space=pl.ANY)],
        vmem(),
        [pltpu.VMEM(conv_second.shape, BF16), pltpu.SemaphoreType.DMA((checkpoints,))],
        flops=2 * slots * frames * feature * 3 * channels,
        moved=2 * conv_second.size,
    )(lengths, take_list, waveforms, conv_first.transpose(1, 0, 2), norm_gain, norm_shift, conv_second)

    norms, weights_sum = call(
        norms_kernel,
        "norms",
        (fast((latents, LANES), F32), fast((8, latents), F32)),
        [vmem()],
        (vmem(), vmem()),
        flops=4 * dec_weight.size,
        moved=2 * dec_weight.size,
    )(decoder)

    blocks = [packed] + [exchange(packed, step * k) for k in range(1, outer)]
    pieces = [
        call(
            join_kernel,
            "join",
            fast((outer * slots * frames, feature), BF16),
            [pl.BlockSpec(memory_space=pl.ANY)] * 2 + [vmem()] * outer,
            vmem(),
            moved=4 * outer * slots * frames * feature,
        )(near(norms), encoder, *[near(block) for block in blocks])
    ]
    rel = [0]
    bit = 2
    while bit < step:
        pieces += [exchange(piece, bit) for piece in pieces]
        rel += [r ^ bit for r in rel]
        bit *= 2
    pieces += [exchange(piece, 1) for piece in pieces]
    rel += [r ^ 1 for r in rel]

    half = tokens // 2
    chunk = half // outer

    def encode(*refs):
        encode_kernel(len(pieces), outer, inner, slots, frames, rel, *refs)

    own, send, shift, inputs, latent = call(
        encode,
        "encode",
        (
            fast((half, wide), F32),
            fast((half, wide), F32),
            fast((chunk, wide), F32),
            fast((tokens, feature), BF16),
            fast((tokens, latents), F32),
        ),
        [smem()] + [vmem()] * (len(pieces) + 5),
        (vmem(),) * 5,
        flops=4 * tokens * feature * latents,
        moved=4 * dec_weight.size,
    )(
        position,
        *[near(piece) for piece in pieces],
        encoder,
        enc_bias.reshape(1, latents),
        decoder,
        near(weights_sum),
        dec_bias,
    )

    inputs_t, latent_t, scale = call(
        turn_kernel,
        "turn",
        (fast((feature, tokens), BF16), fast((latents, tokens), BF16), fast((latents, LANES), F32)),
        [vmem()] * 3,
        (vmem(),) * 3,
        flops=2 * tokens * feature,
        moved=4 * tokens * feature,
    )(near(inputs), near(latent), near(norms))

    part = own + exchange(send, 1)
    small = part.astype(BF16)
    blocks = [part[:chunk]]
    for k in range(1, outer):
        blocks.append(exchange(small[k * chunk : (k + 1) * chunk], step * k))
    part = call(
        sum_kernel,
        "sum",
        fast((chunk, wide), F32),
        [pl.BlockSpec(memory_space=pl.ANY)] + [vmem()] * outer,
        vmem(),
        moved=8 * chunk * wide,
    )(near(scale), *[near(block) for block in blocks])
    rows = chunk // inner
    bit = 2
    while bit < step:
        width = (bit // 2) * rows
        other = exchange(part, bit).reshape(-1, 2, width, wide)
        part = part + other[:, ::-1].reshape(chunk, wide)
        bit *= 2
    errors = (part + shift).astype(BF16)
    blocks = [errors] + [exchange(errors, step * k) for k in range(1, outer)]
    blocks += [exchange(block, 1) for block in blocks]

    def gradients(*refs):
        gradients_kernel(len(blocks), inner, float(tokens * feature), *refs)

    any_space = pl.BlockSpec(memory_space=pl.ANY)
    enc_grad, dec_grad, enc_bias_grad, dec_bias_grad, mean_loss, errors_own = call(
        gradients,
        "gradients",
        (
            shape((feature, latents), BF16),
            shape((latents, feature), BF16),
            shape((1, latents), F32),
            shape((feature,), F32),
            shape((1,), F32),
            shape((ROWS_DEV, feature), BF16),
        ),
        [vmem()] * (len(blocks) + 6),
        (any_space, any_space, vmem(), vmem(), smem(), vmem()),
        [
            pltpu.VMEM((feature, latents), BF16),
            pltpu.VMEM((latents, feature), BF16),
            pltpu.SemaphoreType.DMA((8,)),
        ],
        flops=6 * tokens * feature * latents,
        moved=8 * dec_weight.size,
    )(
        *[near(block) for block in blocks],
        decoder,
        near(weights_sum),
        near(inputs_t),
        near(latent_t),
        near(latent),
        near(scale),
    )
    return (
        enc_grad,
        dec_grad,
        enc_bias_grad.reshape(latents),
        dec_bias_grad,
        mean_loss,
        errors_own,
    )


def solution(mesh):
    return jax.shard_map(
        shards,
        mesh=mesh,
        in_specs=(
            P(("groups", "utt"), None),
            P(("groups", "utt")),
            P(("groups", "utt")),
            P(),
            P(),
            P(),
            P(),
            P(None, "utt"),
            P("utt"),
            P("utt", None),
            P(),
        ),
        out_specs=(
            P("groups", "utt"),
            P(("groups", "utt"), None),
            P(("groups", "utt")),
            P("groups"),
            P("groups"),
            P(("groups", "utt"), None),
        ),
        check_vma=False,
    )
```

```python
import functools

import jax
import jax.numpy as jnp
from jax import lax
from jax.experimental import pallas as pl
from jax.experimental.pallas import tpu as pltpu
from jax.sharding import PartitionSpec as P

ROWS_DEV = 8
EXTRA = 128
LANES = 128
VMEM_BYTES = 56 << 20
PINNED_BYTES = 24 << 20
PINNED_TOKENS = 256

sparsity = 0.5
epsilon = 1e-05

F32 = jnp.float32
BF16 = jnp.bfloat16

ERF_LIMIT = 3.7439211627767994
ERF_TOP = (
    0.00022905065861350646,
    0.0034082910107109506,
    0.050955695062380861,
    0.18520832239976145,
    1.128379143519084,
)
ERF_BOTTOM = (
    -1.1791602954361697e-7,
    0.000023547966471313185,
    0.0010179625278914885,
    0.014070470171167667,
    0.11098505178285362,
    0.49746925110067538,
    1.0,
)


def polynomial(x, terms):
    total = jnp.full_like(x, terms[0])
    for term in terms[1:]:
        total = total * x + term
    return total


def gelu(x):
    z = jnp.clip(x * 0.7071067811865476, -ERF_LIMIT, ERF_LIMIT)
    square = z * z
    erf = z * polynomial(square, ERF_TOP) / polynomial(square, ERF_BOTTOM)
    return 0.5 * x * (1.0 + erf)


def normalize(values, gain, shift):
    center = values - jnp.mean(values, axis=-1, keepdims=True)
    spread = jnp.mean(center * center, axis=-1, keepdims=True)
    return center * lax.rsqrt(spread + epsilon) * gain + shift


def levels(devices):
    chips = devices // 2
    outer = 1
    while outer * outer < chips:
        outer *= 2
    return outer, chips // outer


def exchange(value, bit):
    devices = lax.axis_size("utt")
    return lax.ppermute(value, "utt", [(i, i ^ bit) for i in range(devices)])


def tree(parts):
    while len(parts) > 1:
        parts = [parts[i] + parts[i + 1] for i in range(0, len(parts), 2)]
    return parts[0]


def iota(shape, dim):
    return lax.broadcasted_iota(jnp.int32, shape, dim)


def log2(n):
    return n.bit_length() - 1


def vmem():
    return pl.BlockSpec(memory_space=pltpu.VMEM)


def smem():
    return pl.BlockSpec(memory_space=pltpu.SMEM)


def launch(limit, kernel, name, out_shape, in_specs, out_specs, scratch=(), flops=0, moved=0):
    return pl.pallas_call(
        kernel,
        name=name,
        out_shape=out_shape,
        in_specs=in_specs,
        out_specs=out_specs,
        scratch_shapes=list(scratch),
        compiler_params=pltpu.CompilerParams(vmem_limit_bytes=limit),
        cost_estimate=pl.CostEstimate(flops=flops, bytes_accessed=moved, transcendentals=0),
    )


def shape(dims, kind):
    return jax.ShapeDtypeStruct(dims, kind)


def features_kernel(*refs):
    sources, out, held, second_w, sems, more = refs[:7], refs[7], refs[8:14], refs[14], refs[15], refs[16]
    small = [pltpu.make_async_copy(sources[i], held[i], sems.at[i]) for i in range(6)]
    for copy in small:
        copy.start()
    length, take, wave, first_w, gain, shift = held
    taps_first, checkpoints, channels = first_w.shape
    slots, samples = wave.shape
    frames = out.shape[0] // slots
    copies = []
    for c in range(checkpoints):
        copies.append(pltpu.make_async_copy(sources[6].at[c], second_w.at[c], more.at[c]))
        copies[-1].start()
    for copy in small:
        copy.wait()
    lane = iota((frames, samples), 1)
    start = iota((frames, samples), 0) * 10
    columns = []
    for s in range(slots):
        row = jnp.broadcast_to(wave[s : s + 1, :], (frames, samples))
        columns.append(
            [
                jnp.sum(jnp.where(lane == start + o, row, 0.0), axis=1, keepdims=True)
                for o in range(taps_first + 10)
            ]
        )
    taps = [
        jnp.concatenate(
            [columns[s][5 * tap + k] for tap in range(3) for s in range(slots)], axis=0
        )
        for k in range(taps_first)
    ]
    hidden = []
    for c in range(checkpoints):
        total = taps[0] * first_w[0, c : c + 1, :]
        for k in range(1, taps_first):
            total = total + taps[k] * first_w[k, c : c + 1, :]
        total = normalize(total, gain[c, 0:1, :], shift[c, 0:1, :])
        hidden.append(gelu(total).astype(BF16))
    rows = slots * frames
    for c in range(checkpoints):
        copies[c].wait()
        total = jnp.zeros((rows, channels), F32)
        for tap in range(3):
            total = total + jnp.dot(
                hidden[c][tap * rows : (tap + 1) * rows],
                second_w[c, tap * channels : (tap + 1) * channels, :],
                preferred_element_type=F32,
            )
        total = gelu(normalize(total, gain[c, 1:2, :], shift[c, 1:2, :]))
        if c == 0:
            spot = iota((rows, channels), 1)
            line = iota((rows, channels), 0)
            for s in range(slots):
                note = jnp.where(
                    spot == 0, length[s].astype(F32), take[s].astype(F32)
                )
                total = jnp.where(line == (s + 1) * frames - 1, note, total)
        out[:, c * channels : (c + 1) * channels] = total.astype(BF16)


def join_kernel(*refs):
    out = refs[-1]
    at = 0
    for ref in refs[1:-1]:
        out[at : at + ref.shape[0], :] = ref[...]
        at += ref.shape[0]


def norms_kernel(dec, norms, row):
    latents, feature = dec.shape
    channels = 512
    spot = iota((latents, LANES), 1)
    packed = jnp.zeros((latents, LANES), F32)
    total = jnp.zeros((latents, 1), F32)
    for c in range(feature // channels):
        block = dec[:, c * channels : (c + 1) * channels].astype(F32)
        norm = jnp.sqrt(jnp.sum(block * block, axis=1, keepdims=True) + 1e-06)
        total = total + norm
        packed = jnp.where(spot == c, norm, packed)
    norms[...] = packed
    row[...] = jnp.broadcast_to(total, (latents, LANES)).T[:8]


def encode_kernel(count, outer, inner, slots, frames, rel, *refs):
    me_ref = refs[0]
    pieces = refs[1 : 1 + count]
    enc, bias, dec, weights_sum, dec_bias = refs[1 + count : 6 + count]
    own, send, shift, inputs_out, latent_out = refs[6 + count :]
    me = me_ref[0]
    step = 2 * inner
    tokens, feature = inputs_out.shape
    rows = pieces[0].shape[0]
    held = rows // frames
    shift_frames, shift_slots = log2(frames), log2(slots)
    choose = (iota((held, rows), 1) == iota((held, rows), 0) * frames + frames - 1).astype(BF16)
    takes, starts = [], []
    for piece, bits in zip(pieces, rel):
        notes = jnp.dot(choose, piece[:, :LANES], preferred_element_type=F32)
        takes.append(notes[:, 1:2].astype(jnp.int32))
        device = me ^ ((iota((held, 1), 0) >> shift_slots) * step + bits)
        starts.append(device * ROWS_DEV)
    takes = jnp.concatenate(takes, axis=0)
    starts = jnp.concatenate(starts, axis=0)
    kinds = iota(takes.shape, 0) & (slots - 1)
    r = iota((tokens, 1), 0) >> log2(ROWS_DEV)
    holder = (
        (r & (outer - 1)) * step + ((r >> log2(outer)) & (inner - 1)) * 2 + (r >> log2(outer * inner))
    )
    token = (me ^ holder) * ROWS_DEV + (iota((tokens, 1), 0) & (ROWS_DEV - 1))
    lane = iota((1, rows), 1)
    frame = lane & (frames - 1)
    last = (iota((rows, rows), 0) == (iota((rows, rows), 1) | (frames - 1))).astype(BF16)
    ident = (iota((16, LANES), 0) == iota((16, LANES), 1)).astype(BF16)
    total = jnp.zeros((tokens, feature), F32)
    for piece, bits in zip(pieces, rel):
        turned = lax.dot_general(
            ident, piece[:, :LANES], (((1,), (1,)), ((), ())), preferred_element_type=F32
        )
        turned = jnp.dot(turned.astype(BF16), last, preferred_element_type=F32)
        size = turned[0:1, :].astype(jnp.int32)
        device = me ^ ((lane >> (shift_frames + shift_slots)) * step + bits)
        label = device * slots + ((lane >> shift_frames) & (slots - 1))
        match = takes == label
        begin = jnp.sum(jnp.where(match, starts, 0), axis=0, keepdims=True)
        second = jnp.sum(jnp.where(match, kinds, 0), axis=0, keepdims=True)
        target = begin + second * (ROWS_DEV - size) + frame
        target = jnp.where(frame < size, target, -1)
        pick = jnp.where(token == target, 1.0, 0.0).astype(BF16)
        total = total + jnp.dot(pick, piece[...], preferred_element_type=F32)
    inputs = total.astype(BF16)
    inputs_out[...] = inputs
    latent = jnp.maximum(jnp.dot(inputs, enc[...], preferred_element_type=F32) + bias[...], 0.0)
    latent_out[...] = latent
    part = jnp.dot(latent.astype(BF16), dec[...], preferred_element_type=F32)
    weighted = latent * weights_sum[0:1, :]
    extra = weighted[:, :LANES]
    for q in range(1, weighted.shape[1] // LANES):
        extra = extra + weighted[:, q * LANES : (q + 1) * LANES]
    half = tokens // 2
    own[:, :feature] = part[:half]
    own[:, feature:] = extra[:half]
    send[:, :feature] = part[half:]
    send[:, feature:] = extra[half:]
    chunk = shift.shape[0]
    shift[:, :feature] = dec_bias[...].reshape(1, feature) - inputs[:chunk].astype(F32)
    shift[:, feature:] = jnp.zeros((chunk, EXTRA), F32)


def turn_kernel(inputs, latent, norms, inputs_t, latent_t, scale):
    inputs_t[...] = inputs[...].astype(F32).T.astype(BF16)
    turned = latent[...].T
    latent_t[...] = turned.astype(BF16)
    activity = jnp.sum(turned, axis=1, keepdims=True)
    scale[...] = (sparsity * activity) / jnp.maximum(norms[...], 1e-30)


def sum_kernel(*refs):
    shift, parts, out, own = refs[1], refs[2:-2], refs[-2], refs[-1]
    wide = [part[...].astype(F32) for part in parts]
    blocks = []
    for p in range(len(parts)):
        terms = []
        for k in range(len(parts)):
            at = (p ^ k) * ROWS_DEV
            terms.append(wide[k][at : at + ROWS_DEV])
        blocks.append(tree(terms))
    errors = (jnp.concatenate(blocks, axis=0) + shift[...]).astype(BF16)
    out[...] = errors
    own[...] = errors[:ROWS_DEV, : own.shape[1]]


def gradients_kernel(count, outer, cells, *refs):
    pieces = refs[:count]
    dec, weights_sum, inputs_t, latent_t, latent, scale = refs[count : count + 6]
    enc_out, dec_out, enc_bias_out, dec_bias_out, loss_out = refs[count + 6 : count + 11]
    enc_buf, dec_buf, sems = refs[count + 11 :]
    latents, feature = dec.shape
    channels = 512
    errors = jnp.concatenate([piece[:, :feature] for piece in pieces], axis=0)
    copies = []
    parts = 4
    size = latents // parts
    for i in range(parts):
        at = slice(i * size, (i + 1) * size)
        grad = 2.0 * jnp.dot(latent_t[at], errors, preferred_element_type=F32)
        for c in range(feature // channels):
            lanes = slice(c * channels, (c + 1) * channels)
            term = scale[at, c : c + 1] * dec[at, lanes].astype(F32)
            dec_buf[at, lanes] = (grad[:, lanes] + term).astype(BF16)
        copies.append(pltpu.make_async_copy(dec_buf.at[at], dec_out.at[at], sems.at[i]))
        copies[-1].start()
    upstream = lax.dot_general(
        errors, dec[...], (((1,), (1,)), ((), ())), preferred_element_type=F32
    )
    upstream = 2.0 * upstream + sparsity * weights_sum[0:1, :]
    through = jnp.where(latent[...] > 0.0, upstream, 0.0)
    enc_bias_out[...] = jnp.sum(through, axis=0, keepdims=True)
    through = through.astype(BF16)
    size = feature // parts
    for i in range(parts):
        at = slice(i * size, (i + 1) * size)
        grad = jnp.dot(inputs_t[at], through, preferred_element_type=F32)
        enc_buf[at] = grad.astype(BF16)
        copies.append(pltpu.make_async_copy(enc_buf.at[at], enc_out.at[at], sems.at[parts + i]))
        copies[-1].start()
    wide = [piece[...].astype(F32) for piece in pieces]
    plain = tree(wide)
    squares = tree([w[:, :feature] * w[:, :feature] for w in wide])
    plain = tree([plain[i * ROWS_DEV : (i + 1) * ROWS_DEV] for i in range(outer)])
    squares = tree([squares[i * ROWS_DEV : (i + 1) * ROWS_DEV] for i in range(outer)])
    dec_bias_out[...] = 2.0 * jnp.sum(plain[:, :feature], axis=0)
    loss = jnp.sum(squares) + sparsity * jnp.sum(plain[:, feature:])
    loss_out[0] = loss / cells
    for copy in copies:
        copy.wait()


def shards(
    waveforms,
    lengths,
    take_list,
    conv_first,
    conv_second,
    norm_gain,
    norm_shift,
    enc_weight,
    enc_bias,
    dec_weight,
    dec_bias,
):
    slots = take_list.shape[0]
    devices = lax.axis_size("utt")
    outer, inner = levels(devices)
    step = 2 * inner
    tokens = ROWS_DEV * devices
    position = lax.axis_index("utt").astype(jnp.int32).reshape(1)
    feature, latents = enc_weight.shape
    checkpoints, _, channels = conv_first.shape
    frames = (waveforms.shape[1] - 10) // 10
    wide = feature + EXTRA

    pinned = tokens <= PINNED_TOKENS
    call = functools.partial(launch, PINNED_BYTES if pinned else VMEM_BYTES)

    def fast(dims, kind):
        return pltpu.VMEM(dims, kind) if pinned else shape(dims, kind)

    def near(value):
        return pltpu.with_memory_space_constraint(value, pltpu.VMEM) if pinned else value

    def far(value):
        return pltpu.with_memory_space_constraint(value, pltpu.HBM)

    kernels = conv_first.transpose(1, 0, 2)
    encoder = near(enc_weight)
    decoder = near(dec_weight)

    packed = call(
        features_kernel,
        "features",
        fast((slots * frames, feature), BF16),
        [pl.BlockSpec(memory_space=pl.ANY)] * 7,
        vmem(),
        [
            pltpu.SMEM(lengths.shape, jnp.int32),
            pltpu.SMEM(take_list.shape, jnp.int32),
            pltpu.VMEM(waveforms.shape, F32),
            pltpu.VMEM(kernels.shape, F32),
            pltpu.VMEM(norm_gain.shape, F32),
            pltpu.VMEM(norm_shift.shape, F32),
            pltpu.VMEM(conv_second.shape, BF16),
            pltpu.SemaphoreType.DMA((6,)),
            pltpu.SemaphoreType.DMA((checkpoints,)),
        ],
        flops=2 * slots * frames * feature * 3 * channels,
        moved=2 * conv_second.size,
    )(
        *[
            far(value)
            for value in (lengths, take_list, waveforms, kernels, norm_gain, norm_shift, conv_second)
        ]
    )

    norms, weights_sum = call(
        norms_kernel,
        "norms",
        (fast((latents, LANES), F32), fast((8, latents), F32)),
        [vmem()],
        (vmem(), vmem()),
        flops=4 * dec_weight.size,
        moved=2 * dec_weight.size,
    )(decoder)

    blocks = [packed] + [exchange(packed, step * k) for k in range(1, outer)]
    pieces = [
        call(
            join_kernel,
            "join",
            fast((outer * slots * frames, feature), BF16),
            [pl.BlockSpec(memory_space=pl.ANY)] + [vmem()] * outer,
            vmem(),
            moved=4 * outer * slots * frames * feature,
        )(near(norms), *[near(block) for block in blocks])
    ]
    rel = [0]
    bit = 2
    while bit < step:
        pieces += [exchange(piece, bit) for piece in pieces]
        rel += [r ^ bit for r in rel]
        bit *= 2
    pieces += [exchange(piece, 1) for piece in pieces]
    rel += [r ^ 1 for r in rel]

    half = tokens // 2
    chunk = half // inner

    def encode(*refs):
        encode_kernel(len(pieces), outer, inner, slots, frames, rel, *refs)

    own, send, shift, inputs, latent = call(
        encode,
        "encode",
        (
            fast((half, wide), F32),
            fast((half, wide), F32),
            fast((chunk, wide), F32),
            fast((tokens, feature), BF16),
            fast((tokens, latents), F32),
        ),
        [smem()] + [vmem()] * (len(pieces) + 5),
        (vmem(),) * 5,
        flops=4 * tokens * feature * latents,
        moved=4 * dec_weight.size,
    )(
        position,
        *[near(piece) for piece in pieces],
        encoder,
        enc_bias.reshape(1, latents),
        decoder,
        near(weights_sum),
        dec_bias,
    )

    inputs_t, latent_t, scale = call(
        turn_kernel,
        "turn",
        (fast((feature, tokens), BF16), fast((latents, tokens), BF16), fast((latents, LANES), F32)),
        [vmem()] * 3,
        (vmem(),) * 3,
        flops=2 * tokens * feature,
        moved=4 * tokens * feature,
    )(near(inputs), near(latent), near(norms))

    part = own + exchange(send, 1)
    small = part.astype(BF16)
    total = part[:chunk]
    for k in range(1, inner):
        total = total + exchange(small[k * chunk : (k + 1) * chunk], 2 * k).astype(F32)
    total = total.astype(BF16)
    blocks = [total] + [exchange(total, step * k) for k in range(1, outer)]
    errors, errors_own = call(
        sum_kernel,
        "sum",
        (fast((chunk, wide), BF16), shape((ROWS_DEV, feature), BF16)),
        [pl.BlockSpec(memory_space=pl.ANY)] + [vmem()] * (1 + outer),
        (vmem(), vmem()),
        moved=8 * chunk * wide,
    )(near(scale), near(shift), *[near(block) for block in blocks])
    blocks = [errors]
    bit = 2
    while bit < step:
        blocks += [exchange(block, bit) for block in blocks]
        bit *= 2
    blocks += [exchange(block, 1) for block in blocks]

    def gradients(*refs):
        gradients_kernel(len(blocks), outer, float(tokens * feature), *refs)

    any_space = pl.BlockSpec(memory_space=pl.ANY)
    enc_grad, dec_grad, enc_bias_grad, dec_bias_grad, mean_loss = call(
        gradients,
        "gradients",
        (
            shape((feature, latents), BF16),
            shape((latents, feature), BF16),
            shape((1, latents), F32),
            shape((feature,), F32),
            shape((1,), F32),
        ),
        [vmem()] * (len(blocks) + 6),
        (any_space, any_space, vmem(), vmem(), smem()),
        [
            pltpu.VMEM((feature, latents), BF16),
            pltpu.VMEM((latents, feature), BF16),
            pltpu.SemaphoreType.DMA((8,)),
        ],
        flops=6 * tokens * feature * latents,
        moved=8 * dec_weight.size,
    )(
        *[near(block) for block in blocks],
        decoder,
        near(weights_sum),
        near(inputs_t),
        near(latent_t),
        near(latent),
        near(scale),
    )
    return (
        enc_grad,
        dec_grad,
        enc_bias_grad.reshape(latents),
        dec_bias_grad,
        mean_loss,
        errors_own,
    )


def solution(mesh):
    return jax.shard_map(
        shards,
        mesh=mesh,
        in_specs=(
            P(("groups", "utt"), None),
            P(("groups", "utt")),
            P(("groups", "utt")),
            P(),
            P(),
            P(),
            P(),
            P(None, "utt"),
            P("utt"),
            P("utt", None),
            P(),
        ),
        out_specs=(
            P("groups", "utt"),
            P(("groups", "utt"), None),
            P(("groups", "utt")),
            P("groups"),
            P("groups"),
            P(("groups", "utt"), None),
        ),
        check_vma=False,
    )
```

```python
import functools

import jax
import jax.numpy as jnp
from jax import lax
from jax.experimental import pallas as pl
from jax.experimental.pallas import tpu as pltpu
from jax.sharding import PartitionSpec as P

ROWS_DEV = 8
EXTRA = 128
LANES = 128
VMEM_BYTES = 56 << 20
PINNED_BYTES = 24 << 20
PINNED_TOKENS = 256

sparsity = 0.5
epsilon = 1e-05

F32 = jnp.float32
BF16 = jnp.bfloat16

ERF_LIMIT = 3.7439211627767994
ERF_TOP = (
    0.00022905065861350646,
    0.0034082910107109506,
    0.050955695062380861,
    0.18520832239976145,
    1.128379143519084,
)
ERF_BOTTOM = (
    -1.1791602954361697e-7,
    0.000023547966471313185,
    0.0010179625278914885,
    0.014070470171167667,
    0.11098505178285362,
    0.49746925110067538,
    1.0,
)


def polynomial(x, terms):
    total = jnp.full_like(x, terms[0])
    for term in terms[1:]:
        total = total * x + term
    return total


def gelu(x):
    z = jnp.clip(x * 0.7071067811865476, -ERF_LIMIT, ERF_LIMIT)
    square = z * z
    erf = z * polynomial(square, ERF_TOP) / polynomial(square, ERF_BOTTOM)
    return 0.5 * x * (1.0 + erf)


def normalize(values, gain, shift):
    center = values - jnp.mean(values, axis=-1, keepdims=True)
    spread = jnp.mean(center * center, axis=-1, keepdims=True)
    return center * lax.rsqrt(spread + epsilon) * gain + shift


def levels(devices):
    chips = devices // 2
    outer = 1
    while outer * outer < chips:
        outer *= 2
    return outer, chips // outer


def exchange(value, bit):
    devices = lax.axis_size("utt")
    return lax.ppermute(value, "utt", [(i, i ^ bit) for i in range(devices)])


def tree(parts):
    while len(parts) > 1:
        parts = [parts[i] + parts[i + 1] for i in range(0, len(parts), 2)]
    return parts[0]


def iota(shape, dim):
    return lax.broadcasted_iota(jnp.int32, shape, dim)


def log2(n):
    return n.bit_length() - 1


def vmem():
    return pl.BlockSpec(memory_space=pltpu.VMEM)


def smem():
    return pl.BlockSpec(memory_space=pltpu.SMEM)


def launch(limit, kernel, name, out_shape, in_specs, out_specs, scratch=(), flops=0, moved=0):
    return pl.pallas_call(
        kernel,
        name=name,
        out_shape=out_shape,
        in_specs=in_specs,
        out_specs=out_specs,
        scratch_shapes=list(scratch),
        compiler_params=pltpu.CompilerParams(vmem_limit_bytes=limit),
        cost_estimate=pl.CostEstimate(flops=flops, bytes_accessed=moved, transcendentals=0),
    )


def shape(dims, kind):
    return jax.ShapeDtypeStruct(dims, kind)


def features_kernel(*refs):
    sources, out, held, second_w, sems, more = refs[:7], refs[7], refs[8:14], refs[14], refs[15], refs[16]
    small = [pltpu.make_async_copy(sources[i], held[i], sems.at[i]) for i in range(6)]
    for copy in small:
        copy.start()
    length, take, wave, first_w, gain, shift = held
    taps_first, checkpoints, channels = first_w.shape
    slots, samples = wave.shape
    frames = out.shape[0] // slots
    copies = []
    for c in range(checkpoints):
        copies.append(pltpu.make_async_copy(sources[6].at[c], second_w.at[c], more.at[c]))
        copies[-1].start()
    for copy in small:
        copy.wait()
    lane = iota((frames, samples), 1)
    start = iota((frames, samples), 0) * 10
    columns = []
    for s in range(slots):
        row = jnp.broadcast_to(wave[s : s + 1, :], (frames, samples))
        columns.append(
            [
                jnp.sum(jnp.where(lane == start + o, row, 0.0), axis=1, keepdims=True)
                for o in range(taps_first + 10)
            ]
        )
    taps = [
        jnp.concatenate(
            [columns[s][5 * tap + k] for tap in range(3) for s in range(slots)], axis=0
        )
        for k in range(taps_first)
    ]

    def layer_one(c):
        total = taps[0] * first_w[0, c : c + 1, :]
        for k in range(1, taps_first):
            total = total + taps[k] * first_w[k, c : c + 1, :]
        return gelu(normalize(total, gain[c, 0:1, :], shift[c, 0:1, :])).astype(BF16)

    rows = slots * frames

    def layer_two(c, hidden):
        total = jnp.zeros((rows, channels), F32)
        for tap in range(3):
            total = total + jnp.dot(
                hidden[tap * rows : (tap + 1) * rows],
                second_w[c, tap * channels : (tap + 1) * channels, :],
                preferred_element_type=F32,
            )
        return total

    def finish(c, total):
        total = gelu(normalize(total, gain[c, 1:2, :], shift[c, 1:2, :]))
        if c == 0:
            spot = iota((rows, channels), 1)
            line = iota((rows, channels), 0)
            for s in range(slots):
                note = jnp.where(spot == 0, length[s].astype(F32), take[s].astype(F32))
                total = jnp.where(line == (s + 1) * frames - 1, note, total)
        out[:, c * channels : (c + 1) * channels] = total.astype(BF16)

    hidden = layer_one(0)
    held_back = None
    for c in range(checkpoints):
        copies[c].wait()
        total = layer_two(c, hidden)
        if c + 1 < checkpoints:
            hidden = layer_one(c + 1)
        if held_back is not None:
            finish(c - 1, held_back)
        held_back = total
    finish(checkpoints - 1, held_back)


def join_kernel(*refs):
    out = refs[-1]
    at = 0
    for ref in refs[1:-1]:
        out[at : at + ref.shape[0], :] = ref[...]
        at += ref.shape[0]


def norms_kernel(dec, norms, row):
    latents, feature = dec.shape
    channels = 512
    spot = iota((latents, LANES), 1)
    packed = jnp.zeros((latents, LANES), F32)
    total = jnp.zeros((latents, 1), F32)
    for c in range(feature // channels):
        block = dec[:, c * channels : (c + 1) * channels].astype(F32)
        norm = jnp.sqrt(jnp.sum(block * block, axis=1, keepdims=True) + 1e-06)
        total = total + norm
        packed = jnp.where(spot == c, norm, packed)
    norms[...] = packed
    row[...] = jnp.broadcast_to(total, (latents, LANES)).T[:8]


def encode_kernel(count, outer, inner, slots, frames, rel, *refs):
    me_ref = refs[0]
    pieces = refs[1 : 1 + count]
    enc, bias, dec, weights_sum, dec_bias = refs[1 + count : 6 + count]
    own, send, shift, inputs_out, latent_out = refs[6 + count :]
    me = me_ref[0]
    step = 2 * inner
    tokens, feature = inputs_out.shape
    rows = pieces[0].shape[0]
    held = rows // frames
    shift_frames, shift_slots = log2(frames), log2(slots)
    choose = (iota((held, rows), 1) == iota((held, rows), 0) * frames + frames - 1).astype(BF16)
    takes, starts = [], []
    for piece, bits in zip(pieces, rel):
        notes = jnp.dot(choose, piece[:, :LANES], preferred_element_type=F32)
        takes.append(notes[:, 1:2].astype(jnp.int32))
        device = me ^ ((iota((held, 1), 0) >> shift_slots) * step + bits)
        starts.append(device * ROWS_DEV)
    takes = jnp.concatenate(takes, axis=0)
    starts = jnp.concatenate(starts, axis=0)
    kinds = iota(takes.shape, 0) & (slots - 1)
    r = iota((tokens, 1), 0) >> log2(ROWS_DEV)
    holder = (
        ((r >> log2(inner)) & (outer - 1)) * step + (r & (inner - 1)) * 2 + (r >> log2(outer * inner))
    )
    token = (me ^ holder) * ROWS_DEV + (iota((tokens, 1), 0) & (ROWS_DEV - 1))
    lane = iota((1, rows), 1)
    frame = lane & (frames - 1)
    last = (iota((rows, rows), 0) == (iota((rows, rows), 1) | (frames - 1))).astype(BF16)
    ident = (iota((16, LANES), 0) == iota((16, LANES), 1)).astype(BF16)
    total = jnp.zeros((tokens, feature), F32)
    for piece, bits in zip(pieces, rel):
        turned = lax.dot_general(
            ident, piece[:, :LANES], (((1,), (1,)), ((), ())), preferred_element_type=F32
        )
        turned = jnp.dot(turned.astype(BF16), last, preferred_element_type=F32)
        size = turned[0:1, :].astype(jnp.int32)
        device = me ^ ((lane >> (shift_frames + shift_slots)) * step + bits)
        label = device * slots + ((lane >> shift_frames) & (slots - 1))
        match = takes == label
        begin = jnp.sum(jnp.where(match, starts, 0), axis=0, keepdims=True)
        second = jnp.sum(jnp.where(match, kinds, 0), axis=0, keepdims=True)
        target = begin + second * (ROWS_DEV - size) + frame
        target = jnp.where(frame < size, target, -1)
        pick = jnp.where(token == target, 1.0, 0.0).astype(BF16)
        total = total + jnp.dot(pick, piece[...], preferred_element_type=F32)
    inputs = total.astype(BF16)
    inputs_out[...] = inputs
    latent = jnp.maximum(jnp.dot(inputs, enc[...], preferred_element_type=F32) + bias[...], 0.0)
    latent_out[...] = latent
    part = jnp.dot(latent.astype(BF16), dec[...], preferred_element_type=F32)
    weighted = latent * weights_sum[0:1, :]
    extra = weighted[:, :LANES]
    for q in range(1, weighted.shape[1] // LANES):
        extra = extra + weighted[:, q * LANES : (q + 1) * LANES]
    half = tokens // 2
    own[:, :feature] = part[:half]
    own[:, feature:] = extra[:half]
    send[:, :feature] = part[half:]
    send[:, feature:] = extra[half:]
    chunk = shift.shape[0]
    shift[:, :feature] = dec_bias[...].reshape(1, feature) - inputs[:chunk].astype(F32)
    shift[:, feature:] = jnp.zeros((chunk, EXTRA), F32)


def turn_kernel(inputs, latent, norms, inputs_t, latent_t, scale):
    inputs_t[...] = inputs[...].astype(F32).T.astype(BF16)
    turned = latent[...].T
    latent_t[...] = turned.astype(BF16)
    activity = jnp.sum(turned, axis=1, keepdims=True)
    scale[...] = (sparsity * activity) / jnp.maximum(norms[...], 1e-30)


def sum_kernel(*refs):
    total = refs[1][...]
    for ref in refs[2:-1]:
        total = total + ref[...].astype(F32)
    refs[-1][...] = total.astype(BF16)


def gradients_kernel(count, inner, cells, *refs):
    pieces = refs[:count]
    dec, weights_sum, inputs_t, latent_t, latent, scale = refs[count : count + 6]
    enc_out, dec_out, enc_bias_out, dec_bias_out, loss_out, errors_out = refs[count + 6 : count + 12]
    enc_buf, dec_buf, sems = refs[count + 12 :]
    latents, feature = dec.shape
    channels = 512
    errors = jnp.concatenate([piece[:, :feature] for piece in pieces], axis=0)
    copies = []
    parts = 4
    size = latents // parts
    for i in range(parts):
        at = slice(i * size, (i + 1) * size)
        grad = 2.0 * jnp.dot(latent_t[at], errors, preferred_element_type=F32)
        for c in range(feature // channels):
            lanes = slice(c * channels, (c + 1) * channels)
            term = scale[at, c : c + 1] * dec[at, lanes].astype(F32)
            dec_buf[at, lanes] = (grad[:, lanes] + term).astype(BF16)
        copies.append(pltpu.make_async_copy(dec_buf.at[at], dec_out.at[at], sems.at[i]))
        copies[-1].start()
    upstream = lax.dot_general(
        errors, dec[...], (((1,), (1,)), ((), ())), preferred_element_type=F32
    )
    upstream = 2.0 * upstream + sparsity * weights_sum[0:1, :]
    through = jnp.where(latent[...] > 0.0, upstream, 0.0)
    enc_bias_out[...] = jnp.sum(through, axis=0, keepdims=True)
    through = through.astype(BF16)
    size = feature // parts
    for i in range(parts):
        at = slice(i * size, (i + 1) * size)
        grad = jnp.dot(inputs_t[at], through, preferred_element_type=F32)
        enc_buf[at] = grad.astype(BF16)
        copies.append(pltpu.make_async_copy(enc_buf.at[at], enc_out.at[at], sems.at[parts + i]))
        copies[-1].start()
    errors_out[...] = pieces[0][:ROWS_DEV, :feature]
    wide = [piece[...].astype(F32) for piece in pieces]
    plain = tree(wide)
    squares = tree([w[:, :feature] * w[:, :feature] for w in wide])
    plain = tree([plain[i * ROWS_DEV : (i + 1) * ROWS_DEV] for i in range(inner)])
    squares = tree([squares[i * ROWS_DEV : (i + 1) * ROWS_DEV] for i in range(inner)])
    dec_bias_out[...] = 2.0 * jnp.sum(plain[:, :feature], axis=0)
    loss = jnp.sum(squares) + sparsity * jnp.sum(plain[:, feature:])
    loss_out[0] = loss / cells
    for copy in copies:
        copy.wait()


def shards(
    waveforms,
    lengths,
    take_list,
    conv_first,
    conv_second,
    norm_gain,
    norm_shift,
    enc_weight,
    enc_bias,
    dec_weight,
    dec_bias,
):
    slots = take_list.shape[0]
    devices = lax.axis_size("utt")
    outer, inner = levels(devices)
    step = 2 * inner
    tokens = ROWS_DEV * devices
    position = lax.axis_index("utt").astype(jnp.int32).reshape(1)
    feature, latents = enc_weight.shape
    checkpoints, _, channels = conv_first.shape
    frames = (waveforms.shape[1] - 10) // 10
    wide = feature + EXTRA

    pinned = tokens <= PINNED_TOKENS
    call = functools.partial(launch, PINNED_BYTES if pinned else VMEM_BYTES)

    def fast(dims, kind):
        return pltpu.VMEM(dims, kind) if pinned else shape(dims, kind)

    def near(value):
        return pltpu.with_memory_space_constraint(value, pltpu.VMEM) if pinned else value

    def far(value):
        return pltpu.with_memory_space_constraint(value, pltpu.HBM)

    kernels = conv_first.transpose(1, 0, 2)
    encoder = near(enc_weight)
    decoder = near(dec_weight)

    packed = call(
        features_kernel,
        "features",
        fast((slots * frames, feature), BF16),
        [pl.BlockSpec(memory_space=pl.ANY)] * 7,
        vmem(),
        [
            pltpu.SMEM(lengths.shape, jnp.int32),
            pltpu.SMEM(take_list.shape, jnp.int32),
            pltpu.VMEM(waveforms.shape, F32),
            pltpu.VMEM(kernels.shape, F32),
            pltpu.VMEM(norm_gain.shape, F32),
            pltpu.VMEM(norm_shift.shape, F32),
            pltpu.VMEM(conv_second.shape, BF16),
            pltpu.SemaphoreType.DMA((6,)),
            pltpu.SemaphoreType.DMA((checkpoints,)),
        ],
        flops=2 * slots * frames * feature * 3 * channels,
        moved=2 * conv_second.size,
    )(
        *[
            far(value)
            for value in (lengths, take_list, waveforms, kernels, norm_gain, norm_shift, conv_second)
        ]
    )

    norms, weights_sum = call(
        norms_kernel,
        "norms",
        (fast((latents, LANES), F32), fast((8, latents), F32)),
        [vmem()],
        (vmem(), vmem()),
        flops=4 * dec_weight.size,
        moved=2 * dec_weight.size,
    )(decoder)

    blocks = [packed] + [exchange(packed, step * k) for k in range(1, outer)]
    pieces = [
        call(
            join_kernel,
            "join",
            fast((outer * slots * frames, feature), BF16),
            [pl.BlockSpec(memory_space=pl.ANY)] + [vmem()] * outer,
            vmem(),
            moved=4 * outer * slots * frames * feature,
        )(near(norms), *[near(block) for block in blocks])
    ]
    rel = [0]
    bit = 2
    while bit < step:
        pieces += [exchange(piece, bit) for piece in pieces]
        rel += [r ^ bit for r in rel]
        bit *= 2
    pieces += [exchange(piece, 1) for piece in pieces]
    rel += [r ^ 1 for r in rel]

    half = tokens // 2
    chunk = half // outer

    def encode(*refs):
        encode_kernel(len(pieces), outer, inner, slots, frames, rel, *refs)

    own, send, shift, inputs, latent = call(
        encode,
        "encode",
        (
            fast((half, wide), F32),
            fast((half, wide), F32),
            fast((chunk, wide), F32),
            fast((tokens, feature), BF16),
            fast((tokens, latents), F32),
        ),
        [smem()] + [vmem()] * (len(pieces) + 5),
        (vmem(),) * 5,
        flops=4 * tokens * feature * latents,
        moved=4 * dec_weight.size,
    )(
        position,
        *[near(piece) for piece in pieces],
        encoder,
        enc_bias.reshape(1, latents),
        decoder,
        near(weights_sum),
        dec_bias,
    )

    inputs_t, latent_t, scale = call(
        turn_kernel,
        "turn",
        (fast((feature, tokens), BF16), fast((latents, tokens), BF16), fast((latents, LANES), F32)),
        [vmem()] * 3,
        (vmem(),) * 3,
        flops=2 * tokens * feature,
        moved=4 * tokens * feature,
    )(near(inputs), near(latent), near(norms))

    part = own + exchange(send, 1)
    small = part.astype(BF16)
    blocks = [part[:chunk]]
    for k in range(1, outer):
        blocks.append(exchange(small[k * chunk : (k + 1) * chunk], step * k))
    total = call(
        sum_kernel,
        "sum",
        fast((chunk, wide), BF16),
        [pl.BlockSpec(memory_space=pl.ANY)] + [vmem()] * outer,
        vmem(),
        moved=8 * chunk * wide,
    )(near(scale), *[near(block) for block in blocks])
    bit = 2
    while bit < step:
        width = (bit // 2) * ROWS_DEV
        other = exchange(total, bit).astype(F32).reshape(-1, 2, width, wide)
        part = total.astype(F32) + other[:, ::-1].reshape(chunk, wide)
        total = part.astype(BF16)
        bit *= 2
    errors = (part + shift).astype(BF16)
    blocks = [errors] + [exchange(errors, step * k) for k in range(1, outer)]
    blocks += [exchange(block, 1) for block in blocks]

    def gradients(*refs):
        gradients_kernel(len(blocks), inner, float(tokens * feature), *refs)

    any_space = pl.BlockSpec(memory_space=pl.ANY)
    enc_grad, dec_grad, enc_bias_grad, dec_bias_grad, mean_loss, errors_own = call(
        gradients,
        "gradients",
        (
            shape((feature, latents), BF16),
            shape((latents, feature), BF16),
            shape((1, latents), F32),
            shape((feature,), F32),
            shape((1,), F32),
            shape((ROWS_DEV, feature), BF16),
        ),
        [vmem()] * (len(blocks) + 6),
        (any_space, any_space, vmem(), vmem(), smem(), vmem()),
        [
            pltpu.VMEM((feature, latents), BF16),
            pltpu.VMEM((latents, feature), BF16),
            pltpu.SemaphoreType.DMA((8,)),
        ],
        flops=6 * tokens * feature * latents,
        moved=8 * dec_weight.size,
    )(
        *[near(block) for block in blocks],
        decoder,
        near(weights_sum),
        near(inputs_t),
        near(latent_t),
        near(latent),
        near(scale),
    )
    return (
        enc_grad,
        dec_grad,
        enc_bias_grad.reshape(latents),
        dec_bias_grad,
        mean_loss,
        errors_own,
    )


def solution(mesh):
    return jax.shard_map(
        shards,
        mesh=mesh,
        in_specs=(
            P(("groups", "utt"), None),
            P(("groups", "utt")),
            P(("groups", "utt")),
            P(),
            P(),
            P(),
            P(),
            P(None, "utt"),
            P("utt"),
            P("utt", None),
            P(),
        ),
        out_specs=(
            P("groups", "utt"),
            P(("groups", "utt"), None),
            P(("groups", "utt")),
            P("groups"),
            P("groups"),
            P(("groups", "utt"), None),
        ),
        check_vma=False,
    )
```

```python
import functools

import jax
import jax.numpy as jnp
from jax import lax
from jax.experimental import pallas as pl
from jax.experimental.pallas import tpu as pltpu
from jax.sharding import PartitionSpec as P

ROWS_DEV = 8
EXTRA = 128
LANES = 128
VMEM_BYTES = 56 << 20
PINNED_BYTES = 24 << 20
PINNED_TOKENS = 256
GROUP_ROWS = 256

sparsity = 0.5
epsilon = 1e-05

F32 = jnp.float32
BF16 = jnp.bfloat16

ERF_LIMIT = 3.7439211627767994
ERF_TOP = (
    0.00022905065861350646,
    0.0034082910107109506,
    0.050955695062380861,
    0.18520832239976145,
    1.128379143519084,
)
ERF_BOTTOM = (
    -1.1791602954361697e-7,
    0.000023547966471313185,
    0.0010179625278914885,
    0.014070470171167667,
    0.11098505178285362,
    0.49746925110067538,
    1.0,
)


def polynomial(x, terms):
    total = jnp.full_like(x, terms[0])
    for term in terms[1:]:
        total = total * x + term
    return total


def gelu(x):
    z = jnp.clip(x * 0.7071067811865476, -ERF_LIMIT, ERF_LIMIT)
    square = z * z
    erf = z * polynomial(square, ERF_TOP) / polynomial(square, ERF_BOTTOM)
    return 0.5 * x * (1.0 + erf)


def normalize(values, gain, shift):
    center = values - jnp.mean(values, axis=-1, keepdims=True)
    spread = jnp.mean(center * center, axis=-1, keepdims=True)
    return center * lax.rsqrt(spread + epsilon) * gain + shift


def levels(devices):
    chips = devices // 2
    outer = 1
    while outer * outer < chips:
        outer *= 2
    return outer, chips // outer


def exchange(value, bit):
    devices = lax.axis_size("utt")
    return lax.ppermute(value, "utt", [(i, i ^ bit) for i in range(devices)])


def tree(parts):
    while len(parts) > 1:
        parts = [parts[i] + parts[i + 1] for i in range(0, len(parts), 2)]
    return parts[0]


def iota(shape, dim):
    return lax.broadcasted_iota(jnp.int32, shape, dim)


def log2(n):
    return n.bit_length() - 1


def vmem():
    return pl.BlockSpec(memory_space=pltpu.VMEM)


def smem():
    return pl.BlockSpec(memory_space=pltpu.SMEM)


def launch(limit, kernel, name, out_shape, in_specs, out_specs, scratch=(), flops=0, moved=0):
    return pl.pallas_call(
        kernel,
        name=name,
        out_shape=out_shape,
        in_specs=in_specs,
        out_specs=out_specs,
        scratch_shapes=list(scratch),
        compiler_params=pltpu.CompilerParams(vmem_limit_bytes=limit),
        cost_estimate=pl.CostEstimate(flops=flops, bytes_accessed=moved, transcendentals=0),
    )


def shape(dims, kind):
    return jax.ShapeDtypeStruct(dims, kind)


def features_kernel(*refs):
    sources, out, held, second_w, sems, more = refs[:7], refs[7], refs[8:14], refs[14], refs[15], refs[16]
    small = [pltpu.make_async_copy(sources[i], held[i], sems.at[i]) for i in range(6)]
    for copy in small:
        copy.start()
    length, take, wave, first_w, gain, shift = held
    taps_first, checkpoints, channels = first_w.shape
    slots, samples = wave.shape
    frames = out.shape[0] // slots
    copies = []
    for c in range(checkpoints):
        copies.append(pltpu.make_async_copy(sources[6].at[c], second_w.at[c], more.at[c]))
        copies[-1].start()
    for copy in small:
        copy.wait()
    lane = iota((frames, samples), 1)
    start = iota((frames, samples), 0) * 10
    columns = []
    for s in range(slots):
        row = jnp.broadcast_to(wave[s : s + 1, :], (frames, samples))
        columns.append(
            [
                jnp.sum(jnp.where(lane == start + o, row, 0.0), axis=1, keepdims=True)
                for o in range(taps_first + 10)
            ]
        )
    taps = [
        jnp.concatenate(
            [columns[s][5 * tap + k] for tap in range(3) for s in range(slots)], axis=0
        )
        for k in range(taps_first)
    ]

    def layer_one(c):
        total = taps[0] * first_w[0, c : c + 1, :]
        for k in range(1, taps_first):
            total = total + taps[k] * first_w[k, c : c + 1, :]
        return gelu(normalize(total, gain[c, 0:1, :], shift[c, 0:1, :])).astype(BF16)

    rows = slots * frames

    def layer_two(c, hidden):
        total = jnp.zeros((rows, channels), F32)
        for tap in range(3):
            total = total + jnp.dot(
                hidden[tap * rows : (tap + 1) * rows],
                second_w[c, tap * channels : (tap + 1) * channels, :],
                preferred_element_type=F32,
            )
        return total

    def finish(c, total):
        total = gelu(normalize(total, gain[c, 1:2, :], shift[c, 1:2, :]))
        if c == 0:
            spot = iota((rows, channels), 1)
            line = iota((rows, channels), 0)
            for s in range(slots):
                note = jnp.where(spot == 0, length[s].astype(F32), take[s].astype(F32))
                total = jnp.where(line == (s + 1) * frames - 1, note, total)
        out[:, c * channels : (c + 1) * channels] = total.astype(BF16)

    hidden = layer_one(0)
    held_back = None
    for c in range(checkpoints):
        copies[c].wait()
        total = layer_two(c, hidden)
        if c + 1 < checkpoints:
            hidden = layer_one(c + 1)
        if held_back is not None:
            finish(c - 1, held_back)
        held_back = total
    finish(checkpoints - 1, held_back)


def join_kernel(*refs):
    out = refs[-1]
    at = 0
    for ref in refs[:-1]:
        out[at : at + ref.shape[0], :] = ref[...]
        at += ref.shape[0]


def norms_kernel(dec, norms, row):
    latents, feature = dec.shape
    channels = 512
    spot = iota((latents, LANES), 1)
    packed = jnp.zeros((latents, LANES), F32)
    total = jnp.zeros((latents, 1), F32)
    for c in range(feature // channels):
        block = dec[:, c * channels : (c + 1) * channels].astype(F32)
        norm = jnp.sqrt(jnp.sum(block * block, axis=1, keepdims=True) + 1e-06)
        total = total + norm
        packed = jnp.where(spot == c, norm, packed)
    norms[...] = packed
    row[...] = jnp.broadcast_to(total, (latents, LANES)).T[:8]


def encode_kernel(count, outer, inner, slots, frames, *refs):
    me_ref = refs[0]
    pieces = refs[1 : 1 + count]
    enc, bias, dec, weights_sum, dec_bias = refs[1 + count : 6 + count]
    own, send, shift, inputs_out, latent_out = refs[6 + count :]
    me = me_ref[0]
    step = 2 * inner
    tokens, feature = inputs_out.shape
    rows = pieces[0].shape[0]
    group = max(GROUP_ROWS // rows, 1)
    width = group * rows
    held = width // frames
    shift_frames, shift_slots = log2(frames), log2(slots)

    def device_of(place):
        bits = (place & (outer - 1)) * step
        bits = bits + ((place >> log2(outer)) & (inner - 1)) * 2 + (place >> log2(outer * inner))
        return me ^ bits

    choose = (iota((held, width), 1) == iota((held, width), 0) * frames + frames - 1).astype(BF16)
    last = (iota((width, width), 0) == (iota((width, width), 1) | (frames - 1))).astype(BF16)
    ident = (iota((16, LANES), 0) == iota((16, LANES), 1)).astype(BF16)
    groups, takes, starts = [], [], []
    for g in range(0, len(pieces), group):
        parts = [piece[...] for piece in pieces[g : g + group]]
        groups.append(parts[0] if group == 1 else jnp.concatenate(parts, axis=0))
        notes = jnp.dot(choose, groups[-1][:, :LANES], preferred_element_type=F32)
        takes.append(notes[:, 1:2].astype(jnp.int32))
        slot = g * rows // frames + iota((held, 1), 0)
        starts.append(device_of(slot >> shift_slots) * ROWS_DEV)
    takes = jnp.concatenate(takes, axis=0)
    starts = jnp.concatenate(starts, axis=0)
    kinds = iota(takes.shape, 0) & (slots - 1)
    r = iota((tokens, 1), 0) >> log2(ROWS_DEV)
    holder = (
        ((r >> log2(inner)) & (outer - 1)) * step + (r & (inner - 1)) * 2 + (r >> log2(outer * inner))
    )
    token = (me ^ holder) * ROWS_DEV + (iota((tokens, 1), 0) & (ROWS_DEV - 1))
    lane = iota((1, width), 1)
    frame = lane & (frames - 1)
    total = jnp.zeros((tokens, feature), F32)
    for g, block in enumerate(groups):
        turned = lax.dot_general(
            ident, block[:, :LANES], (((1,), (1,)), ((), ())), preferred_element_type=F32
        )
        turned = jnp.dot(turned.astype(BF16), last, preferred_element_type=F32)
        size = turned[0:1, :].astype(jnp.int32)
        device = device_of((g * width + lane) >> (shift_frames + shift_slots))
        label = device * slots + ((lane >> shift_frames) & (slots - 1))
        match = takes == label
        begin = jnp.sum(jnp.where(match, starts, 0), axis=0, keepdims=True)
        second = jnp.sum(jnp.where(match, kinds, 0), axis=0, keepdims=True)
        target = begin + second * (ROWS_DEV - size) + frame
        target = jnp.where(frame < size, target, -1)
        pick = jnp.where(token == target, 1.0, 0.0).astype(BF16)
        total = total + jnp.dot(pick, block, preferred_element_type=F32)
    inputs = total.astype(BF16)
    inputs_out[...] = inputs
    latent = jnp.maximum(jnp.dot(inputs, enc[...], preferred_element_type=F32) + bias[...], 0.0)
    latent_out[...] = latent
    part = jnp.dot(latent.astype(BF16), dec[...], preferred_element_type=F32)
    weighted = latent * weights_sum[0:1, :]
    extra = weighted[:, :LANES]
    for q in range(1, weighted.shape[1] // LANES):
        extra = extra + weighted[:, q * LANES : (q + 1) * LANES]
    half = tokens // 2
    own[:, :feature] = part[:half]
    own[:, feature:] = extra[:half]
    send[:, :feature] = part[half:]
    send[:, feature:] = extra[half:]
    chunk = shift.shape[0]
    shift[:, :feature] = dec_bias[...].reshape(1, feature) - inputs[:chunk].astype(F32)
    shift[:, feature:] = jnp.zeros((chunk, EXTRA), F32)


def turn_kernel(inputs, latent, norms, inputs_t, latent_t, scale):
    inputs_t[...] = inputs[...].astype(F32).T.astype(BF16)
    turned = latent[...].T
    latent_t[...] = turned.astype(BF16)
    activity = jnp.sum(turned, axis=1, keepdims=True)
    scale[...] = (sparsity * activity) / jnp.maximum(norms[...], 1e-30)


def sum_kernel(*refs):
    total = refs[1][...]
    for ref in refs[2:-1]:
        total = total + ref[...].astype(F32)
    refs[-1][...] = total.astype(BF16)


def gradients_kernel(count, inner, cells, *refs):
    pieces = refs[:count]
    dec, weights_sum, inputs_t, latent_t, latent, scale = refs[count : count + 6]
    enc_out, dec_out, enc_bias_out, dec_bias_out, loss_out, errors_out = refs[count + 6 : count + 12]
    enc_buf, dec_buf, sems = refs[count + 12 :]
    latents, feature = dec.shape
    channels = 512
    errors = jnp.concatenate([piece[:, :feature] for piece in pieces], axis=0)
    copies = []
    parts = 4
    size = latents // parts
    for i in range(parts):
        at = slice(i * size, (i + 1) * size)
        grad = 2.0 * jnp.dot(latent_t[at], errors, preferred_element_type=F32)
        for c in range(feature // channels):
            lanes = slice(c * channels, (c + 1) * channels)
            term = scale[at, c : c + 1] * dec[at, lanes].astype(F32)
            dec_buf[at, lanes] = (grad[:, lanes] + term).astype(BF16)
        copies.append(pltpu.make_async_copy(dec_buf.at[at], dec_out.at[at], sems.at[i]))
        copies[-1].start()
    upstream = lax.dot_general(
        errors, dec[...], (((1,), (1,)), ((), ())), preferred_element_type=F32
    )
    upstream = 2.0 * upstream + sparsity * weights_sum[0:1, :]
    through = jnp.where(latent[...] > 0.0, upstream, 0.0)
    enc_bias_out[...] = jnp.sum(through, axis=0, keepdims=True)
    through = through.astype(BF16)
    size = feature // parts
    for i in range(parts):
        at = slice(i * size, (i + 1) * size)
        grad = jnp.dot(inputs_t[at], through, preferred_element_type=F32)
        enc_buf[at] = grad.astype(BF16)
        copies.append(pltpu.make_async_copy(enc_buf.at[at], enc_out.at[at], sems.at[parts + i]))
        copies[-1].start()
    errors_out[...] = pieces[0][:ROWS_DEV, :feature]
    wide = [piece[...].astype(F32) for piece in pieces]
    plain = tree(wide)
    squares = tree([w[:, :feature] * w[:, :feature] for w in wide])
    plain = tree([plain[i * ROWS_DEV : (i + 1) * ROWS_DEV] for i in range(inner)])
    squares = tree([squares[i * ROWS_DEV : (i + 1) * ROWS_DEV] for i in range(inner)])
    dec_bias_out[...] = 2.0 * jnp.sum(plain[:, :feature], axis=0)
    loss = jnp.sum(squares) + sparsity * jnp.sum(plain[:, feature:])
    loss_out[0] = loss / cells
    for copy in copies:
        copy.wait()


def shards(
    waveforms,
    lengths,
    take_list,
    conv_first,
    conv_second,
    norm_gain,
    norm_shift,
    enc_weight,
    enc_bias,
    dec_weight,
    dec_bias,
):
    slots = take_list.shape[0]
    devices = lax.axis_size("utt")
    outer, inner = levels(devices)
    step = 2 * inner
    tokens = ROWS_DEV * devices
    position = lax.axis_index("utt").astype(jnp.int32).reshape(1)
    feature, latents = enc_weight.shape
    checkpoints, _, channels = conv_first.shape
    frames = (waveforms.shape[1] - 10) // 10
    wide = feature + EXTRA

    pinned = tokens <= PINNED_TOKENS
    call = functools.partial(launch, PINNED_BYTES if pinned else VMEM_BYTES)

    def fast(dims, kind):
        return pltpu.VMEM(dims, kind) if pinned else shape(dims, kind)

    def near(value):
        return pltpu.with_memory_space_constraint(value, pltpu.VMEM) if pinned else value

    def far(value):
        return pltpu.with_memory_space_constraint(value, pltpu.HBM)

    kernels = conv_first.transpose(1, 0, 2)
    encoder = near(enc_weight)
    decoder = near(dec_weight)

    packed = call(
        features_kernel,
        "features",
        fast((slots * frames, feature), BF16),
        [pl.BlockSpec(memory_space=pl.ANY)] * 7,
        vmem(),
        [
            pltpu.SMEM(lengths.shape, jnp.int32),
            pltpu.SMEM(take_list.shape, jnp.int32),
            pltpu.VMEM(waveforms.shape, F32),
            pltpu.VMEM(kernels.shape, F32),
            pltpu.VMEM(norm_gain.shape, F32),
            pltpu.VMEM(norm_shift.shape, F32),
            pltpu.VMEM(conv_second.shape, BF16),
            pltpu.SemaphoreType.DMA((6,)),
            pltpu.SemaphoreType.DMA((checkpoints,)),
        ],
        flops=2 * slots * frames * feature * 3 * channels,
        moved=2 * conv_second.size,
    )(
        *[
            far(value)
            for value in (lengths, take_list, waveforms, kernels, norm_gain, norm_shift, conv_second)
        ]
    )

    norms, weights_sum = call(
        norms_kernel,
        "norms",
        (fast((latents, LANES), F32), fast((8, latents), F32)),
        [vmem()],
        (vmem(), vmem()),
        flops=4 * dec_weight.size,
        moved=2 * dec_weight.size,
    )(decoder)

    blocks = [packed] + [exchange(packed, step * k) for k in range(1, outer)]
    pieces = blocks
    if not pinned:
        pieces = [
            call(
                join_kernel,
                "join",
                shape((outer * slots * frames, feature), BF16),
                [vmem()] * outer,
                vmem(),
                moved=4 * outer * slots * frames * feature,
            )(*blocks)
        ]
    bit = 2
    while bit < step:
        pieces = pieces + [exchange(piece, bit) for piece in pieces]
        bit *= 2
    pieces = pieces + [exchange(piece, 1) for piece in pieces]

    half = tokens // 2
    chunk = half // outer

    def encode(*refs):
        encode_kernel(len(pieces), outer, inner, slots, frames, *refs)

    own, send, shift, inputs, latent = call(
        encode,
        "encode",
        (
            fast((half, wide), F32),
            fast((half, wide), F32),
            fast((chunk, wide), F32),
            fast((tokens, feature), BF16),
            fast((tokens, latents), F32),
        ),
        [smem()] + [vmem()] * (len(pieces) + 5),
        (vmem(),) * 5,
        flops=4 * tokens * feature * latents,
        moved=4 * dec_weight.size,
    )(
        position,
        *[near(piece) for piece in pieces],
        encoder,
        enc_bias.reshape(1, latents),
        decoder,
        near(weights_sum),
        dec_bias,
    )

    inputs_t, latent_t, scale = call(
        turn_kernel,
        "turn",
        (fast((feature, tokens), BF16), fast((latents, tokens), BF16), fast((latents, LANES), F32)),
        [vmem()] * 3,
        (vmem(),) * 3,
        flops=2 * tokens * feature,
        moved=4 * tokens * feature,
    )(near(inputs), near(latent), near(norms))

    part = own + exchange(send, 1)
    small = part.astype(BF16)
    blocks = [part[:chunk]]
    for k in range(1, outer):
        blocks.append(exchange(small[k * chunk : (k + 1) * chunk], step * k))
    total = call(
        sum_kernel,
        "sum",
        fast((chunk, wide), BF16),
        [pl.BlockSpec(memory_space=pl.ANY)] + [vmem()] * outer,
        vmem(),
        moved=8 * chunk * wide,
    )(near(scale), *[near(block) for block in blocks])
    bit = 2
    while bit < step:
        width = (bit // 2) * ROWS_DEV
        other = exchange(total, bit).astype(F32).reshape(-1, 2, width, wide)
        part = total.astype(F32) + other[:, ::-1].reshape(chunk, wide)
        total = part.astype(BF16)
        bit *= 2
    errors = (part + shift).astype(BF16)
    blocks = [errors] + [exchange(errors, step * k) for k in range(1, outer)]
    blocks += [exchange(block, 1) for block in blocks]

    def gradients(*refs):
        gradients_kernel(len(blocks), inner, float(tokens * feature), *refs)

    any_space = pl.BlockSpec(memory_space=pl.ANY)
    enc_grad, dec_grad, enc_bias_grad, dec_bias_grad, mean_loss, errors_own = call(
        gradients,
        "gradients",
        (
            shape((feature, latents), BF16),
            shape((latents, feature), BF16),
            shape((1, latents), F32),
            shape((feature,), F32),
            shape((1,), F32),
            shape((ROWS_DEV, feature), BF16),
        ),
        [vmem()] * (len(blocks) + 6),
        (any_space, any_space, vmem(), vmem(), smem(), vmem()),
        [
            pltpu.VMEM((feature, latents), BF16),
            pltpu.VMEM((latents, feature), BF16),
            pltpu.SemaphoreType.DMA((8,)),
        ],
        flops=6 * tokens * feature * latents,
        moved=8 * dec_weight.size,
    )(
        *[near(block) for block in blocks],
        decoder,
        near(weights_sum),
        near(inputs_t),
        near(latent_t),
        near(latent),
        near(scale),
    )
    return (
        enc_grad,
        dec_grad,
        enc_bias_grad.reshape(latents),
        dec_bias_grad,
        mean_loss,
        errors_own,
    )


def solution(mesh):
    return jax.shard_map(
        shards,
        mesh=mesh,
        in_specs=(
            P(("groups", "utt"), None),
            P(("groups", "utt")),
            P(("groups", "utt")),
            P(),
            P(),
            P(),
            P(),
            P(None, "utt"),
            P("utt"),
            P("utt", None),
            P(),
        ),
        out_specs=(
            P("groups", "utt"),
            P(("groups", "utt"), None),
            P(("groups", "utt")),
            P("groups"),
            P("groups"),
            P(("groups", "utt"), None),
        ),
        check_vma=False,
    )
```

```python
import functools

import jax
import jax.numpy as jnp
from jax import lax
from jax.experimental import pallas as pl
from jax.experimental.pallas import tpu as pltpu
from jax.sharding import PartitionSpec as P

ROWS_DEV = 8
EXTRA = 128
LANES = 128
VMEM_BYTES = 56 << 20
PINNED_BYTES = 24 << 20
PINNED_TOKENS = 256
GROUP_ROWS = 256

sparsity = 0.5
epsilon = 1e-05

F32 = jnp.float32
BF16 = jnp.bfloat16

ERF_LIMIT = 3.7439211627767994
ERF_TOP = (
    0.00022905065861350646,
    0.0034082910107109506,
    0.050955695062380861,
    0.18520832239976145,
    1.128379143519084,
)
ERF_BOTTOM = (
    -1.1791602954361697e-7,
    0.000023547966471313185,
    0.0010179625278914885,
    0.014070470171167667,
    0.11098505178285362,
    0.49746925110067538,
    1.0,
)


def polynomial(x, terms):
    total = jnp.full_like(x, terms[0])
    for term in terms[1:]:
        total = total * x + term
    return total


def gelu(x):
    z = jnp.clip(x * 0.7071067811865476, -ERF_LIMIT, ERF_LIMIT)
    square = z * z
    erf = z * polynomial(square, ERF_TOP) / polynomial(square, ERF_BOTTOM)
    return 0.5 * x * (1.0 + erf)


def normalize(values, gain, shift):
    center = values - jnp.mean(values, axis=-1, keepdims=True)
    spread = jnp.mean(center * center, axis=-1, keepdims=True)
    return center * lax.rsqrt(spread + epsilon) * gain + shift


def levels(devices):
    chips = devices // 2
    outer = 1
    while outer * outer < chips:
        outer *= 2
    return outer, chips // outer


def exchange(value, bit):
    devices = lax.axis_size("utt")
    return lax.ppermute(value, "utt", [(i, i ^ bit) for i in range(devices)])


def tree(parts):
    while len(parts) > 1:
        parts = [parts[i] + parts[i + 1] for i in range(0, len(parts), 2)]
    return parts[0]


def iota(shape, dim):
    return lax.broadcasted_iota(jnp.int32, shape, dim)


def log2(n):
    return n.bit_length() - 1


def vmem():
    return pl.BlockSpec(memory_space=pltpu.VMEM)


def smem():
    return pl.BlockSpec(memory_space=pltpu.SMEM)


def launch(
    kernel, name, out_shape, in_specs, out_specs, scratch=(), flops=0, moved=0, limit=0, aliases=None
):
    return pl.pallas_call(
        kernel,
        name=name,
        out_shape=out_shape,
        in_specs=in_specs,
        out_specs=out_specs,
        scratch_shapes=list(scratch),
        input_output_aliases=aliases or {},
        compiler_params=pltpu.CompilerParams(vmem_limit_bytes=limit),
        cost_estimate=pl.CostEstimate(flops=flops, bytes_accessed=moved, transcendentals=0),
    )


def shape(dims, kind):
    return jax.ShapeDtypeStruct(dims, kind)


def features_kernel(*refs):
    sources, out, held, second_w, sems, more = refs[:7], refs[7], refs[8:14], refs[14], refs[15], refs[16]
    small = [pltpu.make_async_copy(sources[i], held[i], sems.at[i]) for i in range(6)]
    for copy in small:
        copy.start()
    length, take, wave, first_w, gain, shift = held
    taps_first, checkpoints, channels = first_w.shape
    slots, samples = wave.shape
    frames = out.shape[0] // slots
    copies = []
    for i in range(checkpoints * 3):
        at = (i // 3, pl.ds((i % 3) * channels, channels))
        copies.append(pltpu.make_async_copy(sources[6].at[at], second_w.at[at], more.at[i]))
        copies[-1].start()
    for copy in small:
        copy.wait()
    lane = iota((frames, samples), 1)
    start = iota((frames, samples), 0) * 10
    columns = []
    for s in range(slots):
        row = jnp.broadcast_to(wave[s : s + 1, :], (frames, samples))
        columns.append(
            [
                jnp.sum(jnp.where(lane == start + o, row, 0.0), axis=1, keepdims=True)
                for o in range(taps_first + 10)
            ]
        )
    taps = [
        jnp.concatenate(
            [columns[s][5 * tap + k] for tap in range(3) for s in range(slots)], axis=0
        )
        for k in range(taps_first)
    ]

    def layer_one(c):
        total = taps[0] * first_w[0, c : c + 1, :]
        for k in range(1, taps_first):
            total = total + taps[k] * first_w[k, c : c + 1, :]
        return gelu(normalize(total, gain[c, 0:1, :], shift[c, 0:1, :])).astype(BF16)

    rows = slots * frames

    def layer_two(c, hidden):
        total = jnp.zeros((rows, channels), F32)
        for tap in range(3):
            total = total + jnp.dot(
                hidden[tap * rows : (tap + 1) * rows],
                second_w[c, tap * channels : (tap + 1) * channels, :],
                preferred_element_type=F32,
            )
        return total

    def finish(c, total):
        total = gelu(normalize(total, gain[c, 1:2, :], shift[c, 1:2, :]))
        if c == 0:
            spot = iota((rows, channels), 1)
            line = iota((rows, channels), 0)
            for s in range(slots):
                note = jnp.where(spot == 0, length[s].astype(F32), take[s].astype(F32))
                total = jnp.where(line == (s + 1) * frames - 1, note, total)
        out[:, c * channels : (c + 1) * channels] = total.astype(BF16)

    hidden = layer_one(0)
    held_back = None
    for c in range(checkpoints):
        for tap in range(3):
            copies[3 * c + tap].wait()
        total = layer_two(c, hidden)
        if c + 1 < checkpoints:
            hidden = layer_one(c + 1)
        if held_back is not None:
            finish(c - 1, held_back)
        held_back = total
    finish(checkpoints - 1, held_back)


def join_kernel(*refs):
    out = refs[-1]
    at = 0
    for ref in refs[:-1]:
        out[at : at + ref.shape[0], :] = ref[...]
        at += ref.shape[0]


def pass_kernel(*_):
    pass


def norms_kernel(dec, norms, row):
    latents, feature = dec.shape
    channels = 512
    spot = iota((latents, LANES), 1)
    packed = jnp.zeros((latents, LANES), F32)
    total = jnp.zeros((latents, 1), F32)
    for c in range(feature // channels):
        block = dec[:, c * channels : (c + 1) * channels].astype(F32)
        norm = jnp.sqrt(jnp.sum(block * block, axis=1, keepdims=True) + 1e-06)
        total = total + norm
        packed = jnp.where(spot == c, norm, packed)
    norms[...] = packed
    row[...] = jnp.broadcast_to(total, (latents, LANES)).T[:8]


def encode_kernel(count, outer, inner, slots, frames, *refs):
    me_ref = refs[0]
    pieces = refs[1 : 1 + count]
    enc, bias, dec, weights_sum, dec_bias = refs[1 + count : 6 + count]
    own, send, shift, inputs_out, latent_out, enc_buf, sem = refs[6 + count :]
    fetch = pltpu.make_async_copy(enc, enc_buf, sem)
    fetch.start()
    me = me_ref[0]
    step = 2 * inner
    tokens, feature = inputs_out.shape
    rows = pieces[0].shape[0]
    group = max(GROUP_ROWS // rows, 1)
    width = group * rows
    held = width // frames
    shift_frames, shift_slots = log2(frames), log2(slots)

    def device_of(place):
        bits = (place & (outer - 1)) * step
        bits = bits + ((place >> log2(outer)) & (inner - 1)) * 2 + (place >> log2(outer * inner))
        return me ^ bits

    choose = (iota((held, width), 1) == iota((held, width), 0) * frames + frames - 1).astype(BF16)
    last = (iota((width, width), 0) == (iota((width, width), 1) | (frames - 1))).astype(BF16)
    ident = (iota((16, LANES), 0) == iota((16, LANES), 1)).astype(BF16)
    groups, takes, starts = [], [], []
    for g in range(0, len(pieces), group):
        parts = [piece[...] for piece in pieces[g : g + group]]
        groups.append(parts[0] if group == 1 else jnp.concatenate(parts, axis=0))
        notes = jnp.dot(choose, groups[-1][:, :LANES], preferred_element_type=F32)
        takes.append(notes[:, 1:2].astype(jnp.int32))
        slot = g * rows // frames + iota((held, 1), 0)
        starts.append(device_of(slot >> shift_slots) * ROWS_DEV)
    takes = jnp.concatenate(takes, axis=0)
    starts = jnp.concatenate(starts, axis=0)
    kinds = iota(takes.shape, 0) & (slots - 1)
    r = iota((tokens, 1), 0) >> log2(ROWS_DEV)
    holder = (
        ((r >> log2(inner)) & (outer - 1)) * step + (r & (inner - 1)) * 2 + (r >> log2(outer * inner))
    )
    token = (me ^ holder) * ROWS_DEV + (iota((tokens, 1), 0) & (ROWS_DEV - 1))
    lane = iota((1, width), 1)
    frame = lane & (frames - 1)
    total = jnp.zeros((tokens, feature), F32)
    for g, block in enumerate(groups):
        turned = lax.dot_general(
            ident, block[:, :LANES], (((1,), (1,)), ((), ())), preferred_element_type=F32
        )
        turned = jnp.dot(turned.astype(BF16), last, preferred_element_type=F32)
        size = turned[0:1, :].astype(jnp.int32)
        device = device_of((g * width + lane) >> (shift_frames + shift_slots))
        label = device * slots + ((lane >> shift_frames) & (slots - 1))
        match = takes == label
        begin = jnp.sum(jnp.where(match, starts, 0), axis=0, keepdims=True)
        second = jnp.sum(jnp.where(match, kinds, 0), axis=0, keepdims=True)
        target = begin + second * (ROWS_DEV - size) + frame
        target = jnp.where(frame < size, target, -1)
        pick = jnp.where(token == target, 1.0, 0.0).astype(BF16)
        total = total + jnp.dot(pick, block, preferred_element_type=F32)
    inputs = total.astype(BF16)
    inputs_out[...] = inputs
    fetch.wait()
    latent = jnp.maximum(jnp.dot(inputs, enc_buf[...], preferred_element_type=F32) + bias[...], 0.0)
    latent_out[...] = latent
    part = jnp.dot(latent.astype(BF16), dec[...], preferred_element_type=F32)
    weighted = latent * weights_sum[0:1, :]
    extra = weighted[:, :LANES]
    for q in range(1, weighted.shape[1] // LANES):
        extra = extra + weighted[:, q * LANES : (q + 1) * LANES]
    half = tokens // 2
    own[:, :feature] = part[:half]
    own[:, feature:] = extra[:half]
    send[:, :feature] = part[half:]
    send[:, feature:] = extra[half:]
    chunk = shift.shape[0]
    shift[:, :feature] = dec_bias[...].reshape(1, feature) - inputs[:chunk].astype(F32)
    shift[:, feature:] = jnp.zeros((chunk, EXTRA), F32)


def turn_kernel(inputs, latent, norms, dec, inputs_t, latent_t, term):
    inputs_t[...] = inputs[...].astype(F32).T.astype(BF16)
    turned = latent[...].T
    latent_t[...] = (2.0 * turned).astype(BF16)
    activity = sparsity * jnp.sum(turned, axis=1, keepdims=True)
    channels = 512
    for c in range(dec.shape[1] // channels):
        lanes = slice(c * channels, (c + 1) * channels)
        term[:, lanes] = (activity / norms[:, c : c + 1]) * dec[:, lanes].astype(F32)


def sum_kernel(*refs):
    total = refs[1][...]
    for ref in refs[2:-1]:
        total = total + ref[...].astype(F32)
    refs[-1][...] = total.astype(BF16)


def gradients_kernel(count, inner, cells, *refs):
    pieces = refs[:count]
    dec, weights_sum, inputs_t, latent_t, latent, term = refs[count : count + 6]
    enc_out, dec_out, enc_bias_out, dec_bias_out, loss_out, errors_out = refs[count + 6 : count + 12]
    enc_buf, dec_buf, sems = refs[count + 12 :]
    latents, feature = dec.shape
    errors = jnp.concatenate([piece[:, :feature] for piece in pieces], axis=0)
    copies = []
    parts = 4
    size = latents // parts
    for i in range(parts):
        at = slice(i * size, (i + 1) * size)
        grad = jnp.dot(latent_t[at], errors, preferred_element_type=F32)
        dec_buf[at] = (grad + term[at]).astype(BF16)
        copies.append(pltpu.make_async_copy(dec_buf.at[at], dec_out.at[at], sems.at[i]))
        copies[-1].start()
    upstream = lax.dot_general(
        errors, dec[...], (((1,), (1,)), ((), ())), preferred_element_type=F32
    )
    upstream = 2.0 * upstream + sparsity * weights_sum[0:1, :]
    through = jnp.where(latent[...] > 0.0, upstream, 0.0)
    enc_bias_out[...] = jnp.sum(through, axis=0, keepdims=True)
    through = through.astype(BF16)
    size = feature // parts
    for i in range(parts):
        at = slice(i * size, (i + 1) * size)
        grad = jnp.dot(inputs_t[at], through, preferred_element_type=F32)
        enc_buf[at] = grad.astype(BF16)
        copies.append(pltpu.make_async_copy(enc_buf.at[at], enc_out.at[at], sems.at[parts + i]))
        copies[-1].start()
    errors_out[...] = pieces[0][:ROWS_DEV, :feature]
    wide = [piece[...].astype(F32) for piece in pieces]
    plain = tree(wide)
    squares = tree([w[:, :feature] * w[:, :feature] for w in wide])
    plain = tree([plain[i * ROWS_DEV : (i + 1) * ROWS_DEV] for i in range(inner)])
    squares = tree([squares[i * ROWS_DEV : (i + 1) * ROWS_DEV] for i in range(inner)])
    dec_bias_out[...] = 2.0 * jnp.sum(plain[:, :feature], axis=0)
    loss = jnp.sum(squares) + sparsity * jnp.sum(plain[:, feature:])
    loss_out[0] = loss / cells
    for copy in copies:
        copy.wait()


def shards(
    waveforms,
    lengths,
    take_list,
    conv_first,
    conv_second,
    norm_gain,
    norm_shift,
    enc_weight,
    enc_bias,
    dec_weight,
    dec_bias,
):
    slots = take_list.shape[0]
    devices = lax.axis_size("utt")
    outer, inner = levels(devices)
    step = 2 * inner
    tokens = ROWS_DEV * devices
    position = lax.axis_index("utt").astype(jnp.int32).reshape(1)
    feature, latents = enc_weight.shape
    checkpoints, _, channels = conv_first.shape
    frames = (waveforms.shape[1] - 10) // 10
    wide = feature + EXTRA

    pinned = tokens <= PINNED_TOKENS
    call = functools.partial(launch, limit=PINNED_BYTES if pinned else VMEM_BYTES)

    def fast(dims, kind):
        return pltpu.VMEM(dims, kind) if pinned else shape(dims, kind)

    def near(value):
        return pltpu.with_memory_space_constraint(value, pltpu.VMEM) if pinned else value

    def far(value):
        return pltpu.with_memory_space_constraint(value, pltpu.HBM)

    kernels = conv_first.transpose(1, 0, 2)
    encoder = far(enc_weight)
    decoder = near(dec_weight)

    packed = call(
        features_kernel,
        "features",
        fast((slots * frames, feature), BF16),
        [pl.BlockSpec(memory_space=pl.ANY)] * 7,
        vmem(),
        [
            pltpu.SMEM(lengths.shape, jnp.int32),
            pltpu.SMEM(take_list.shape, jnp.int32),
            pltpu.VMEM(waveforms.shape, F32),
            pltpu.VMEM(kernels.shape, F32),
            pltpu.VMEM(norm_gain.shape, F32),
            pltpu.VMEM(norm_shift.shape, F32),
            pltpu.VMEM(conv_second.shape, BF16),
            pltpu.SemaphoreType.DMA((6,)),
            pltpu.SemaphoreType.DMA((3 * checkpoints,)),
        ],
        flops=2 * slots * frames * feature * 3 * channels,
        moved=2 * conv_second.size,
    )(
        *[
            far(value)
            for value in (lengths, take_list, waveforms, kernels, norm_gain, norm_shift, conv_second)
        ]
    )

    norms, weights_sum = call(
        norms_kernel,
        "norms",
        (fast((latents, LANES), F32), fast((8, latents), F32)),
        [vmem()],
        (vmem(), vmem()),
        flops=4 * dec_weight.size,
        moved=2 * dec_weight.size,
    )(decoder)

    blocks = [packed] + [exchange(packed, step * k) for k in range(1, outer)]
    if pinned:
        blocks[1] = call(
            pass_kernel,
            "pass",
            fast(packed.shape, BF16),
            [pl.BlockSpec(memory_space=pl.ANY)] * 2,
            pl.BlockSpec(memory_space=pl.ANY),
            aliases={1: 0},
        )(near(norms), near(blocks[1]))
    pieces = blocks
    if not pinned:
        pieces = [
            call(
                join_kernel,
                "join",
                shape((outer * slots * frames, feature), BF16),
                [vmem()] * outer,
                vmem(),
                moved=4 * outer * slots * frames * feature,
            )(*blocks)
        ]
    bit = 2
    while bit < step:
        pieces = pieces + [exchange(piece, bit) for piece in pieces]
        bit *= 2
    pieces = pieces + [exchange(piece, 1) for piece in pieces]

    half = tokens // 2
    chunk = half // outer

    def encode(*refs):
        encode_kernel(len(pieces), outer, inner, slots, frames, *refs)

    own, send, shift, inputs, latent = call(
        encode,
        "encode",
        (
            fast((half, wide), F32),
            fast((half, wide), F32),
            fast((chunk, wide), F32),
            fast((tokens, feature), BF16),
            fast((tokens, latents), F32),
        ),
        [smem()]
        + [vmem()] * len(pieces)
        + [pl.BlockSpec(memory_space=pl.ANY)]
        + [vmem()] * 4,
        (vmem(),) * 5,
        [pltpu.VMEM(enc_weight.shape, BF16), pltpu.SemaphoreType.DMA],
        limit=VMEM_BYTES,
        flops=4 * tokens * feature * latents,
        moved=4 * dec_weight.size,
    )(
        position,
        *[near(piece) for piece in pieces],
        encoder,
        enc_bias.reshape(1, latents),
        decoder,
        near(weights_sum),
        dec_bias,
    )

    inputs_t, latent_t, term = call(
        turn_kernel,
        "turn",
        (fast((feature, tokens), BF16), fast((latents, tokens), BF16), fast((latents, feature), F32)),
        [vmem()] * 4,
        (vmem(),) * 3,
        flops=2 * tokens * feature,
        moved=4 * tokens * feature,
    )(near(inputs), near(latent), near(norms), decoder)

    part = own + exchange(send, 1)
    small = part.astype(BF16)
    blocks = [part[:chunk]]
    for k in range(1, outer):
        blocks.append(exchange(small[k * chunk : (k + 1) * chunk], step * k))
    total = call(
        sum_kernel,
        "sum",
        fast((chunk, wide), BF16),
        [pl.BlockSpec(memory_space=pl.ANY)] + [vmem()] * outer,
        vmem(),
        moved=8 * chunk * wide,
    )(near(term), *[near(block) for block in blocks])
    bit = 2
    while bit < step:
        width = (bit // 2) * ROWS_DEV
        other = exchange(total, bit).astype(F32).reshape(-1, 2, width, wide)
        part = total.astype(F32) + other[:, ::-1].reshape(chunk, wide)
        total = part.astype(BF16)
        bit *= 2
    errors = (part + shift).astype(BF16)
    blocks = [errors] + [exchange(errors, step * k) for k in range(1, outer)]
    blocks += [exchange(block, 1) for block in blocks]

    def gradients(*refs):
        gradients_kernel(len(blocks), inner, float(tokens * feature), *refs)

    any_space = pl.BlockSpec(memory_space=pl.ANY)
    enc_grad, dec_grad, enc_bias_grad, dec_bias_grad, mean_loss, errors_own = call(
        gradients,
        "gradients",
        (
            shape((feature, latents), BF16),
            shape((latents, feature), BF16),
            shape((1, latents), F32),
            shape((feature,), F32),
            shape((1,), F32),
            shape((ROWS_DEV, feature), BF16),
        ),
        [vmem()] * (len(blocks) + 6),
        (any_space, any_space, vmem(), vmem(), smem(), vmem()),
        [
            pltpu.VMEM((feature, latents), BF16),
            pltpu.VMEM((latents, feature), BF16),
            pltpu.SemaphoreType.DMA((8,)),
        ],
        flops=6 * tokens * feature * latents,
        moved=8 * dec_weight.size,
    )(
        *[near(block) for block in blocks],
        decoder,
        near(weights_sum),
        near(inputs_t),
        near(latent_t),
        near(latent),
        near(term),
    )
    return (
        enc_grad,
        dec_grad,
        enc_bias_grad.reshape(latents),
        dec_bias_grad,
        mean_loss,
        errors_own,
    )


def solution(mesh):
    return jax.shard_map(
        shards,
        mesh=mesh,
        in_specs=(
            P(("groups", "utt"), None),
            P(("groups", "utt")),
            P(("groups", "utt")),
            P(),
            P(),
            P(),
            P(),
            P(None, "utt"),
            P("utt"),
            P("utt", None),
            P(),
        ),
        out_specs=(
            P("groups", "utt"),
            P(("groups", "utt"), None),
            P(("groups", "utt")),
            P("groups"),
            P("groups"),
            P(("groups", "utt"), None),
        ),
        check_vma=False,
    )
```

```python
import functools

import jax
import jax.numpy as jnp
from jax import lax
from jax.experimental import pallas as pl
from jax.experimental.pallas import tpu as pltpu
from jax.sharding import PartitionSpec as P

ROWS_DEV = 8
EXTRA = 128
LANES = 128
VMEM_BYTES = 56 << 20
PINNED_BYTES = 24 << 20
PINNED_TOKENS = 256
GROUP_ROWS = 256

sparsity = 0.5
epsilon = 1e-05

F32 = jnp.float32
BF16 = jnp.bfloat16

ERF_LIMIT = 3.7439211627767994
ERF_TOP = (
    0.00022905065861350646,
    0.0034082910107109506,
    0.050955695062380861,
    0.18520832239976145,
    1.128379143519084,
)
ERF_BOTTOM = (
    -1.1791602954361697e-7,
    0.000023547966471313185,
    0.0010179625278914885,
    0.014070470171167667,
    0.11098505178285362,
    0.49746925110067538,
    1.0,
)


def polynomial(x, terms):
    total = jnp.full_like(x, terms[0])
    for term in terms[1:]:
        total = total * x + term
    return total


def gelu(x):
    z = jnp.clip(x * 0.7071067811865476, -ERF_LIMIT, ERF_LIMIT)
    square = z * z
    erf = z * polynomial(square, ERF_TOP) / polynomial(square, ERF_BOTTOM)
    return 0.5 * x * (1.0 + erf)


def normalize(values, gain, shift):
    center = values - jnp.mean(values, axis=-1, keepdims=True)
    spread = jnp.mean(center * center, axis=-1, keepdims=True)
    return center * lax.rsqrt(spread + epsilon) * gain + shift


def levels(devices):
    chips = devices // 2
    outer = 1
    while outer * outer < chips:
        outer *= 2
    return outer, chips // outer


def exchange(value, bit):
    devices = lax.axis_size("utt")
    return lax.ppermute(value, "utt", [(i, i ^ bit) for i in range(devices)])


def tree(parts):
    while len(parts) > 1:
        parts = [parts[i] + parts[i + 1] for i in range(0, len(parts), 2)]
    return parts[0]


def iota(shape, dim):
    return lax.broadcasted_iota(jnp.int32, shape, dim)


def log2(n):
    return n.bit_length() - 1


def vmem():
    return pl.BlockSpec(memory_space=pltpu.VMEM)


def smem():
    return pl.BlockSpec(memory_space=pltpu.SMEM)


def launch(
    kernel, name, out_shape, in_specs, out_specs, scratch=(), flops=0, moved=0, limit=0, aliases=None
):
    return pl.pallas_call(
        kernel,
        name=name,
        out_shape=out_shape,
        in_specs=in_specs,
        out_specs=out_specs,
        scratch_shapes=list(scratch),
        input_output_aliases=aliases or {},
        compiler_params=pltpu.CompilerParams(vmem_limit_bytes=limit),
        cost_estimate=pl.CostEstimate(flops=flops, bytes_accessed=moved, transcendentals=0),
    )


def shape(dims, kind):
    return jax.ShapeDtypeStruct(dims, kind)


def features_kernel(*refs):
    sources, out, held, second_w, sems, more = refs[:7], refs[7], refs[8:14], refs[14], refs[15], refs[16]
    small = [pltpu.make_async_copy(sources[i], held[i], sems.at[i]) for i in range(6)]
    for copy in small:
        copy.start()
    length, take, wave, first_w, gain, shift = held
    taps_first, checkpoints, channels = first_w.shape
    slots, samples = wave.shape
    frames = out.shape[0] // slots
    copies = []
    for c in range(checkpoints):
        copies.append(pltpu.make_async_copy(sources[6].at[c], second_w.at[c], more.at[c]))
        copies[-1].start()
    for copy in small:
        copy.wait()
    lane = iota((frames, samples), 1)
    start = iota((frames, samples), 0) * 10
    columns = []
    for s in range(slots):
        row = jnp.broadcast_to(wave[s : s + 1, :], (frames, samples))
        columns.append(
            [
                jnp.sum(jnp.where(lane == start + o, row, 0.0), axis=1, keepdims=True)
                for o in range(taps_first + 10)
            ]
        )
    taps = [
        jnp.concatenate(
            [columns[s][5 * tap + k] for tap in range(3) for s in range(slots)], axis=0
        )
        for k in range(taps_first)
    ]

    def layer_one(c):
        total = taps[0] * first_w[0, c : c + 1, :]
        for k in range(1, taps_first):
            total = total + taps[k] * first_w[k, c : c + 1, :]
        return gelu(normalize(total, gain[c, 0:1, :], shift[c, 0:1, :])).astype(BF16)

    rows = slots * frames

    def layer_two(c, hidden):
        total = jnp.zeros((rows, channels), F32)
        for tap in range(3):
            total = total + jnp.dot(
                hidden[tap * rows : (tap + 1) * rows],
                second_w[c, tap * channels : (tap + 1) * channels, :],
                preferred_element_type=F32,
            )
        return total

    def finish(c, total):
        total = gelu(normalize(total, gain[c, 1:2, :], shift[c, 1:2, :]))
        if c == 0:
            spot = iota((rows, channels), 1)
            line = iota((rows, channels), 0)
            for s in range(slots):
                note = jnp.where(spot == 0, length[s].astype(F32), take[s].astype(F32))
                total = jnp.where(line == (s + 1) * frames - 1, note, total)
        out[:, c * channels : (c + 1) * channels] = total.astype(BF16)

    hidden = layer_one(0)
    held_back = None
    for c in range(checkpoints):
        copies[c].wait()
        total = layer_two(c, hidden)
        if c + 1 < checkpoints:
            hidden = layer_one(c + 1)
        if held_back is not None:
            finish(c - 1, held_back)
        held_back = total
    finish(checkpoints - 1, held_back)


def join_kernel(*refs):
    out = refs[-1]
    at = 0
    for ref in refs[:-1]:
        out[at : at + ref.shape[0], :] = ref[...]
        at += ref.shape[0]


def pass_kernel(*_):
    pass


def norms_kernel(dec, norms, row):
    latents, feature = dec.shape
    channels = 512
    spot = iota((latents, LANES), 1)
    packed = jnp.zeros((latents, LANES), F32)
    total = jnp.zeros((latents, 1), F32)
    for c in range(feature // channels):
        block = dec[:, c * channels : (c + 1) * channels].astype(F32)
        norm = jnp.sqrt(jnp.sum(block * block, axis=1, keepdims=True) + 1e-06)
        total = total + norm
        packed = jnp.where(spot == c, norm, packed)
    norms[...] = packed
    row[...] = jnp.broadcast_to(total, (latents, LANES)).T[:8]


def encode_kernel(count, outer, inner, slots, frames, *refs):
    me_ref = refs[0]
    pieces = refs[1 : 1 + count]
    enc, bias, dec_hbm, weights_sum, dec_bias = refs[1 + count : 6 + count]
    own, send, shift, inputs_out, latent_out, dec, sem = refs[6 + count :]
    fetch = pltpu.make_async_copy(dec_hbm, dec, sem)
    fetch.start()
    me = me_ref[0]
    step = 2 * inner
    tokens, feature = inputs_out.shape
    rows = pieces[0].shape[0]
    group = max(GROUP_ROWS // rows, 1)
    width = group * rows
    held = width // frames
    shift_frames, shift_slots = log2(frames), log2(slots)

    def device_of(place):
        bits = (place & (outer - 1)) * step
        bits = bits + ((place >> log2(outer)) & (inner - 1)) * 2 + (place >> log2(outer * inner))
        return me ^ bits

    choose = (iota((held, width), 1) == iota((held, width), 0) * frames + frames - 1).astype(BF16)
    last = (iota((width, width), 0) == (iota((width, width), 1) | (frames - 1))).astype(BF16)
    ident = (iota((16, LANES), 0) == iota((16, LANES), 1)).astype(BF16)
    groups, takes, starts = [], [], []
    for g in range(0, len(pieces), group):
        parts = [piece[...] for piece in pieces[g : g + group]]
        groups.append(parts[0] if group == 1 else jnp.concatenate(parts, axis=0))
        notes = jnp.dot(choose, groups[-1][:, :LANES], preferred_element_type=F32)
        takes.append(notes[:, 1:2].astype(jnp.int32))
        slot = g * rows // frames + iota((held, 1), 0)
        starts.append(device_of(slot >> shift_slots) * ROWS_DEV)
    takes = jnp.concatenate(takes, axis=0)
    starts = jnp.concatenate(starts, axis=0)
    kinds = iota(takes.shape, 0) & (slots - 1)
    r = iota((tokens, 1), 0) >> log2(ROWS_DEV)
    holder = (
        ((r >> log2(inner)) & (outer - 1)) * step + (r & (inner - 1)) * 2 + (r >> log2(outer * inner))
    )
    token = (me ^ holder) * ROWS_DEV + (iota((tokens, 1), 0) & (ROWS_DEV - 1))
    lane = iota((1, width), 1)
    frame = lane & (frames - 1)
    total = jnp.zeros((tokens, feature), F32)
    for g, block in enumerate(groups):
        turned = lax.dot_general(
            ident, block[:, :LANES], (((1,), (1,)), ((), ())), preferred_element_type=F32
        )
        turned = jnp.dot(turned.astype(BF16), last, preferred_element_type=F32)
        size = turned[0:1, :].astype(jnp.int32)
        device = device_of((g * width + lane) >> (shift_frames + shift_slots))
        label = device * slots + ((lane >> shift_frames) & (slots - 1))
        match = takes == label
        begin = jnp.sum(jnp.where(match, starts, 0), axis=0, keepdims=True)
        second = jnp.sum(jnp.where(match, kinds, 0), axis=0, keepdims=True)
        target = begin + second * (ROWS_DEV - size) + frame
        target = jnp.where(frame < size, target, -1)
        pick = jnp.where(token == target, 1.0, 0.0).astype(BF16)
        total = total + jnp.dot(pick, block, preferred_element_type=F32)
    inputs = total.astype(BF16)
    inputs_out[...] = inputs
    latent = jnp.maximum(jnp.dot(inputs, enc[...], preferred_element_type=F32) + bias[...], 0.0)
    latent_out[...] = latent
    fetch.wait()
    part = jnp.dot(latent.astype(BF16), dec[...], preferred_element_type=F32)
    weighted = latent * weights_sum[0:1, :]
    extra = weighted[:, :LANES]
    for q in range(1, weighted.shape[1] // LANES):
        extra = extra + weighted[:, q * LANES : (q + 1) * LANES]
    half = tokens // 2
    own[:, :feature] = part[:half]
    own[:, feature:] = extra[:half]
    send[:, :feature] = part[half:]
    send[:, feature:] = extra[half:]
    chunk = shift.shape[0]
    shift[:, :feature] = dec_bias[...].reshape(1, feature) - inputs[:chunk].astype(F32)
    shift[:, feature:] = jnp.zeros((chunk, EXTRA), F32)


def turn_kernel(inputs, latent, norms, inputs_t, latent_t, scale):
    inputs_t[...] = inputs[...].astype(F32).T.astype(BF16)
    turned = latent[...].T
    latent_t[...] = (2.0 * turned).astype(BF16)
    activity = jnp.sum(turned, axis=1, keepdims=True)
    scale[...] = (sparsity * activity) / jnp.maximum(norms[...], 1e-30)


def sum_kernel(*refs):
    total = refs[2][...]
    for ref in refs[3:-1]:
        total = total + ref[...].astype(F32)
    refs[-1][...] = total.astype(BF16)


def gradients_kernel(count, inner, cells, *refs):
    pieces = refs[:count]
    dec, weights_sum, inputs_t, latent_t, latent, scale = refs[count : count + 6]
    enc_out, dec_out, enc_bias_out, dec_bias_out, loss_out, errors_out = refs[count + 6 : count + 12]
    enc_buf, dec_buf, sems = refs[count + 12 :]
    latents, feature = dec.shape
    channels = 512
    errors = jnp.concatenate([piece[:, :feature] for piece in pieces], axis=0)
    copies = []
    parts = 4
    size = latents // parts
    for i in range(parts):
        at = slice(i * size, (i + 1) * size)
        grad = jnp.dot(latent_t[at], errors, preferred_element_type=F32)
        for c in range(feature // channels):
            lanes = slice(c * channels, (c + 1) * channels)
            term = scale[at, c : c + 1] * dec[at, lanes].astype(F32)
            dec_buf[at, lanes] = (grad[:, lanes] + term).astype(BF16)
        copies.append(pltpu.make_async_copy(dec_buf.at[at], dec_out.at[at], sems.at[i]))
        copies[-1].start()
    upstream = lax.dot_general(
        errors, dec[...], (((1,), (1,)), ((), ())), preferred_element_type=F32
    )
    upstream = 2.0 * upstream + sparsity * weights_sum[0:1, :]
    through = jnp.where(latent[...] > 0.0, upstream, 0.0)
    enc_bias_out[...] = jnp.sum(through, axis=0, keepdims=True)
    through = through.astype(BF16)
    size = feature // parts
    for i in range(parts):
        at = slice(i * size, (i + 1) * size)
        grad = jnp.dot(inputs_t[at], through, preferred_element_type=F32)
        enc_buf[at] = grad.astype(BF16)
        copies.append(pltpu.make_async_copy(enc_buf.at[at], enc_out.at[at], sems.at[parts + i]))
        copies[-1].start()
    errors_out[...] = pieces[0][:ROWS_DEV, :feature]
    wide = [piece[...].astype(F32) for piece in pieces]
    plain = tree(wide)
    squares = tree([w[:, :feature] * w[:, :feature] for w in wide])
    plain = tree([plain[i * ROWS_DEV : (i + 1) * ROWS_DEV] for i in range(inner)])
    squares = tree([squares[i * ROWS_DEV : (i + 1) * ROWS_DEV] for i in range(inner)])
    dec_bias_out[...] = 2.0 * jnp.sum(plain[:, :feature], axis=0)
    loss = jnp.sum(squares) + sparsity * jnp.sum(plain[:, feature:])
    loss_out[0] = loss / cells
    for copy in copies:
        copy.wait()


def shards(
    waveforms,
    lengths,
    take_list,
    conv_first,
    conv_second,
    norm_gain,
    norm_shift,
    enc_weight,
    enc_bias,
    dec_weight,
    dec_bias,
):
    slots = take_list.shape[0]
    devices = lax.axis_size("utt")
    outer, inner = levels(devices)
    step = 2 * inner
    tokens = ROWS_DEV * devices
    position = lax.axis_index("utt").astype(jnp.int32).reshape(1)
    feature, latents = enc_weight.shape
    checkpoints, _, channels = conv_first.shape
    frames = (waveforms.shape[1] - 10) // 10
    wide = feature + EXTRA

    pinned = tokens <= PINNED_TOKENS
    call = functools.partial(launch, limit=PINNED_BYTES if pinned else VMEM_BYTES)

    def fast(dims, kind):
        return pltpu.VMEM(dims, kind) if pinned else shape(dims, kind)

    def near(value):
        return pltpu.with_memory_space_constraint(value, pltpu.VMEM) if pinned else value

    def far(value):
        return pltpu.with_memory_space_constraint(value, pltpu.HBM)

    kernels = conv_first.transpose(1, 0, 2)
    encoder = near(enc_weight)
    decoder = near(dec_weight)

    packed = call(
        features_kernel,
        "features",
        fast((slots * frames, feature), BF16),
        [pl.BlockSpec(memory_space=pl.ANY)] * 7,
        vmem(),
        [
            pltpu.SMEM(lengths.shape, jnp.int32),
            pltpu.SMEM(take_list.shape, jnp.int32),
            pltpu.VMEM(waveforms.shape, F32),
            pltpu.VMEM(kernels.shape, F32),
            pltpu.VMEM(norm_gain.shape, F32),
            pltpu.VMEM(norm_shift.shape, F32),
            pltpu.VMEM(conv_second.shape, BF16),
            pltpu.SemaphoreType.DMA((6,)),
            pltpu.SemaphoreType.DMA((checkpoints,)),
        ],
        flops=2 * slots * frames * feature * 3 * channels,
        moved=2 * conv_second.size,
    )(
        *[
            far(value)
            for value in (lengths, take_list, waveforms, kernels, norm_gain, norm_shift, conv_second)
        ]
    )

    norms, weights_sum = call(
        norms_kernel,
        "norms",
        (fast((latents, LANES), F32), fast((8, latents), F32)),
        [vmem()],
        (vmem(), vmem()),
        flops=4 * dec_weight.size,
        moved=2 * dec_weight.size,
    )(far(dec_weight))

    blocks = [packed] + [exchange(packed, step * k) for k in range(1, outer)]
    if pinned:
        blocks[1] = call(
            pass_kernel,
            "pass",
            fast(packed.shape, BF16),
            [pl.BlockSpec(memory_space=pl.ANY)] * 3,
            pl.BlockSpec(memory_space=pl.ANY),
            aliases={2: 0},
        )(near(norms), encoder, near(blocks[1]))
    pieces = blocks
    if not pinned:
        pieces = [
            call(
                join_kernel,
                "join",
                shape((outer * slots * frames, feature), BF16),
                [vmem()] * outer,
                vmem(),
                moved=4 * outer * slots * frames * feature,
            )(*blocks)
        ]
    bit = 2
    while bit < step:
        pieces = pieces + [exchange(piece, bit) for piece in pieces]
        bit *= 2
    pieces = pieces + [exchange(piece, 1) for piece in pieces]

    half = tokens // 2
    chunk = half // outer

    def encode(*refs):
        encode_kernel(len(pieces), outer, inner, slots, frames, *refs)

    own, send, shift, inputs, latent = call(
        encode,
        "encode",
        (
            fast((half, wide), F32),
            fast((half, wide), F32),
            fast((chunk, wide), F32),
            fast((tokens, feature), BF16),
            fast((tokens, latents), F32),
        ),
        [smem()] + [vmem()] * (len(pieces) + 2) + [pl.BlockSpec(memory_space=pl.ANY)] + [vmem()] * 2,
        (vmem(),) * 5,
        [pltpu.VMEM(dec_weight.shape, BF16), pltpu.SemaphoreType.DMA],
        flops=4 * tokens * feature * latents,
        moved=4 * dec_weight.size,
    )(
        position,
        *[near(piece) for piece in pieces],
        encoder,
        enc_bias.reshape(1, latents),
        far(dec_weight),
        near(weights_sum),
        dec_bias,
    )

    inputs_t, latent_t, scale = call(
        turn_kernel,
        "turn",
        (fast((feature, tokens), BF16), fast((latents, tokens), BF16), fast((latents, LANES), F32)),
        [vmem()] * 3,
        (vmem(),) * 3,
        flops=2 * tokens * feature,
        moved=4 * tokens * feature,
    )(near(inputs), near(latent), near(norms))

    part = own + exchange(send, 1)
    small = part.astype(BF16)
    blocks = [part[:chunk]]
    for k in range(1, outer):
        blocks.append(exchange(small[k * chunk : (k + 1) * chunk], step * k))
    total = call(
        sum_kernel,
        "sum",
        fast((chunk, wide), BF16),
        [pl.BlockSpec(memory_space=pl.ANY)] * 2 + [vmem()] * outer,
        vmem(),
        moved=8 * chunk * wide,
    )(near(scale), decoder, *[near(block) for block in blocks])
    bit = 2
    while bit < step:
        width = (bit // 2) * ROWS_DEV
        other = exchange(total, bit).astype(F32).reshape(-1, 2, width, wide)
        part = total.astype(F32) + other[:, ::-1].reshape(chunk, wide)
        total = part.astype(BF16)
        bit *= 2
    errors = (part + shift).astype(BF16)
    blocks = [errors] + [exchange(errors, step * k) for k in range(1, outer)]
    blocks += [exchange(block, 1) for block in blocks]

    def gradients(*refs):
        gradients_kernel(len(blocks), inner, float(tokens * feature), *refs)

    any_space = pl.BlockSpec(memory_space=pl.ANY)
    enc_grad, dec_grad, enc_bias_grad, dec_bias_grad, mean_loss, errors_own = call(
        gradients,
        "gradients",
        (
            shape((feature, latents), BF16),
            shape((latents, feature), BF16),
            shape((1, latents), F32),
            shape((feature,), F32),
            shape((1,), F32),
            shape((ROWS_DEV, feature), BF16),
        ),
        [vmem()] * (len(blocks) + 6),
        (any_space, any_space, vmem(), vmem(), smem(), vmem()),
        [
            pltpu.VMEM((feature, latents), BF16),
            pltpu.VMEM((latents, feature), BF16),
            pltpu.SemaphoreType.DMA((8,)),
        ],
        flops=6 * tokens * feature * latents,
        moved=8 * dec_weight.size,
    )(
        *[near(block) for block in blocks],
        decoder,
        near(weights_sum),
        near(inputs_t),
        near(latent_t),
        near(latent),
        near(scale),
    )
    return (
        enc_grad,
        dec_grad,
        enc_bias_grad.reshape(latents),
        dec_bias_grad,
        mean_loss,
        errors_own,
    )


def solution(mesh):
    return jax.shard_map(
        shards,
        mesh=mesh,
        in_specs=(
            P(("groups", "utt"), None),
            P(("groups", "utt")),
            P(("groups", "utt")),
            P(),
            P(),
            P(),
            P(),
            P(None, "utt"),
            P("utt"),
            P("utt", None),
            P(),
        ),
        out_specs=(
            P("groups", "utt"),
            P(("groups", "utt"), None),
            P(("groups", "utt")),
            P("groups"),
            P("groups"),
            P(("groups", "utt"), None),
        ),
        check_vma=False,
    )
```

```python
import functools

import jax
import jax.numpy as jnp
from jax import lax
from jax.experimental import pallas as pl
from jax.experimental.pallas import tpu as pltpu
from jax.sharding import PartitionSpec as P

ROWS_DEV = 8
EXTRA = 128
LANES = 128
VMEM_BYTES = 56 << 20
PINNED_BYTES = 24 << 20
PINNED_TOKENS = 256
GROUP_ROWS = 256
DEC_PARTS = 2

sparsity = 0.5
epsilon = 1e-05

F32 = jnp.float32
BF16 = jnp.bfloat16

ERF_LIMIT = 3.7439211627767994
ERF_TOP = (
    0.00022905065861350646,
    0.0034082910107109506,
    0.050955695062380861,
    0.18520832239976145,
    1.128379143519084,
)
ERF_BOTTOM = (
    -1.1791602954361697e-7,
    0.000023547966471313185,
    0.0010179625278914885,
    0.014070470171167667,
    0.11098505178285362,
    0.49746925110067538,
    1.0,
)


def polynomial(x, terms):
    total = jnp.full_like(x, terms[0])
    for term in terms[1:]:
        total = total * x + term
    return total


def gelu(x):
    z = jnp.clip(x * 0.7071067811865476, -ERF_LIMIT, ERF_LIMIT)
    square = z * z
    erf = z * polynomial(square, ERF_TOP) / polynomial(square, ERF_BOTTOM)
    return 0.5 * x * (1.0 + erf)


def normalize(values, gain, shift):
    center = values - jnp.mean(values, axis=-1, keepdims=True)
    spread = jnp.mean(center * center, axis=-1, keepdims=True)
    return center * lax.rsqrt(spread + epsilon) * gain + shift


def levels(devices):
    chips = devices // 2
    outer = 1
    while outer * outer < chips:
        outer *= 2
    return outer, chips // outer


def exchange(value, bit):
    devices = lax.axis_size("utt")
    return lax.ppermute(value, "utt", [(i, i ^ bit) for i in range(devices)])


def tree(parts):
    while len(parts) > 1:
        parts = [parts[i] + parts[i + 1] for i in range(0, len(parts), 2)]
    return parts[0]


def iota(shape, dim):
    return lax.broadcasted_iota(jnp.int32, shape, dim)


def log2(n):
    return n.bit_length() - 1


def vmem():
    return pl.BlockSpec(memory_space=pltpu.VMEM)


def smem():
    return pl.BlockSpec(memory_space=pltpu.SMEM)


def launch(
    kernel, name, out_shape, in_specs, out_specs, scratch=(), flops=0, moved=0, limit=0
):
    return pl.pallas_call(
        kernel,
        name=name,
        out_shape=out_shape,
        in_specs=in_specs,
        out_specs=out_specs,
        scratch_shapes=list(scratch),
        compiler_params=pltpu.CompilerParams(vmem_limit_bytes=limit),
        cost_estimate=pl.CostEstimate(flops=flops, bytes_accessed=moved, transcendentals=0),
    )


def shape(dims, kind):
    return jax.ShapeDtypeStruct(dims, kind)


def features_kernel(*refs):
    sources, out, held, second_w, sems, more = refs[:7], refs[7], refs[8:14], refs[14], refs[15], refs[16]
    small = [pltpu.make_async_copy(sources[i], held[i], sems.at[i]) for i in range(6)]
    for copy in small:
        copy.start()
    length, take, wave, first_w, gain, shift = held
    taps_first, checkpoints, channels = first_w.shape
    slots, samples = wave.shape
    frames = out.shape[0] // slots
    copies = []
    for c in range(checkpoints):
        copies.append(pltpu.make_async_copy(sources[6].at[c], second_w.at[c], more.at[c]))
        copies[-1].start()
    for copy in small:
        copy.wait()
    lane = iota((frames, samples), 1)
    start = iota((frames, samples), 0) * 10
    columns = []
    for s in range(slots):
        row = jnp.broadcast_to(wave[s : s + 1, :], (frames, samples))
        columns.append(
            [
                jnp.sum(jnp.where(lane == start + o, row, 0.0), axis=1, keepdims=True)
                for o in range(taps_first + 10)
            ]
        )
    taps = [
        jnp.concatenate(
            [columns[s][5 * tap + k] for tap in range(3) for s in range(slots)], axis=0
        )
        for k in range(taps_first)
    ]

    def layer_one(c):
        total = taps[0] * first_w[0, c : c + 1, :]
        for k in range(1, taps_first):
            total = total + taps[k] * first_w[k, c : c + 1, :]
        return gelu(normalize(total, gain[c, 0:1, :], shift[c, 0:1, :])).astype(BF16)

    rows = slots * frames

    def layer_two(c, hidden):
        total = jnp.zeros((rows, channels), F32)
        for tap in range(3):
            total = total + jnp.dot(
                hidden[tap * rows : (tap + 1) * rows],
                second_w[c, tap * channels : (tap + 1) * channels, :],
                preferred_element_type=F32,
            )
        return total

    def finish(c, total):
        total = gelu(normalize(total, gain[c, 1:2, :], shift[c, 1:2, :]))
        if c == 0:
            spot = iota((rows, channels), 1)
            line = iota((rows, channels), 0)
            for s in range(slots):
                note = jnp.where(spot == 0, length[s].astype(F32), take[s].astype(F32))
                total = jnp.where(line == (s + 1) * frames - 1, note, total)
        out[:, c * channels : (c + 1) * channels] = total.astype(BF16)

    hidden = layer_one(0)
    held_back = None
    for c in range(checkpoints):
        copies[c].wait()
        total = layer_two(c, hidden)
        if c + 1 < checkpoints:
            hidden = layer_one(c + 1)
        if held_back is not None:
            finish(c - 1, held_back)
        held_back = total
    finish(checkpoints - 1, held_back)


def join_kernel(*refs):
    out = refs[-1]
    at = 0
    for ref in refs[2:-1]:
        out[at : at + ref.shape[0], :] = ref[...]
        at += ref.shape[0]


def norms_kernel(dec, norms, row):
    latents, feature = dec.shape
    channels = 512
    spot = iota((latents, LANES), 1)
    packed = jnp.zeros((latents, LANES), F32)
    total = jnp.zeros((latents, 1), F32)
    for c in range(feature // channels):
        block = dec[:, c * channels : (c + 1) * channels].astype(F32)
        norm = jnp.sqrt(jnp.sum(block * block, axis=1, keepdims=True) + 1e-06)
        total = total + norm
        packed = jnp.where(spot == c, norm, packed)
    norms[...] = packed
    row[...] = jnp.broadcast_to(total, (latents, LANES)).T[:8]


def encode_kernel(count, outer, inner, slots, frames, *refs):
    me_ref = refs[0]
    pieces = refs[1 : 1 + count]
    enc, bias, dec_hbm, weights_sum, dec_bias = refs[1 + count : 6 + count]
    own, send, shift, inputs_out, latent_out, dec, sems = refs[6 + count :]
    quarter = dec.shape[0] // DEC_PARTS
    fetches = []
    for i in range(DEC_PARTS):
        at = pl.ds(i * quarter, quarter)
        fetches.append(pltpu.make_async_copy(dec_hbm.at[at], dec.at[at], sems.at[i]))
        fetches[-1].start()
    me = me_ref[0]
    step = 2 * inner
    tokens, feature = inputs_out.shape
    rows = pieces[0].shape[0]
    group = max(GROUP_ROWS // rows, 1)
    width = group * rows
    held = width // frames
    shift_frames, shift_slots = log2(frames), log2(slots)

    def device_of(place):
        bits = (place & (outer - 1)) * step
        bits = bits + ((place >> log2(outer)) & (inner - 1)) * 2 + (place >> log2(outer * inner))
        return me ^ bits

    choose = (iota((held, width), 1) == iota((held, width), 0) * frames + frames - 1).astype(BF16)
    last = (iota((width, width), 0) == (iota((width, width), 1) | (frames - 1))).astype(BF16)
    ident = (iota((16, LANES), 0) == iota((16, LANES), 1)).astype(BF16)
    groups, takes, starts = [], [], []
    for g in range(0, len(pieces), group):
        parts = [piece[...] for piece in pieces[g : g + group]]
        groups.append(parts[0] if group == 1 else jnp.concatenate(parts, axis=0))
        notes = jnp.dot(choose, groups[-1][:, :LANES], preferred_element_type=F32)
        takes.append(notes[:, 1:2].astype(jnp.int32))
        slot = g * rows // frames + iota((held, 1), 0)
        starts.append(device_of(slot >> shift_slots) * ROWS_DEV)
    takes = jnp.concatenate(takes, axis=0)
    starts = jnp.concatenate(starts, axis=0)
    kinds = iota(takes.shape, 0) & (slots - 1)
    r = iota((tokens, 1), 0) >> log2(ROWS_DEV)
    holder = (
        ((r >> log2(inner)) & (outer - 1)) * step + (r & (inner - 1)) * 2 + (r >> log2(outer * inner))
    )
    token = (me ^ holder) * ROWS_DEV + (iota((tokens, 1), 0) & (ROWS_DEV - 1))
    lane = iota((1, width), 1)
    frame = lane & (frames - 1)
    total = jnp.zeros((tokens, feature), F32)
    for g, block in enumerate(groups):
        turned = lax.dot_general(
            ident, block[:, :LANES], (((1,), (1,)), ((), ())), preferred_element_type=F32
        )
        turned = jnp.dot(turned.astype(BF16), last, preferred_element_type=F32)
        size = turned[0:1, :].astype(jnp.int32)
        device = device_of((g * width + lane) >> (shift_frames + shift_slots))
        label = device * slots + ((lane >> shift_frames) & (slots - 1))
        match = takes == label
        begin = jnp.sum(jnp.where(match, starts, 0), axis=0, keepdims=True)
        second = jnp.sum(jnp.where(match, kinds, 0), axis=0, keepdims=True)
        target = begin + second * (ROWS_DEV - size) + frame
        target = jnp.where(frame < size, target, -1)
        pick = jnp.where(token == target, 1.0, 0.0).astype(BF16)
        total = total + jnp.dot(pick, block, preferred_element_type=F32)
    inputs = total.astype(BF16)
    inputs_out[...] = inputs
    latent = jnp.maximum(jnp.dot(inputs, enc[...], preferred_element_type=F32) + bias[...], 0.0)
    latent_out[...] = latent
    rounded = latent.astype(BF16)
    part = jnp.zeros((tokens, feature), F32)
    for i in range(DEC_PARTS):
        fetches[i].wait()
        at = slice(i * quarter, (i + 1) * quarter)
        part = part + jnp.dot(rounded[:, at], dec[at], preferred_element_type=F32)
    weighted = latent * weights_sum[0:1, :]
    extra = weighted[:, :LANES]
    for q in range(1, weighted.shape[1] // LANES):
        extra = extra + weighted[:, q * LANES : (q + 1) * LANES]
    half = tokens // 2
    own[:, :feature] = part[:half]
    own[:, feature:] = extra[:half]
    send[:, :feature] = part[half:].astype(BF16)
    send[:, feature:] = extra[half:].astype(BF16)
    chunk = shift.shape[0]
    shift[:, :feature] = dec_bias[...].reshape(1, feature) - inputs[:chunk].astype(F32)
    shift[:, feature:] = jnp.zeros((chunk, EXTRA), F32)


def turn_kernel(inputs, latent, norms, inputs_t, latent_t, scale):
    inputs_t[...] = inputs[...].astype(F32).T.astype(BF16)
    turned = latent[...].T
    latent_t[...] = (2.0 * turned).astype(BF16)
    activity = jnp.sum(turned, axis=1, keepdims=True)
    scale[...] = (sparsity * activity) / jnp.maximum(norms[...], 1e-30)


def sum_kernel(*refs):
    total = refs[2][...]
    for ref in refs[3:-1]:
        total = total + ref[...].astype(F32)
    refs[-1][...] = total.astype(BF16)


def gradients_kernel(count, inner, cells, *refs):
    pieces = refs[:count]
    dec, weights_sum, inputs_t, latent_t, latent, scale = refs[count : count + 6]
    enc_out, dec_out, enc_bias_out, dec_bias_out, loss_out, errors_out = refs[count + 6 : count + 12]
    enc_buf, dec_buf, sems = refs[count + 12 :]
    latents, feature = dec.shape
    channels = 512
    errors = jnp.concatenate([piece[:, :feature] for piece in pieces], axis=0)
    copies = []
    parts = 4
    size = latents // parts
    for i in range(parts):
        at = slice(i * size, (i + 1) * size)
        grad = jnp.dot(latent_t[at], errors, preferred_element_type=F32)
        for c in range(feature // channels):
            lanes = slice(c * channels, (c + 1) * channels)
            term = scale[at, c : c + 1] * dec[at, lanes].astype(F32)
            dec_buf[at, lanes] = (grad[:, lanes] + term).astype(BF16)
        copies.append(pltpu.make_async_copy(dec_buf.at[at], dec_out.at[at], sems.at[i]))
        copies[-1].start()
    upstream = lax.dot_general(
        errors, dec[...], (((1,), (1,)), ((), ())), preferred_element_type=F32
    )
    upstream = 2.0 * upstream + sparsity * weights_sum[0:1, :]
    through = jnp.where(latent[...] > 0.0, upstream, 0.0)
    enc_bias_out[...] = jnp.sum(through, axis=0, keepdims=True)
    through = through.astype(BF16)
    size = feature // parts
    for i in range(parts):
        at = slice(i * size, (i + 1) * size)
        grad = jnp.dot(inputs_t[at], through, preferred_element_type=F32)
        enc_buf[at] = grad.astype(BF16)
        copies.append(pltpu.make_async_copy(enc_buf.at[at], enc_out.at[at], sems.at[parts + i]))
        copies[-1].start()
    errors_out[...] = pieces[0][:ROWS_DEV, :feature]
    wide = [piece[...].astype(F32) for piece in pieces]
    plain = tree(wide)
    squares = tree([w[:, :feature] * w[:, :feature] for w in wide])
    plain = tree([plain[i * ROWS_DEV : (i + 1) * ROWS_DEV] for i in range(inner)])
    squares = tree([squares[i * ROWS_DEV : (i + 1) * ROWS_DEV] for i in range(inner)])
    dec_bias_out[...] = 2.0 * jnp.sum(plain[:, :feature], axis=0)
    loss = jnp.sum(squares) + sparsity * jnp.sum(plain[:, feature:])
    loss_out[0] = loss / cells
    for copy in copies:
        copy.wait()


def shards(
    waveforms,
    lengths,
    take_list,
    conv_first,
    conv_second,
    norm_gain,
    norm_shift,
    enc_weight,
    enc_bias,
    dec_weight,
    dec_bias,
):
    slots = take_list.shape[0]
    devices = lax.axis_size("utt")
    outer, inner = levels(devices)
    step = 2 * inner
    tokens = ROWS_DEV * devices
    position = lax.axis_index("utt").astype(jnp.int32).reshape(1)
    feature, latents = enc_weight.shape
    checkpoints, _, channels = conv_first.shape
    frames = (waveforms.shape[1] - 10) // 10
    wide = feature + EXTRA

    pinned = tokens <= PINNED_TOKENS
    call = functools.partial(launch, limit=PINNED_BYTES if pinned else VMEM_BYTES)

    def fast(dims, kind):
        return pltpu.VMEM(dims, kind) if pinned else shape(dims, kind)

    def near(value):
        return pltpu.with_memory_space_constraint(value, pltpu.VMEM) if pinned else value

    def far(value):
        return pltpu.with_memory_space_constraint(value, pltpu.HBM)

    kernels = conv_first.transpose(1, 0, 2)
    encoder = near(enc_weight)
    decoder = near(dec_weight)

    packed = call(
        features_kernel,
        "features",
        fast((slots * frames, feature), BF16),
        [pl.BlockSpec(memory_space=pl.ANY)] * 7,
        vmem(),
        [
            pltpu.SMEM(lengths.shape, jnp.int32),
            pltpu.SMEM(take_list.shape, jnp.int32),
            pltpu.VMEM(waveforms.shape, F32),
            pltpu.VMEM(kernels.shape, F32),
            pltpu.VMEM(norm_gain.shape, F32),
            pltpu.VMEM(norm_shift.shape, F32),
            pltpu.VMEM(conv_second.shape, BF16),
            pltpu.SemaphoreType.DMA((6,)),
            pltpu.SemaphoreType.DMA((checkpoints,)),
        ],
        flops=2 * slots * frames * feature * 3 * channels,
        moved=2 * conv_second.size,
    )(
        *[
            far(value)
            for value in (lengths, take_list, waveforms, kernels, norm_gain, norm_shift, conv_second)
        ]
    )

    norms, weights_sum = call(
        norms_kernel,
        "norms",
        (fast((latents, LANES), F32), fast((8, latents), F32)),
        [vmem()],
        (vmem(), vmem()),
        flops=4 * dec_weight.size,
        moved=2 * dec_weight.size,
    )(decoder)

    blocks = [packed] + [exchange(packed, step * k) for k in range(1, outer)]
    pieces = [
        call(
            join_kernel,
            "join",
            fast((outer * slots * frames, feature), BF16),
            [pl.BlockSpec(memory_space=pl.ANY)] * 2 + [vmem()] * outer,
            vmem(),
            moved=4 * outer * slots * frames * feature,
        )(near(norms), encoder, *[near(block) for block in blocks])
    ]
    bit = 2
    while bit < step:
        pieces = pieces + [exchange(piece, bit) for piece in pieces]
        bit *= 2
    pieces = pieces + [exchange(piece, 1) for piece in pieces]

    half = tokens // 2
    chunk = half // outer

    def encode(*refs):
        encode_kernel(len(pieces), outer, inner, slots, frames, *refs)

    own, send, shift, inputs, latent = call(
        encode,
        "encode",
        (
            fast((half, wide), F32),
            fast((half, wide), BF16),
            fast((chunk, wide), F32),
            fast((tokens, feature), BF16),
            fast((tokens, latents), F32),
        ),
        [smem()] + [vmem()] * (len(pieces) + 2) + [pl.BlockSpec(memory_space=pl.ANY)] + [vmem()] * 2,
        (vmem(),) * 5,
        [pltpu.VMEM(dec_weight.shape, BF16), pltpu.SemaphoreType.DMA((DEC_PARTS,))],
        flops=4 * tokens * feature * latents,
        moved=4 * dec_weight.size,
    )(
        position,
        *[near(piece) for piece in pieces],
        encoder,
        enc_bias.reshape(1, latents),
        far(dec_weight),
        near(weights_sum),
        dec_bias,
    )

    inputs_t, latent_t, scale = call(
        turn_kernel,
        "turn",
        (fast((feature, tokens), BF16), fast((latents, tokens), BF16), fast((latents, LANES), F32)),
        [vmem()] * 3,
        (vmem(),) * 3,
        flops=2 * tokens * feature,
        moved=4 * tokens * feature,
    )(near(inputs), near(latent), near(norms))

    part = own + exchange(send, 1).astype(F32)
    small = part.astype(BF16)
    blocks = [part[:chunk]]
    for k in range(1, outer):
        blocks.append(exchange(small[k * chunk : (k + 1) * chunk], step * k))
    total = call(
        sum_kernel,
        "sum",
        fast((chunk, wide), BF16),
        [pl.BlockSpec(memory_space=pl.ANY)] * 2 + [vmem()] * outer,
        vmem(),
        moved=8 * chunk * wide,
    )(near(scale), decoder, *[near(block) for block in blocks])
    bit = 2
    while bit < step:
        width = (bit // 2) * ROWS_DEV
        other = exchange(total, bit).astype(F32).reshape(-1, 2, width, wide)
        part = total.astype(F32) + other[:, ::-1].reshape(chunk, wide)
        total = part.astype(BF16)
        bit *= 2
    errors = (part + shift).astype(BF16)
    blocks = [errors] + [exchange(errors, step * k) for k in range(1, outer)]
    blocks += [exchange(block, 1) for block in blocks]

    def gradients(*refs):
        gradients_kernel(len(blocks), inner, float(tokens * feature), *refs)

    any_space = pl.BlockSpec(memory_space=pl.ANY)
    enc_grad, dec_grad, enc_bias_grad, dec_bias_grad, mean_loss, errors_own = call(
        gradients,
        "gradients",
        (
            shape((feature, latents), BF16),
            shape((latents, feature), BF16),
            shape((1, latents), F32),
            shape((feature,), F32),
            shape((1,), F32),
            shape((ROWS_DEV, feature), BF16),
        ),
        [vmem()] * (len(blocks) + 6),
        (any_space, any_space, vmem(), vmem(), smem(), vmem()),
        [
            pltpu.VMEM((feature, latents), BF16),
            pltpu.VMEM((latents, feature), BF16),
            pltpu.SemaphoreType.DMA((8,)),
        ],
        flops=6 * tokens * feature * latents,
        moved=8 * dec_weight.size,
    )(
        *[near(block) for block in blocks],
        decoder,
        near(weights_sum),
        near(inputs_t),
        near(latent_t),
        near(latent),
        near(scale),
    )
    return (
        enc_grad,
        dec_grad,
        enc_bias_grad.reshape(latents),
        dec_bias_grad,
        mean_loss,
        errors_own,
    )


def solution(mesh):
    return jax.shard_map(
        shards,
        mesh=mesh,
        in_specs=(
            P(("groups", "utt"), None),
            P(("groups", "utt")),
            P(("groups", "utt")),
            P(),
            P(),
            P(),
            P(),
            P(None, "utt"),
            P("utt"),
            P("utt", None),
            P(),
        ),
        out_specs=(
            P("groups", "utt"),
            P(("groups", "utt"), None),
            P(("groups", "utt")),
            P("groups"),
            P("groups"),
            P(("groups", "utt"), None),
        ),
        check_vma=False,
    )
```

```python
import functools

import jax
import jax.numpy as jnp
from jax import lax
from jax.experimental import pallas as pl
from jax.experimental.pallas import tpu as pltpu
from jax.sharding import PartitionSpec as P

ROWS_DEV = 8
EXTRA = 128
LANES = 128
VMEM_BYTES = 56 << 20
PINNED_BYTES = 24 << 20
PINNED_TOKENS = 256
GROUP_ROWS = 256
DEC_PARTS = 3

sparsity = 0.5
epsilon = 1e-05

F32 = jnp.float32
BF16 = jnp.bfloat16

ERF_LIMIT = 3.7439211627767994
ERF_TOP = (
    0.00022905065861350646,
    0.0034082910107109506,
    0.050955695062380861,
    0.18520832239976145,
    1.128379143519084,
)
ERF_BOTTOM = (
    -1.1791602954361697e-7,
    0.000023547966471313185,
    0.0010179625278914885,
    0.014070470171167667,
    0.11098505178285362,
    0.49746925110067538,
    1.0,
)


def polynomial(x, terms):
    total = jnp.full_like(x, terms[0])
    for term in terms[1:]:
        total = total * x + term
    return total


def gelu(x):
    z = jnp.clip(x * 0.7071067811865476, -ERF_LIMIT, ERF_LIMIT)
    square = z * z
    erf = z * polynomial(square, ERF_TOP) / polynomial(square, ERF_BOTTOM)
    return 0.5 * x * (1.0 + erf)


def normalize(values, gain, shift):
    center = values - jnp.mean(values, axis=-1, keepdims=True)
    spread = jnp.mean(center * center, axis=-1, keepdims=True)
    return center * lax.rsqrt(spread + epsilon) * gain + shift


def levels(devices):
    chips = devices // 2
    outer = 1
    while outer * outer < chips:
        outer *= 2
    return outer, chips // outer


def exchange(value, bit):
    devices = lax.axis_size("utt")
    return lax.ppermute(value, "utt", [(i, i ^ bit) for i in range(devices)])


def tree(parts):
    while len(parts) > 1:
        parts = [parts[i] + parts[i + 1] for i in range(0, len(parts), 2)]
    return parts[0]


def iota(shape, dim):
    return lax.broadcasted_iota(jnp.int32, shape, dim)


def log2(n):
    return n.bit_length() - 1


def vmem():
    return pl.BlockSpec(memory_space=pltpu.VMEM)


def smem():
    return pl.BlockSpec(memory_space=pltpu.SMEM)


def launch(
    kernel, name, out_shape, in_specs, out_specs, scratch=(), flops=0, moved=0, limit=0
):
    return pl.pallas_call(
        kernel,
        name=name,
        out_shape=out_shape,
        in_specs=in_specs,
        out_specs=out_specs,
        scratch_shapes=list(scratch),
        compiler_params=pltpu.CompilerParams(vmem_limit_bytes=limit),
        cost_estimate=pl.CostEstimate(flops=flops, bytes_accessed=moved, transcendentals=0),
    )


def shape(dims, kind):
    return jax.ShapeDtypeStruct(dims, kind)


def features_kernel(*refs):
    sources, out, held, second_w, sems, more = refs[:7], refs[7], refs[8:14], refs[14], refs[15], refs[16]
    small = [pltpu.make_async_copy(sources[i], held[i], sems.at[i]) for i in range(6)]
    for copy in small:
        copy.start()
    length, take, wave, first_w, gain, shift = held
    taps_first, checkpoints, channels = first_w.shape
    slots, samples = wave.shape
    frames = out.shape[0] // slots
    copies = []
    for c in range(checkpoints):
        copies.append(pltpu.make_async_copy(sources[6].at[c], second_w.at[c], more.at[c]))
        copies[-1].start()
    for copy in small:
        copy.wait()
    lane = iota((frames, samples), 1)
    start = iota((frames, samples), 0) * 10
    columns = []
    for s in range(slots):
        row = jnp.broadcast_to(wave[s : s + 1, :], (frames, samples))
        columns.append(
            [
                jnp.sum(jnp.where(lane == start + o, row, 0.0), axis=1, keepdims=True)
                for o in range(taps_first + 10)
            ]
        )
    taps = [
        jnp.concatenate(
            [columns[s][5 * tap + k] for tap in range(3) for s in range(slots)], axis=0
        )
        for k in range(taps_first)
    ]

    def layer_one(c):
        total = taps[0] * first_w[0, c : c + 1, :]
        for k in range(1, taps_first):
            total = total + taps[k] * first_w[k, c : c + 1, :]
        return gelu(normalize(total, gain[c, 0:1, :], shift[c, 0:1, :])).astype(BF16)

    rows = slots * frames

    def layer_two(c, hidden):
        total = jnp.zeros((rows, channels), F32)
        for tap in range(3):
            total = total + jnp.dot(
                hidden[tap * rows : (tap + 1) * rows],
                second_w[c, tap * channels : (tap + 1) * channels, :],
                preferred_element_type=F32,
            )
        return total

    def finish(c, total):
        total = gelu(normalize(total, gain[c, 1:2, :], shift[c, 1:2, :]))
        if c == 0:
            spot = iota((rows, channels), 1)
            line = iota((rows, channels), 0)
            for s in range(slots):
                note = jnp.where(spot == 0, length[s].astype(F32), take[s].astype(F32))
                total = jnp.where(line == (s + 1) * frames - 1, note, total)
        out[:, c * channels : (c + 1) * channels] = total.astype(BF16)

    hidden = layer_one(0)
    held_back = None
    for c in range(checkpoints):
        copies[c].wait()
        total = layer_two(c, hidden)
        if c + 1 < checkpoints:
            hidden = layer_one(c + 1)
        if held_back is not None:
            finish(c - 1, held_back)
        held_back = total
    finish(checkpoints - 1, held_back)


def join_kernel(*refs):
    out = refs[-1]
    at = 0
    for ref in refs[2:-1]:
        out[at : at + ref.shape[0], :] = ref[...]
        at += ref.shape[0]


def norms_kernel(dec, norms, row):
    latents, feature = dec.shape
    channels = 512
    spot = iota((latents, LANES), 1)
    packed = jnp.zeros((latents, LANES), F32)
    total = jnp.zeros((latents, 1), F32)
    for c in range(feature // channels):
        block = dec[:, c * channels : (c + 1) * channels].astype(F32)
        norm = jnp.sqrt(jnp.sum(block * block, axis=1, keepdims=True) + 1e-06)
        total = total + norm
        packed = jnp.where(spot == c, norm, packed)
    norms[...] = packed
    row[...] = jnp.broadcast_to(total, (latents, LANES)).T[:8]


def encode_kernel(count, outer, inner, slots, frames, *refs):
    me_ref = refs[0]
    pieces = refs[1 : 1 + count]
    enc, bias, dec_hbm, weights_sum = refs[1 + count : 5 + count]
    send, inputs_out, latent_out, dec, sems = refs[5 + count :]
    part_width = dec.shape[1] // DEC_PARTS
    fetches = []
    for i in range(DEC_PARTS):
        at = (slice(None), pl.ds(i * part_width, part_width))
        fetches.append(pltpu.make_async_copy(dec_hbm.at[at], dec.at[at], sems.at[i]))
        fetches[-1].start()
    me = me_ref[0]
    step = 2 * inner
    tokens, feature = inputs_out.shape
    rows = pieces[0].shape[0]
    group = max(GROUP_ROWS // rows, 1)
    width = group * rows
    held = width // frames
    shift_frames, shift_slots = log2(frames), log2(slots)

    def device_of(place):
        bits = (place & (outer - 1)) * step
        bits = bits + ((place >> log2(outer)) & (inner - 1)) * 2 + (place >> log2(outer * inner))
        return me ^ bits

    choose = (iota((held, width), 1) == iota((held, width), 0) * frames + frames - 1).astype(BF16)
    last = (iota((width, width), 0) == (iota((width, width), 1) | (frames - 1))).astype(BF16)
    ident = (iota((16, LANES), 0) == iota((16, LANES), 1)).astype(BF16)
    groups, takes, starts = [], [], []
    for g in range(0, len(pieces), group):
        parts = [piece[...] for piece in pieces[g : g + group]]
        groups.append(parts[0] if group == 1 else jnp.concatenate(parts, axis=0))
        notes = jnp.dot(choose, groups[-1][:, :LANES], preferred_element_type=F32)
        takes.append(notes[:, 1:2].astype(jnp.int32))
        slot = g * rows // frames + iota((held, 1), 0)
        starts.append(device_of(slot >> shift_slots) * ROWS_DEV)
    takes = jnp.concatenate(takes, axis=0)
    starts = jnp.concatenate(starts, axis=0)
    kinds = iota(takes.shape, 0) & (slots - 1)
    r = iota((tokens, 1), 0) >> log2(ROWS_DEV)
    holder = (
        ((r >> log2(inner)) & (outer - 1)) * step + (r & (inner - 1)) * 2 + (r >> log2(outer * inner))
    )
    token = (me ^ holder) * ROWS_DEV + (iota((tokens, 1), 0) & (ROWS_DEV - 1))
    lane = iota((1, width), 1)
    frame = lane & (frames - 1)
    total = jnp.zeros((tokens, feature), F32)
    for g, block in enumerate(groups):
        turned = lax.dot_general(
            ident, block[:, :LANES], (((1,), (1,)), ((), ())), preferred_element_type=F32
        )
        turned = jnp.dot(turned.astype(BF16), last, preferred_element_type=F32)
        size = turned[0:1, :].astype(jnp.int32)
        device = device_of((g * width + lane) >> (shift_frames + shift_slots))
        label = device * slots + ((lane >> shift_frames) & (slots - 1))
        match = takes == label
        begin = jnp.sum(jnp.where(match, starts, 0), axis=0, keepdims=True)
        second = jnp.sum(jnp.where(match, kinds, 0), axis=0, keepdims=True)
        target = begin + second * (ROWS_DEV - size) + frame
        target = jnp.where(frame < size, target, -1)
        pick = jnp.where(token == target, 1.0, 0.0).astype(BF16)
        total = total + jnp.dot(pick, block, preferred_element_type=F32)
    inputs = total.astype(BF16)
    inputs_out[...] = inputs
    latent = jnp.maximum(jnp.dot(inputs, enc[...], preferred_element_type=F32) + bias[...], 0.0)
    latent_out[...] = latent
    half = tokens // 2
    rounded = latent[half:].astype(BF16)
    for i in range(DEC_PARTS):
        fetches[i].wait()
        at = slice(i * part_width, (i + 1) * part_width)
        part = jnp.dot(rounded, dec[:, at], preferred_element_type=F32)
        send[:, at] = part.astype(BF16)
    send[:, feature:] = lane_sums(latent[half:] * weights_sum[0:1, :]).astype(BF16)


def lane_sums(weighted):
    extra = weighted[:, :LANES]
    for q in range(1, weighted.shape[1] // LANES):
        extra = extra + weighted[:, q * LANES : (q + 1) * LANES]
    return extra


def own_kernel(inputs, latent, dec, weights_sum, dec_bias, own, shift):
    half, chunk = own.shape[0], shift.shape[0]
    feature = dec.shape[1]
    kept = latent[:half]
    own[:, :feature] = jnp.dot(kept.astype(BF16), dec[...], preferred_element_type=F32)
    own[:, feature:] = lane_sums(kept * weights_sum[0:1, :])
    shift[:, :feature] = dec_bias[...].reshape(1, feature) - inputs[:chunk].astype(F32)
    shift[:, feature:] = jnp.zeros((chunk, EXTRA), F32)


def turn_kernel(inputs, latent, norms, inputs_t, latent_t, scale):
    inputs_t[...] = inputs[...].astype(F32).T.astype(BF16)
    turned = latent[...].T
    latent_t[...] = (2.0 * turned).astype(BF16)
    activity = jnp.sum(turned, axis=1, keepdims=True)
    scale[...] = (sparsity * activity) / jnp.maximum(norms[...], 1e-30)


def sum_kernel(*refs):
    total = refs[1][...]
    for ref in refs[2:-1]:
        total = total + ref[...].astype(F32)
    refs[-1][...] = total.astype(BF16)


def gradients_kernel(count, inner, cells, *refs):
    pieces = refs[:count]
    dec, weights_sum, inputs_t, latent_t, latent, scale = refs[count : count + 6]
    enc_out, dec_out, enc_bias_out, dec_bias_out, loss_out, errors_out = refs[count + 6 : count + 12]
    enc_buf, dec_buf, sems = refs[count + 12 :]
    latents, feature = dec.shape
    channels = 512
    errors = jnp.concatenate([piece[:, :feature] for piece in pieces], axis=0)
    copies = []
    parts = 4
    size = latents // parts
    for i in range(parts):
        at = slice(i * size, (i + 1) * size)
        grad = jnp.dot(latent_t[at], errors, preferred_element_type=F32)
        for c in range(feature // channels):
            lanes = slice(c * channels, (c + 1) * channels)
            term = scale[at, c : c + 1] * dec[at, lanes].astype(F32)
            dec_buf[at, lanes] = (grad[:, lanes] + term).astype(BF16)
        copies.append(pltpu.make_async_copy(dec_buf.at[at], dec_out.at[at], sems.at[i]))
        copies[-1].start()
    upstream = lax.dot_general(
        errors, dec[...], (((1,), (1,)), ((), ())), preferred_element_type=F32
    )
    upstream = 2.0 * upstream + sparsity * weights_sum[0:1, :]
    through = jnp.where(latent[...] > 0.0, upstream, 0.0)
    enc_bias_out[...] = jnp.sum(through, axis=0, keepdims=True)
    through = through.astype(BF16)
    size = feature // parts
    for i in range(parts):
        at = slice(i * size, (i + 1) * size)
        grad = jnp.dot(inputs_t[at], through, preferred_element_type=F32)
        enc_buf[at] = grad.astype(BF16)
        copies.append(pltpu.make_async_copy(enc_buf.at[at], enc_out.at[at], sems.at[parts + i]))
        copies[-1].start()
    errors_out[...] = pieces[0][:ROWS_DEV, :feature]
    wide = [piece[...].astype(F32) for piece in pieces]
    plain = tree(wide)
    squares = tree([w[:, :feature] * w[:, :feature] for w in wide])
    plain = tree([plain[i * ROWS_DEV : (i + 1) * ROWS_DEV] for i in range(inner)])
    squares = tree([squares[i * ROWS_DEV : (i + 1) * ROWS_DEV] for i in range(inner)])
    dec_bias_out[...] = 2.0 * jnp.sum(plain[:, :feature], axis=0)
    loss = jnp.sum(squares) + sparsity * jnp.sum(plain[:, feature:])
    loss_out[0] = loss / cells
    for copy in copies:
        copy.wait()


def shards(
    waveforms,
    lengths,
    take_list,
    conv_first,
    conv_second,
    norm_gain,
    norm_shift,
    enc_weight,
    enc_bias,
    dec_weight,
    dec_bias,
):
    slots = take_list.shape[0]
    devices = lax.axis_size("utt")
    outer, inner = levels(devices)
    step = 2 * inner
    tokens = ROWS_DEV * devices
    position = lax.axis_index("utt").astype(jnp.int32).reshape(1)
    feature, latents = enc_weight.shape
    checkpoints, _, channels = conv_first.shape
    frames = (waveforms.shape[1] - 10) // 10
    wide = feature + EXTRA

    pinned = tokens <= PINNED_TOKENS
    call = functools.partial(launch, limit=PINNED_BYTES if pinned else VMEM_BYTES)

    def fast(dims, kind):
        return pltpu.VMEM(dims, kind) if pinned else shape(dims, kind)

    def near(value):
        return pltpu.with_memory_space_constraint(value, pltpu.VMEM) if pinned else value

    def far(value):
        return pltpu.with_memory_space_constraint(value, pltpu.HBM)

    kernels = conv_first.transpose(1, 0, 2)
    encoder = near(enc_weight)
    decoder = near(dec_weight)

    packed = call(
        features_kernel,
        "features",
        fast((slots * frames, feature), BF16),
        [pl.BlockSpec(memory_space=pl.ANY)] * 7,
        vmem(),
        [
            pltpu.SMEM(lengths.shape, jnp.int32),
            pltpu.SMEM(take_list.shape, jnp.int32),
            pltpu.VMEM(waveforms.shape, F32),
            pltpu.VMEM(kernels.shape, F32),
            pltpu.VMEM(norm_gain.shape, F32),
            pltpu.VMEM(norm_shift.shape, F32),
            pltpu.VMEM(conv_second.shape, BF16),
            pltpu.SemaphoreType.DMA((6,)),
            pltpu.SemaphoreType.DMA((checkpoints,)),
        ],
        flops=2 * slots * frames * feature * 3 * channels,
        moved=2 * conv_second.size,
    )(
        *[
            far(value)
            for value in (lengths, take_list, waveforms, kernels, norm_gain, norm_shift, conv_second)
        ]
    )

    norms, weights_sum = call(
        norms_kernel,
        "norms",
        (fast((latents, LANES), F32), fast((8, latents), F32)),
        [vmem()],
        (vmem(), vmem()),
        flops=4 * dec_weight.size,
        moved=2 * dec_weight.size,
    )(decoder)

    blocks = [packed] + [exchange(packed, step * k) for k in range(1, outer)]
    pieces = [
        call(
            join_kernel,
            "join",
            fast((outer * slots * frames, feature), BF16),
            [pl.BlockSpec(memory_space=pl.ANY)] * 2 + [vmem()] * outer,
            vmem(),
            moved=4 * outer * slots * frames * feature,
        )(near(norms), encoder, *[near(block) for block in blocks])
    ]
    bit = 2
    while bit < step:
        pieces = pieces + [exchange(piece, bit) for piece in pieces]
        bit *= 2
    pieces = pieces + [exchange(piece, 1) for piece in pieces]

    half = tokens // 2
    chunk = half // outer

    def encode(*refs):
        encode_kernel(len(pieces), outer, inner, slots, frames, *refs)

    send, inputs, latent, decoder = call(
        encode,
        "encode",
        (
            fast((half, wide), BF16),
            fast((tokens, feature), BF16),
            fast((tokens, latents), F32),
            fast(dec_weight.shape, BF16),
        ),
        [smem()] + [vmem()] * (len(pieces) + 2) + [pl.BlockSpec(memory_space=pl.ANY), vmem()],
        (vmem(),) * 4,
        [pltpu.SemaphoreType.DMA((DEC_PARTS,))],
        flops=3 * tokens * feature * latents,
        moved=4 * dec_weight.size,
    )(
        position,
        *[near(piece) for piece in pieces],
        encoder,
        enc_bias.reshape(1, latents),
        far(dec_weight),
        near(weights_sum),
    )
    received = exchange(send, 1)
    decoder = near(decoder)
    own, shift = call(
        own_kernel,
        "own",
        (fast((half, wide), F32), fast((chunk, wide), F32)),
        [vmem()] * 5,
        (vmem(),) * 2,
        flops=tokens * feature * latents,
        moved=2 * dec_weight.size,
    )(near(inputs), near(latent), decoder, near(weights_sum), dec_bias)

    inputs_t, latent_t, scale = call(
        turn_kernel,
        "turn",
        (fast((feature, tokens), BF16), fast((latents, tokens), BF16), fast((latents, LANES), F32)),
        [vmem()] * 3,
        (vmem(),) * 3,
        flops=2 * tokens * feature,
        moved=4 * tokens * feature,
    )(near(inputs), near(latent), near(norms))

    part = own + received.astype(F32)
    small = part.astype(BF16)
    blocks = [part[:chunk]]
    for k in range(1, outer):
        blocks.append(exchange(small[k * chunk : (k + 1) * chunk], step * k))
    total = call(
        sum_kernel,
        "sum",
        fast((chunk, wide), BF16),
        [pl.BlockSpec(memory_space=pl.ANY)] + [vmem()] * outer,
        vmem(),
        moved=8 * chunk * wide,
    )(near(scale), *[near(block) for block in blocks])
    bit = 2
    while bit < step:
        width = (bit // 2) * ROWS_DEV
        other = exchange(total, bit).astype(F32).reshape(-1, 2, width, wide)
        part = total.astype(F32) + other[:, ::-1].reshape(chunk, wide)
        total = part.astype(BF16)
        bit *= 2
    errors = (part + shift).astype(BF16)
    blocks = [errors] + [exchange(errors, step * k) for k in range(1, outer)]
    blocks += [exchange(block, 1) for block in blocks]

    def gradients(*refs):
        gradients_kernel(len(blocks), inner, float(tokens * feature), *refs)

    any_space = pl.BlockSpec(memory_space=pl.ANY)
    enc_grad, dec_grad, enc_bias_grad, dec_bias_grad, mean_loss, errors_own = call(
        gradients,
        "gradients",
        (
            shape((feature, latents), BF16),
            shape((latents, feature), BF16),
            shape((1, latents), F32),
            shape((feature,), F32),
            shape((1,), F32),
            shape((ROWS_DEV, feature), BF16),
        ),
        [vmem()] * (len(blocks) + 6),
        (any_space, any_space, vmem(), vmem(), smem(), vmem()),
        [
            pltpu.VMEM((feature, latents), BF16),
            pltpu.VMEM((latents, feature), BF16),
            pltpu.SemaphoreType.DMA((8,)),
        ],
        flops=6 * tokens * feature * latents,
        moved=8 * dec_weight.size,
    )(
        *[near(block) for block in blocks],
        decoder,
        near(weights_sum),
        near(inputs_t),
        near(latent_t),
        near(latent),
        near(scale),
    )
    return (
        enc_grad,
        dec_grad,
        enc_bias_grad.reshape(latents),
        dec_bias_grad,
        mean_loss,
        errors_own,
    )


def solution(mesh):
    return jax.shard_map(
        shards,
        mesh=mesh,
        in_specs=(
            P(("groups", "utt"), None),
            P(("groups", "utt")),
            P(("groups", "utt")),
            P(),
            P(),
            P(),
            P(),
            P(None, "utt"),
            P("utt"),
            P("utt", None),
            P(),
        ),
        out_specs=(
            P("groups", "utt"),
            P(("groups", "utt"), None),
            P(("groups", "utt")),
            P("groups"),
            P("groups"),
            P(("groups", "utt"), None),
        ),
        check_vma=False,
    )
```

```python
import functools

import jax
import jax.numpy as jnp
from jax import lax
from jax.experimental import pallas as pl
from jax.experimental.pallas import tpu as pltpu
from jax.sharding import PartitionSpec as P

ROWS_DEV = 8
EXTRA = 128
LANES = 128
VMEM_BYTES = 56 << 20
PINNED_BYTES = 24 << 20
PINNED_TOKENS = 256
GROUP_ROWS = 256

sparsity = 0.5
epsilon = 1e-05

F32 = jnp.float32
BF16 = jnp.bfloat16

ERF_LIMIT = 3.7439211627767994
ERF_TOP = (
    0.00022905065861350646,
    0.0034082910107109506,
    0.050955695062380861,
    0.18520832239976145,
    1.128379143519084,
)
ERF_BOTTOM = (
    -1.1791602954361697e-7,
    0.000023547966471313185,
    0.0010179625278914885,
    0.014070470171167667,
    0.11098505178285362,
    0.49746925110067538,
    1.0,
)


def polynomial(x, terms):
    total = jnp.full_like(x, terms[0])
    for term in terms[1:]:
        total = total * x + term
    return total


def gelu(x):
    z = jnp.clip(x * 0.7071067811865476, -ERF_LIMIT, ERF_LIMIT)
    square = z * z
    erf = z * polynomial(square, ERF_TOP) / polynomial(square, ERF_BOTTOM)
    return 0.5 * x * (1.0 + erf)


def normalize(values, gain, shift):
    center = values - jnp.mean(values, axis=-1, keepdims=True)
    spread = jnp.mean(center * center, axis=-1, keepdims=True)
    return center * lax.rsqrt(spread + epsilon) * gain + shift


def levels(devices):
    chips = devices // 2
    outer = 1
    while outer * outer < chips:
        outer *= 2
    return outer, chips // outer


def exchange(value, bit):
    devices = lax.axis_size("utt")
    return lax.ppermute(value, "utt", [(i, i ^ bit) for i in range(devices)])


def tree(parts):
    while len(parts) > 1:
        parts = [parts[i] + parts[i + 1] for i in range(0, len(parts), 2)]
    return parts[0]


def iota(shape, dim):
    return lax.broadcasted_iota(jnp.int32, shape, dim)


def log2(n):
    return n.bit_length() - 1


def vmem():
    return pl.BlockSpec(memory_space=pltpu.VMEM)


def smem():
    return pl.BlockSpec(memory_space=pltpu.SMEM)


def launch(
    kernel, name, out_shape, in_specs, out_specs, scratch=(), flops=0, moved=0, limit=0
):
    return pl.pallas_call(
        kernel,
        name=name,
        out_shape=out_shape,
        in_specs=in_specs,
        out_specs=out_specs,
        scratch_shapes=list(scratch),
        compiler_params=pltpu.CompilerParams(vmem_limit_bytes=limit),
        cost_estimate=pl.CostEstimate(flops=flops, bytes_accessed=moved, transcendentals=0),
    )


def shape(dims, kind):
    return jax.ShapeDtypeStruct(dims, kind)


def features_kernel(*refs):
    sources, out, held, second_w, sems, more = refs[:7], refs[7], refs[8:14], refs[14], refs[15], refs[16]
    small = [pltpu.make_async_copy(sources[i], held[i], sems.at[i]) for i in range(6)]
    for copy in small:
        copy.start()
    length, take, wave, first_w, gain, shift = held
    taps_first, checkpoints, channels = first_w.shape
    slots, samples = wave.shape
    frames = out.shape[0] // slots
    copies = []
    for c in range(checkpoints):
        copies.append(pltpu.make_async_copy(sources[6].at[c], second_w.at[c], more.at[c]))
        copies[-1].start()
    for copy in small:
        copy.wait()
    lane = iota((frames, samples), 1)
    start = iota((frames, samples), 0) * 10
    columns = []
    for s in range(slots):
        row = jnp.broadcast_to(wave[s : s + 1, :], (frames, samples))
        columns.append(
            [
                jnp.sum(jnp.where(lane == start + o, row, 0.0), axis=1, keepdims=True)
                for o in range(taps_first + 10)
            ]
        )
    taps = [
        jnp.concatenate(
            [columns[s][5 * tap + k] for tap in range(3) for s in range(slots)], axis=0
        )
        for k in range(taps_first)
    ]

    def layer_one(c):
        total = taps[0] * first_w[0, c : c + 1, :]
        for k in range(1, taps_first):
            total = total + taps[k] * first_w[k, c : c + 1, :]
        return gelu(normalize(total, gain[c, 0:1, :], shift[c, 0:1, :])).astype(BF16)

    rows = slots * frames

    def layer_two(c, hidden):
        total = jnp.zeros((rows, channels), F32)
        for tap in range(3):
            total = total + jnp.dot(
                hidden[tap * rows : (tap + 1) * rows],
                second_w[c, tap * channels : (tap + 1) * channels, :],
                preferred_element_type=F32,
            )
        return total

    def finish(c, total):
        total = gelu(normalize(total, gain[c, 1:2, :], shift[c, 1:2, :]))
        if c == 0:
            spot = iota((rows, channels), 1)
            line = iota((rows, channels), 0)
            for s in range(slots):
                note = jnp.where(spot == 0, length[s].astype(F32), take[s].astype(F32))
                total = jnp.where(line == (s + 1) * frames - 1, note, total)
        out[:, c * channels : (c + 1) * channels] = total.astype(BF16)

    hidden = layer_one(0)
    held_back = None
    for c in range(checkpoints):
        copies[c].wait()
        total = layer_two(c, hidden)
        if c + 1 < checkpoints:
            hidden = layer_one(c + 1)
        if held_back is not None:
            finish(c - 1, held_back)
        held_back = total
    finish(checkpoints - 1, held_back)


def join_kernel(*refs):
    out = refs[-1]
    at = 0
    for ref in refs[2:-1]:
        out[at : at + ref.shape[0], :] = ref[...]
        at += ref.shape[0]


def column_norms(dec):
    channels = 512
    columns = []
    for c in range(dec.shape[1] // channels):
        block = dec[:, c * channels : (c + 1) * channels].astype(F32)
        columns.append(jnp.sqrt(jnp.sum(block * block, axis=1, keepdims=True) + 1e-06))
    return columns


def norms_kernel(dec, row):
    total = sum(column_norms(dec))
    row[...] = jnp.broadcast_to(total, (total.shape[0], LANES)).T[:8]


def encode_kernel(count, outer, inner, slots, frames, *refs):
    me_ref = refs[0]
    pieces = refs[1 : 1 + count]
    enc, enc_hbm, bias, dec, weights_sum = refs[1 + count : 6 + count]
    send, inputs_out, latent_out, enc_late, sem = refs[6 + count :]
    early = enc.shape[0]
    fetch = pltpu.make_async_copy(enc_hbm.at[pl.ds(early, enc_late.shape[0])], enc_late, sem)
    fetch.start()
    me = me_ref[0]
    step = 2 * inner
    tokens, feature = inputs_out.shape
    rows = pieces[0].shape[0]
    group = max(GROUP_ROWS // rows, 1)
    width = group * rows
    held = width // frames
    shift_frames, shift_slots = log2(frames), log2(slots)

    def device_of(place):
        bits = (place & (outer - 1)) * step
        bits = bits + ((place >> log2(outer)) & (inner - 1)) * 2 + (place >> log2(outer * inner))
        return me ^ bits

    choose = (iota((held, width), 1) == iota((held, width), 0) * frames + frames - 1).astype(BF16)
    last = (iota((width, width), 0) == (iota((width, width), 1) | (frames - 1))).astype(BF16)
    ident = (iota((16, LANES), 0) == iota((16, LANES), 1)).astype(BF16)
    groups, takes, starts = [], [], []
    for g in range(0, len(pieces), group):
        parts = [piece[...] for piece in pieces[g : g + group]]
        groups.append(parts[0] if group == 1 else jnp.concatenate(parts, axis=0))
        notes = jnp.dot(choose, groups[-1][:, :LANES], preferred_element_type=F32)
        takes.append(notes[:, 1:2].astype(jnp.int32))
        slot = g * rows // frames + iota((held, 1), 0)
        starts.append(device_of(slot >> shift_slots) * ROWS_DEV)
    takes = jnp.concatenate(takes, axis=0)
    starts = jnp.concatenate(starts, axis=0)
    kinds = iota(takes.shape, 0) & (slots - 1)
    r = iota((tokens, 1), 0) >> log2(ROWS_DEV)
    holder = (
        ((r >> log2(inner)) & (outer - 1)) * step + (r & (inner - 1)) * 2 + (r >> log2(outer * inner))
    )
    token = (me ^ holder) * ROWS_DEV + (iota((tokens, 1), 0) & (ROWS_DEV - 1))
    lane = iota((1, width), 1)
    frame = lane & (frames - 1)
    total = jnp.zeros((tokens, feature), F32)
    for g, block in enumerate(groups):
        turned = lax.dot_general(
            ident, block[:, :LANES], (((1,), (1,)), ((), ())), preferred_element_type=F32
        )
        turned = jnp.dot(turned.astype(BF16), last, preferred_element_type=F32)
        size = turned[0:1, :].astype(jnp.int32)
        device = device_of((g * width + lane) >> (shift_frames + shift_slots))
        label = device * slots + ((lane >> shift_frames) & (slots - 1))
        match = takes == label
        begin = jnp.sum(jnp.where(match, starts, 0), axis=0, keepdims=True)
        second = jnp.sum(jnp.where(match, kinds, 0), axis=0, keepdims=True)
        target = begin + second * (ROWS_DEV - size) + frame
        target = jnp.where(frame < size, target, -1)
        pick = jnp.where(token == target, 1.0, 0.0).astype(BF16)
        total = total + jnp.dot(pick, block, preferred_element_type=F32)
    inputs = total.astype(BF16)
    inputs_out[...] = inputs
    preact = jnp.dot(inputs[:, :early], enc[...], preferred_element_type=F32)
    fetch.wait()
    preact = preact + jnp.dot(inputs[:, early:], enc_late[...], preferred_element_type=F32)
    latent = jnp.maximum(preact + bias[...], 0.0)
    latent_out[...] = latent
    half = tokens // 2
    rounded = latent[half:].astype(BF16)
    send[:, :feature] = jnp.dot(rounded, dec[...], preferred_element_type=F32).astype(BF16)
    send[:, feature:] = lane_sums(latent[half:] * weights_sum[0:1, :]).astype(BF16)


def lane_sums(weighted):
    extra = weighted[:, :LANES]
    for q in range(1, weighted.shape[1] // LANES):
        extra = extra + weighted[:, q * LANES : (q + 1) * LANES]
    return extra


def own_kernel(inputs, latent, dec, weights_sum, dec_bias, own, shift):
    half, chunk = own.shape[0], shift.shape[0]
    feature = dec.shape[1]
    kept = latent[:half]
    own[:, :feature] = jnp.dot(kept.astype(BF16), dec[...], preferred_element_type=F32)
    own[:, feature:] = lane_sums(kept * weights_sum[0:1, :])
    shift[:, :feature] = dec_bias[...].reshape(1, feature) - inputs[:chunk].astype(F32)
    shift[:, feature:] = jnp.zeros((chunk, EXTRA), F32)


def turn_kernel(inputs, latent, dec, inputs_t, latent_t, scale):
    inputs_t[...] = inputs[...].astype(F32).T.astype(BF16)
    turned = latent[...].T
    latent_t[...] = (2.0 * turned).astype(BF16)
    activity = jnp.sum(turned, axis=1, keepdims=True)
    spot = iota(scale.shape, 1)
    packed = jnp.zeros(scale.shape, F32)
    for c, norm in enumerate(column_norms(dec)):
        packed = jnp.where(spot == c, (sparsity * activity) / norm, packed)
    scale[...] = packed


def sum_kernel(*refs):
    total = refs[1][...]
    for ref in refs[2:-1]:
        total = total + ref[...].astype(F32)
    refs[-1][...] = total.astype(BF16)


def gradients_kernel(count, inner, cells, *refs):
    pieces = refs[:count]
    dec, weights_sum, inputs_t, latent_t, latent, scale = refs[count : count + 6]
    enc_out, dec_out, enc_bias_out, dec_bias_out, loss_out, errors_out = refs[count + 6 : count + 12]
    enc_buf, dec_buf, sems = refs[count + 12 :]
    latents, feature = dec.shape
    channels = 512
    errors = jnp.concatenate([piece[:, :feature] for piece in pieces], axis=0)
    copies = []
    parts = 4
    size = latents // parts
    for i in range(parts):
        at = slice(i * size, (i + 1) * size)
        grad = jnp.dot(latent_t[at], errors, preferred_element_type=F32)
        for c in range(feature // channels):
            lanes = slice(c * channels, (c + 1) * channels)
            term = scale[at, c : c + 1] * dec[at, lanes].astype(F32)
            dec_buf[at, lanes] = (grad[:, lanes] + term).astype(BF16)
        copies.append(pltpu.make_async_copy(dec_buf.at[at], dec_out.at[at], sems.at[i]))
        copies[-1].start()
    upstream = lax.dot_general(
        errors, dec[...], (((1,), (1,)), ((), ())), preferred_element_type=F32
    )
    upstream = 2.0 * upstream + sparsity * weights_sum[0:1, :]
    through = jnp.where(latent[...] > 0.0, upstream, 0.0)
    enc_bias_out[...] = jnp.sum(through, axis=0, keepdims=True)
    through = through.astype(BF16)
    size = feature // parts
    for i in range(parts):
        at = slice(i * size, (i + 1) * size)
        grad = jnp.dot(inputs_t[at], through, preferred_element_type=F32)
        enc_buf[at] = grad.astype(BF16)
        copies.append(pltpu.make_async_copy(enc_buf.at[at], enc_out.at[at], sems.at[parts + i]))
        copies[-1].start()
    errors_out[...] = pieces[0][:ROWS_DEV, :feature]
    wide = [piece[...].astype(F32) for piece in pieces]
    plain = tree(wide)
    squares = tree([w[:, :feature] * w[:, :feature] for w in wide])
    plain = tree([plain[i * ROWS_DEV : (i + 1) * ROWS_DEV] for i in range(inner)])
    squares = tree([squares[i * ROWS_DEV : (i + 1) * ROWS_DEV] for i in range(inner)])
    dec_bias_out[...] = 2.0 * jnp.sum(plain[:, :feature], axis=0)
    loss = jnp.sum(squares) + sparsity * jnp.sum(plain[:, feature:])
    loss_out[0] = loss / cells
    for copy in copies:
        copy.wait()


def shards(
    waveforms,
    lengths,
    take_list,
    conv_first,
    conv_second,
    norm_gain,
    norm_shift,
    enc_weight,
    enc_bias,
    dec_weight,
    dec_bias,
):
    slots = take_list.shape[0]
    devices = lax.axis_size("utt")
    outer, inner = levels(devices)
    step = 2 * inner
    tokens = ROWS_DEV * devices
    position = lax.axis_index("utt").astype(jnp.int32).reshape(1)
    feature, latents = enc_weight.shape
    checkpoints, _, channels = conv_first.shape
    frames = (waveforms.shape[1] - 10) // 10
    wide = feature + EXTRA

    pinned = tokens <= PINNED_TOKENS
    call = functools.partial(launch, limit=PINNED_BYTES if pinned else VMEM_BYTES)

    def fast(dims, kind):
        return pltpu.VMEM(dims, kind) if pinned else shape(dims, kind)

    def near(value):
        return pltpu.with_memory_space_constraint(value, pltpu.VMEM) if pinned else value

    def far(value):
        return pltpu.with_memory_space_constraint(value, pltpu.HBM)

    kernels = conv_first.transpose(1, 0, 2)
    early = 2 * feature // 3
    encoder = near(enc_weight[:early])
    decoder = near(dec_weight)

    packed = call(
        features_kernel,
        "features",
        fast((slots * frames, feature), BF16),
        [pl.BlockSpec(memory_space=pl.ANY)] * 7,
        vmem(),
        [
            pltpu.SMEM(lengths.shape, jnp.int32),
            pltpu.SMEM(take_list.shape, jnp.int32),
            pltpu.VMEM(waveforms.shape, F32),
            pltpu.VMEM(kernels.shape, F32),
            pltpu.VMEM(norm_gain.shape, F32),
            pltpu.VMEM(norm_shift.shape, F32),
            pltpu.VMEM(conv_second.shape, BF16),
            pltpu.SemaphoreType.DMA((6,)),
            pltpu.SemaphoreType.DMA((checkpoints,)),
        ],
        flops=2 * slots * frames * feature * 3 * channels,
        moved=2 * conv_second.size,
    )(
        *[
            far(value)
            for value in (lengths, take_list, waveforms, kernels, norm_gain, norm_shift, conv_second)
        ]
    )

    weights_sum = call(
        norms_kernel,
        "norms",
        fast((8, latents), F32),
        [vmem()],
        vmem(),
        flops=4 * dec_weight.size,
        moved=2 * dec_weight.size,
    )(decoder)

    blocks = [packed] + [exchange(packed, step * k) for k in range(1, outer)]
    pieces = [
        call(
            join_kernel,
            "join",
            fast((outer * slots * frames, feature), BF16),
            [pl.BlockSpec(memory_space=pl.ANY)] * 2 + [vmem()] * outer,
            vmem(),
            moved=4 * outer * slots * frames * feature,
        )(near(weights_sum), encoder, *[near(block) for block in blocks])
    ]
    bit = 2
    while bit < step:
        pieces = pieces + [exchange(piece, bit) for piece in pieces]
        bit *= 2
    pieces = pieces + [exchange(piece, 1) for piece in pieces]

    half = tokens // 2
    chunk = half // outer

    def encode(*refs):
        encode_kernel(len(pieces), outer, inner, slots, frames, *refs)

    send, inputs, latent = call(
        encode,
        "encode",
        (fast((half, wide), BF16), fast((tokens, feature), BF16), fast((tokens, latents), F32)),
        [smem()]
        + [vmem()] * (len(pieces) + 1)
        + [pl.BlockSpec(memory_space=pl.ANY)]
        + [vmem()] * 3,
        (vmem(),) * 3,
        [pltpu.VMEM((feature - early, latents), BF16), pltpu.SemaphoreType.DMA],
        flops=3 * tokens * feature * latents,
        moved=4 * dec_weight.size,
    )(
        position,
        *[near(piece) for piece in pieces],
        encoder,
        far(enc_weight),
        enc_bias.reshape(1, latents),
        decoder,
        near(weights_sum),
    )
    received = exchange(send, 1)
    own, shift = call(
        own_kernel,
        "own",
        (fast((half, wide), F32), fast((chunk, wide), F32)),
        [vmem()] * 5,
        (vmem(),) * 2,
        flops=tokens * feature * latents,
        moved=2 * dec_weight.size,
    )(near(inputs), near(latent), decoder, near(weights_sum), dec_bias)

    inputs_t, latent_t, scale = call(
        turn_kernel,
        "turn",
        (fast((feature, tokens), BF16), fast((latents, tokens), BF16), fast((latents, LANES), F32)),
        [vmem()] * 3,
        (vmem(),) * 3,
        flops=2 * tokens * feature,
        moved=4 * tokens * feature,
    )(near(inputs), near(latent), decoder)

    part = own + received.astype(F32)
    small = part.astype(BF16)
    blocks = [part[:chunk]]
    for k in range(1, outer):
        blocks.append(exchange(small[k * chunk : (k + 1) * chunk], step * k))
    total = call(
        sum_kernel,
        "sum",
        fast((chunk, wide), BF16),
        [pl.BlockSpec(memory_space=pl.ANY)] + [vmem()] * outer,
        vmem(),
        moved=8 * chunk * wide,
    )(near(scale), *[near(block) for block in blocks])
    bit = 2
    while bit < step:
        width = (bit // 2) * ROWS_DEV
        other = exchange(total, bit).astype(F32).reshape(-1, 2, width, wide)
        part = total.astype(F32) + other[:, ::-1].reshape(chunk, wide)
        total = part.astype(BF16)
        bit *= 2
    errors = (part + shift).astype(BF16)
    blocks = [errors] + [exchange(errors, step * k) for k in range(1, outer)]
    blocks += [exchange(block, 1) for block in blocks]

    def gradients(*refs):
        gradients_kernel(len(blocks), inner, float(tokens * feature), *refs)

    any_space = pl.BlockSpec(memory_space=pl.ANY)
    enc_grad, dec_grad, enc_bias_grad, dec_bias_grad, mean_loss, errors_own = call(
        gradients,
        "gradients",
        (
            shape((feature, latents), BF16),
            shape((latents, feature), BF16),
            shape((1, latents), F32),
            shape((feature,), F32),
            shape((1,), F32),
            shape((ROWS_DEV, feature), BF16),
        ),
        [vmem()] * (len(blocks) + 6),
        (any_space, any_space, vmem(), vmem(), smem(), vmem()),
        [
            pltpu.VMEM((feature, latents), BF16),
            pltpu.VMEM((latents, feature), BF16),
            pltpu.SemaphoreType.DMA((8,)),
        ],
        flops=6 * tokens * feature * latents,
        moved=8 * dec_weight.size,
    )(
        *[near(block) for block in blocks],
        decoder,
        near(weights_sum),
        near(inputs_t),
        near(latent_t),
        near(latent),
        near(scale),
    )
    return (
        enc_grad,
        dec_grad,
        enc_bias_grad.reshape(latents),
        dec_bias_grad,
        mean_loss,
        errors_own,
    )


def solution(mesh):
    return jax.shard_map(
        shards,
        mesh=mesh,
        in_specs=(
            P(("groups", "utt"), None),
            P(("groups", "utt")),
            P(("groups", "utt")),
            P(),
            P(),
            P(),
            P(),
            P(None, "utt"),
            P("utt"),
            P("utt", None),
            P(),
        ),
        out_specs=(
            P("groups", "utt"),
            P(("groups", "utt"), None),
            P(("groups", "utt")),
            P("groups"),
            P("groups"),
            P(("groups", "utt"), None),
        ),
        check_vma=False,
    )
```

```python
import functools

import jax
import jax.numpy as jnp
from jax import lax
from jax.experimental import pallas as pl
from jax.experimental.pallas import tpu as pltpu
from jax.sharding import PartitionSpec as P

ROWS_DEV = 8
EXTRA = 128
LANES = 128
VMEM_BYTES = 56 << 20
PINNED_BYTES = 24 << 20
PINNED_TOKENS = 256
GROUP_ROWS = 256
DEC_PARTS = 2

sparsity = 0.5
epsilon = 1e-05

F32 = jnp.float32
BF16 = jnp.bfloat16

ERF_LIMIT = 3.7439211627767994
ERF_TOP = (
    0.00022905065861350646,
    0.0034082910107109506,
    0.050955695062380861,
    0.18520832239976145,
    1.128379143519084,
)
ERF_BOTTOM = (
    -1.1791602954361697e-7,
    0.000023547966471313185,
    0.0010179625278914885,
    0.014070470171167667,
    0.11098505178285362,
    0.49746925110067538,
    1.0,
)


def polynomial(x, terms):
    total = jnp.full_like(x, terms[0])
    for term in terms[1:]:
        total = total * x + term
    return total


def gelu(x):
    z = jnp.clip(x * 0.7071067811865476, -ERF_LIMIT, ERF_LIMIT)
    square = z * z
    erf = z * polynomial(square, ERF_TOP) / polynomial(square, ERF_BOTTOM)
    return 0.5 * x * (1.0 + erf)


def normalize(values, gain, shift):
    center = values - jnp.mean(values, axis=-1, keepdims=True)
    spread = jnp.mean(center * center, axis=-1, keepdims=True)
    return center * lax.rsqrt(spread + epsilon) * gain + shift


def levels(devices):
    chips = devices // 2
    outer = 1
    while outer * outer < chips:
        outer *= 2
    return outer, chips // outer


def exchange(value, bit):
    devices = lax.axis_size("utt")
    return lax.ppermute(value, "utt", [(i, i ^ bit) for i in range(devices)])


def tree(parts):
    while len(parts) > 1:
        parts = [parts[i] + parts[i + 1] for i in range(0, len(parts), 2)]
    return parts[0]


def iota(shape, dim):
    return lax.broadcasted_iota(jnp.int32, shape, dim)


def log2(n):
    return n.bit_length() - 1


def vmem():
    return pl.BlockSpec(memory_space=pltpu.VMEM)


def smem():
    return pl.BlockSpec(memory_space=pltpu.SMEM)


def launch(
    kernel, name, out_shape, in_specs, out_specs, scratch=(), flops=0, moved=0, limit=0
):
    return pl.pallas_call(
        kernel,
        name=name,
        out_shape=out_shape,
        in_specs=in_specs,
        out_specs=out_specs,
        scratch_shapes=list(scratch),
        compiler_params=pltpu.CompilerParams(vmem_limit_bytes=limit),
        cost_estimate=pl.CostEstimate(flops=flops, bytes_accessed=moved, transcendentals=0),
    )


def shape(dims, kind):
    return jax.ShapeDtypeStruct(dims, kind)


def features_kernel(*refs):
    sources, out, held, second_w, sems, more = refs[:7], refs[7], refs[8:14], refs[14], refs[15], refs[16]
    small = [pltpu.make_async_copy(sources[i], held[i], sems.at[i]) for i in range(6)]
    for copy in small:
        copy.start()
    length, take, wave, first_w, gain, shift = held
    taps_first, checkpoints, channels = first_w.shape
    slots, samples = wave.shape
    frames = out.shape[0] // slots
    copies = []
    for c in range(checkpoints):
        copies.append(pltpu.make_async_copy(sources[6].at[c], second_w.at[c], more.at[c]))
        copies[-1].start()
    for copy in small:
        copy.wait()
    lane = iota((frames, samples), 1)
    start = iota((frames, samples), 0) * 10
    columns = []
    for s in range(slots):
        row = jnp.broadcast_to(wave[s : s + 1, :], (frames, samples))
        columns.append(
            [
                jnp.sum(jnp.where(lane == start + o, row, 0.0), axis=1, keepdims=True)
                for o in range(taps_first + 10)
            ]
        )
    taps = [
        jnp.concatenate(
            [columns[s][5 * tap + k] for tap in range(3) for s in range(slots)], axis=0
        )
        for k in range(taps_first)
    ]

    def layer_one(c):
        total = taps[0] * first_w[0, c : c + 1, :]
        for k in range(1, taps_first):
            total = total + taps[k] * first_w[k, c : c + 1, :]
        return gelu(normalize(total, gain[c, 0:1, :], shift[c, 0:1, :])).astype(BF16)

    rows = slots * frames

    def layer_two(c, hidden):
        total = jnp.zeros((rows, channels), F32)
        for tap in range(3):
            total = total + jnp.dot(
                hidden[tap * rows : (tap + 1) * rows],
                second_w[c, tap * channels : (tap + 1) * channels, :],
                preferred_element_type=F32,
            )
        return total

    def finish(c, total):
        total = gelu(normalize(total, gain[c, 1:2, :], shift[c, 1:2, :]))
        if c == 0:
            spot = iota((rows, channels), 1)
            line = iota((rows, channels), 0)
            for s in range(slots):
                note = jnp.where(spot == 0, length[s].astype(F32), take[s].astype(F32))
                total = jnp.where(line == (s + 1) * frames - 1, note, total)
        out[:, c * channels : (c + 1) * channels] = total.astype(BF16)

    hidden = layer_one(0)
    held_back = None
    for c in range(checkpoints):
        copies[c].wait()
        total = layer_two(c, hidden)
        if c + 1 < checkpoints:
            hidden = layer_one(c + 1)
        if held_back is not None:
            finish(c - 1, held_back)
        held_back = total
    finish(checkpoints - 1, held_back)


def join_kernel(*refs):
    out = refs[-1]
    at = 0
    for ref in refs[2:-1]:
        out[at : at + ref.shape[0], :] = ref[...]
        at += ref.shape[0]


def norms_kernel(dec, norms, row):
    latents, feature = dec.shape
    channels = 512
    spot = iota((latents, LANES), 1)
    packed = jnp.zeros((latents, LANES), F32)
    total = jnp.zeros((latents, 1), F32)
    for c in range(feature // channels):
        block = dec[:, c * channels : (c + 1) * channels].astype(F32)
        norm = jnp.sqrt(jnp.sum(block * block, axis=1, keepdims=True) + 1e-06)
        total = total + norm
        packed = jnp.where(spot == c, norm, packed)
    norms[...] = packed
    row[...] = jnp.broadcast_to(total, (latents, LANES)).T[:8]


def encode_kernel(count, outer, inner, slots, frames, *refs):
    me_ref = refs[0]
    pieces = refs[1 : 1 + count]
    enc, bias, dec_hbm, weights_sum = refs[1 + count : 5 + count]
    send, inputs_out, latent_out, dec, sems = refs[5 + count :]
    part_rows = dec.shape[0] // DEC_PARTS
    fetches = []
    for i in range(DEC_PARTS):
        at = pl.ds(i * part_rows, part_rows)
        fetches.append(pltpu.make_async_copy(dec_hbm.at[at], dec.at[at], sems.at[i]))
        fetches[-1].start()
    me = me_ref[0]
    step = 2 * inner
    tokens, feature = inputs_out.shape
    rows = pieces[0].shape[0]
    group = max(GROUP_ROWS // rows, 1)
    width = group * rows
    held = width // frames
    shift_frames, shift_slots = log2(frames), log2(slots)

    def device_of(place):
        bits = (place & (outer - 1)) * step
        bits = bits + ((place >> log2(outer)) & (inner - 1)) * 2 + (place >> log2(outer * inner))
        return me ^ bits

    choose = (iota((held, width), 1) == iota((held, width), 0) * frames + frames - 1).astype(BF16)
    last = (iota((width, width), 0) == (iota((width, width), 1) | (frames - 1))).astype(BF16)
    ident = (iota((16, LANES), 0) == iota((16, LANES), 1)).astype(BF16)
    groups, takes, starts = [], [], []
    for g in range(0, len(pieces), group):
        parts = [piece[...] for piece in pieces[g : g + group]]
        groups.append(parts[0] if group == 1 else jnp.concatenate(parts, axis=0))
        notes = jnp.dot(choose, groups[-1][:, :LANES], preferred_element_type=F32)
        takes.append(notes[:, 1:2].astype(jnp.int32))
        slot = g * rows // frames + iota((held, 1), 0)
        starts.append(device_of(slot >> shift_slots) * ROWS_DEV)
    takes = jnp.concatenate(takes, axis=0)
    starts = jnp.concatenate(starts, axis=0)
    kinds = iota(takes.shape, 0) & (slots - 1)
    r = iota((tokens, 1), 0) >> log2(ROWS_DEV)
    holder = (
        ((r >> log2(inner)) & (outer - 1)) * step + (r & (inner - 1)) * 2 + (r >> log2(outer * inner))
    )
    token = (me ^ holder) * ROWS_DEV + (iota((tokens, 1), 0) & (ROWS_DEV - 1))
    lane = iota((1, width), 1)
    frame = lane & (frames - 1)
    total = jnp.zeros((tokens, feature), F32)
    for g, block in enumerate(groups):
        turned = lax.dot_general(
            ident, block[:, :LANES], (((1,), (1,)), ((), ())), preferred_element_type=F32
        )
        turned = jnp.dot(turned.astype(BF16), last, preferred_element_type=F32)
        size = turned[0:1, :].astype(jnp.int32)
        device = device_of((g * width + lane) >> (shift_frames + shift_slots))
        label = device * slots + ((lane >> shift_frames) & (slots - 1))
        match = takes == label
        begin = jnp.sum(jnp.where(match, starts, 0), axis=0, keepdims=True)
        second = jnp.sum(jnp.where(match, kinds, 0), axis=0, keepdims=True)
        target = begin + second * (ROWS_DEV - size) + frame
        target = jnp.where(frame < size, target, -1)
        pick = jnp.where(token == target, 1.0, 0.0).astype(BF16)
        total = total + jnp.dot(pick, block, preferred_element_type=F32)
    inputs = total.astype(BF16)
    inputs_out[...] = inputs
    latent = jnp.maximum(jnp.dot(inputs, enc[...], preferred_element_type=F32) + bias[...], 0.0)
    latent_out[...] = latent
    half = tokens // 2
    rounded = latent[half:].astype(BF16)
    middle = dec.shape[0] // 2
    for fetch in fetches[: DEC_PARTS // 2]:
        fetch.wait()
    part = jnp.dot(rounded[:, :middle], dec[:middle], preferred_element_type=F32)
    for fetch in fetches[DEC_PARTS // 2 :]:
        fetch.wait()
    part = part + jnp.dot(rounded[:, middle:], dec[middle:], preferred_element_type=F32)
    send[:, :feature] = part.astype(BF16)
    send[:, feature:] = lane_sums(latent[half:] * weights_sum[0:1, :]).astype(BF16)


def lane_sums(weighted):
    extra = weighted[:, :LANES]
    for q in range(1, weighted.shape[1] // LANES):
        extra = extra + weighted[:, q * LANES : (q + 1) * LANES]
    return extra


def own_kernel(inputs, latent, dec, weights_sum, dec_bias, own, shift):
    half, chunk = own.shape[0], shift.shape[0]
    feature = dec.shape[1]
    kept = latent[:half]
    own[:, :feature] = jnp.dot(kept.astype(BF16), dec[...], preferred_element_type=F32)
    own[:, feature:] = lane_sums(kept * weights_sum[0:1, :])
    shift[:, :feature] = dec_bias[...].reshape(1, feature) - inputs[:chunk].astype(F32)
    shift[:, feature:] = jnp.zeros((chunk, EXTRA), F32)


def turn_kernel(inputs, latent, norms, inputs_t, latent_t, scale):
    inputs_t[...] = inputs[...].astype(F32).T.astype(BF16)
    turned = latent[...].T
    latent_t[...] = (2.0 * turned).astype(BF16)
    activity = jnp.sum(turned, axis=1, keepdims=True)
    scale[...] = (sparsity * activity) / jnp.maximum(norms[...], 1e-30)


def sum_kernel(*refs):
    total = refs[1][...]
    for ref in refs[2:-1]:
        total = total + ref[...].astype(F32)
    refs[-1][...] = total.astype(BF16)


def gradients_kernel(count, inner, cells, *refs):
    pieces = refs[:count]
    dec, weights_sum, inputs_t, latent_t, latent, scale = refs[count : count + 6]
    enc_out, dec_out, enc_bias_out, dec_bias_out, loss_out, errors_out = refs[count + 6 : count + 12]
    enc_buf, dec_buf, sems = refs[count + 12 :]
    latents, feature = dec.shape
    channels = 512
    errors = jnp.concatenate([piece[:, :feature] for piece in pieces], axis=0)
    copies = []
    parts = 4
    size = latents // parts
    for i in range(parts):
        at = slice(i * size, (i + 1) * size)
        grad = jnp.dot(latent_t[at], errors, preferred_element_type=F32)
        for c in range(feature // channels):
            lanes = slice(c * channels, (c + 1) * channels)
            term = scale[at, c : c + 1] * dec[at, lanes].astype(F32)
            dec_buf[at, lanes] = (grad[:, lanes] + term).astype(BF16)
        copies.append(pltpu.make_async_copy(dec_buf.at[at], dec_out.at[at], sems.at[i]))
        copies[-1].start()
    upstream = lax.dot_general(
        errors, dec[...], (((1,), (1,)), ((), ())), preferred_element_type=F32
    )
    upstream = 2.0 * upstream + sparsity * weights_sum[0:1, :]
    through = jnp.where(latent[...] > 0.0, upstream, 0.0)
    enc_bias_out[...] = jnp.sum(through, axis=0, keepdims=True)
    through = through.astype(BF16)
    size = feature // parts
    for i in range(parts):
        at = slice(i * size, (i + 1) * size)
        grad = jnp.dot(inputs_t[at], through, preferred_element_type=F32)
        enc_buf[at] = grad.astype(BF16)
        copies.append(pltpu.make_async_copy(enc_buf.at[at], enc_out.at[at], sems.at[parts + i]))
        copies[-1].start()
    errors_out[...] = pieces[0][:ROWS_DEV, :feature]
    wide = [piece[...].astype(F32) for piece in pieces]
    plain = tree(wide)
    squares = tree([w[:, :feature] * w[:, :feature] for w in wide])
    plain = tree([plain[i * ROWS_DEV : (i + 1) * ROWS_DEV] for i in range(inner)])
    squares = tree([squares[i * ROWS_DEV : (i + 1) * ROWS_DEV] for i in range(inner)])
    dec_bias_out[...] = 2.0 * jnp.sum(plain[:, :feature], axis=0)
    loss = jnp.sum(squares) + sparsity * jnp.sum(plain[:, feature:])
    loss_out[0] = loss / cells
    for copy in copies:
        copy.wait()


def shards(
    waveforms,
    lengths,
    take_list,
    conv_first,
    conv_second,
    norm_gain,
    norm_shift,
    enc_weight,
    enc_bias,
    dec_weight,
    dec_bias,
):
    slots = take_list.shape[0]
    devices = lax.axis_size("utt")
    outer, inner = levels(devices)
    step = 2 * inner
    tokens = ROWS_DEV * devices
    position = lax.axis_index("utt").astype(jnp.int32).reshape(1)
    feature, latents = enc_weight.shape
    checkpoints, _, channels = conv_first.shape
    frames = (waveforms.shape[1] - 10) // 10
    wide = feature + EXTRA

    pinned = tokens <= PINNED_TOKENS
    call = functools.partial(launch, limit=PINNED_BYTES if pinned else VMEM_BYTES)

    def fast(dims, kind):
        return pltpu.VMEM(dims, kind) if pinned else shape(dims, kind)

    def near(value):
        return pltpu.with_memory_space_constraint(value, pltpu.VMEM) if pinned else value

    def far(value):
        return pltpu.with_memory_space_constraint(value, pltpu.HBM)

    kernels = conv_first.transpose(1, 0, 2)
    encoder = near(enc_weight)
    decoder = near(dec_weight)

    packed = call(
        features_kernel,
        "features",
        fast((slots * frames, feature), BF16),
        [pl.BlockSpec(memory_space=pl.ANY)] * 7,
        vmem(),
        [
            pltpu.SMEM(lengths.shape, jnp.int32),
            pltpu.SMEM(take_list.shape, jnp.int32),
            pltpu.VMEM(waveforms.shape, F32),
            pltpu.VMEM(kernels.shape, F32),
            pltpu.VMEM(norm_gain.shape, F32),
            pltpu.VMEM(norm_shift.shape, F32),
            pltpu.VMEM(conv_second.shape, BF16),
            pltpu.SemaphoreType.DMA((6,)),
            pltpu.SemaphoreType.DMA((checkpoints,)),
        ],
        flops=2 * slots * frames * feature * 3 * channels,
        moved=2 * conv_second.size,
    )(
        *[
            far(value)
            for value in (lengths, take_list, waveforms, kernels, norm_gain, norm_shift, conv_second)
        ]
    )

    norms, weights_sum = call(
        norms_kernel,
        "norms",
        (fast((latents, LANES), F32), fast((8, latents), F32)),
        [vmem()],
        (vmem(), vmem()),
        flops=4 * dec_weight.size,
        moved=2 * dec_weight.size,
    )(decoder)

    blocks = [packed] + [exchange(packed, step * k) for k in range(1, outer)]
    pieces = [
        call(
            join_kernel,
            "join",
            fast((outer * slots * frames, feature), BF16),
            [pl.BlockSpec(memory_space=pl.ANY)] * 2 + [vmem()] * outer,
            vmem(),
            moved=4 * outer * slots * frames * feature,
        )(near(norms), encoder, *[near(block) for block in blocks])
    ]
    bit = 2
    while bit < step:
        pieces = pieces + [exchange(piece, bit) for piece in pieces]
        bit *= 2
    pieces = pieces + [exchange(piece, 1) for piece in pieces]

    half = tokens // 2
    chunk = half // outer

    def encode(*refs):
        encode_kernel(len(pieces), outer, inner, slots, frames, *refs)

    send, inputs, latent, decoder = call(
        encode,
        "encode",
        (
            fast((half, wide), BF16),
            fast((tokens, feature), BF16),
            fast((tokens, latents), F32),
            fast(dec_weight.shape, BF16),
        ),
        [smem()] + [vmem()] * (len(pieces) + 2) + [pl.BlockSpec(memory_space=pl.ANY), vmem()],
        (vmem(),) * 4,
        [pltpu.SemaphoreType.DMA((DEC_PARTS,))],
        flops=3 * tokens * feature * latents,
        moved=4 * dec_weight.size,
    )(
        position,
        *[near(piece) for piece in pieces],
        encoder,
        enc_bias.reshape(1, latents),
        far(dec_weight),
        near(weights_sum),
    )
    received = exchange(send, 1)
    decoder = near(decoder)
    own, shift = call(
        own_kernel,
        "own",
        (fast((half, wide), F32), fast((chunk, wide), F32)),
        [vmem()] * 5,
        (vmem(),) * 2,
        flops=tokens * feature * latents,
        moved=2 * dec_weight.size,
    )(near(inputs), near(latent), decoder, near(weights_sum), dec_bias)

    inputs_t, latent_t, scale = call(
        turn_kernel,
        "turn",
        (fast((feature, tokens), BF16), fast((latents, tokens), BF16), fast((latents, LANES), F32)),
        [vmem()] * 3,
        (vmem(),) * 3,
        flops=2 * tokens * feature,
        moved=4 * tokens * feature,
    )(near(inputs), near(latent), near(norms))

    part = own + received.astype(F32)
    small = part.astype(BF16)
    blocks = [part[:chunk]]
    for k in range(1, outer):
        blocks.append(exchange(small[k * chunk : (k + 1) * chunk], step * k))
    total = call(
        sum_kernel,
        "sum",
        fast((chunk, wide), BF16),
        [pl.BlockSpec(memory_space=pl.ANY)] + [vmem()] * outer,
        vmem(),
        moved=8 * chunk * wide,
    )(near(scale), *[near(block) for block in blocks])
    bit = 2
    while bit < step:
        width = (bit // 2) * ROWS_DEV
        other = exchange(total, bit).astype(F32).reshape(-1, 2, width, wide)
        part = total.astype(F32) + other[:, ::-1].reshape(chunk, wide)
        total = part.astype(BF16)
        bit *= 2
    errors = (part + shift).astype(BF16)
    blocks = [errors] + [exchange(errors, step * k) for k in range(1, outer)]
    blocks += [exchange(block, 1) for block in blocks]

    def gradients(*refs):
        gradients_kernel(len(blocks), inner, float(tokens * feature), *refs)

    any_space = pl.BlockSpec(memory_space=pl.ANY)
    enc_grad, dec_grad, enc_bias_grad, dec_bias_grad, mean_loss, errors_own = call(
        gradients,
        "gradients",
        (
            shape((feature, latents), BF16),
            shape((latents, feature), BF16),
            shape((1, latents), F32),
            shape((feature,), F32),
            shape((1,), F32),
            shape((ROWS_DEV, feature), BF16),
        ),
        [vmem()] * (len(blocks) + 6),
        (any_space, any_space, vmem(), vmem(), smem(), vmem()),
        [
            pltpu.VMEM((feature, latents), BF16),
            pltpu.VMEM((latents, feature), BF16),
            pltpu.SemaphoreType.DMA((8,)),
        ],
        flops=6 * tokens * feature * latents,
        moved=8 * dec_weight.size,
    )(
        *[near(block) for block in blocks],
        decoder,
        near(weights_sum),
        near(inputs_t),
        near(latent_t),
        near(latent),
        near(scale),
    )
    return (
        enc_grad,
        dec_grad,
        enc_bias_grad.reshape(latents),
        dec_bias_grad,
        mean_loss,
        errors_own,
    )


def solution(mesh):
    return jax.shard_map(
        shards,
        mesh=mesh,
        in_specs=(
            P(("groups", "utt"), None),
            P(("groups", "utt")),
            P(("groups", "utt")),
            P(),
            P(),
            P(),
            P(),
            P(None, "utt"),
            P("utt"),
            P("utt", None),
            P(),
        ),
        out_specs=(
            P("groups", "utt"),
            P(("groups", "utt"), None),
            P(("groups", "utt")),
            P("groups"),
            P("groups"),
            P(("groups", "utt"), None),
        ),
        check_vma=False,
    )
```

```python
import functools

import jax
import jax.numpy as jnp
from jax import lax
from jax.experimental import pallas as pl
from jax.experimental.pallas import tpu as pltpu
from jax.sharding import PartitionSpec as P

ROWS_DEV = 8
EXTRA = 128
LANES = 128
VMEM_BYTES = 56 << 20
PINNED_BYTES = 24 << 20
PINNED_TOKENS = 256
GROUP_ROWS = 256
DEC_PARTS = 2

sparsity = 0.5
epsilon = 1e-05

F32 = jnp.float32
BF16 = jnp.bfloat16

ERF_LIMIT = 3.7439211627767994
ERF_TOP = (
    0.00022905065861350646,
    0.0034082910107109506,
    0.050955695062380861,
    0.18520832239976145,
    1.128379143519084,
)
ERF_BOTTOM = (
    -1.1791602954361697e-7,
    0.000023547966471313185,
    0.0010179625278914885,
    0.014070470171167667,
    0.11098505178285362,
    0.49746925110067538,
    1.0,
)


def polynomial(x, terms):
    total = jnp.full_like(x, terms[0])
    for term in terms[1:]:
        total = total * x + term
    return total


def gelu(x):
    z = jnp.clip(x * 0.7071067811865476, -ERF_LIMIT, ERF_LIMIT)
    square = z * z
    erf = z * polynomial(square, ERF_TOP) / polynomial(square, ERF_BOTTOM)
    return 0.5 * x * (1.0 + erf)


def normalize(values, gain, shift):
    center = values - jnp.mean(values, axis=-1, keepdims=True)
    spread = jnp.mean(center * center, axis=-1, keepdims=True)
    return center * lax.rsqrt(spread + epsilon) * gain + shift


def levels(devices):
    chips = devices // 2
    outer = 1
    while outer * outer < chips:
        outer *= 2
    return outer, chips // outer


def exchange(value, bit):
    devices = lax.axis_size("utt")
    return lax.ppermute(value, "utt", [(i, i ^ bit) for i in range(devices)])


def tree(parts):
    while len(parts) > 1:
        parts = [parts[i] + parts[i + 1] for i in range(0, len(parts), 2)]
    return parts[0]


def iota(shape, dim):
    return lax.broadcasted_iota(jnp.int32, shape, dim)


def log2(n):
    return n.bit_length() - 1


def vmem():
    return pl.BlockSpec(memory_space=pltpu.VMEM)


def smem():
    return pl.BlockSpec(memory_space=pltpu.SMEM)


def launch(
    kernel, name, out_shape, in_specs, out_specs, scratch=(), flops=0, moved=0, limit=0
):
    return pl.pallas_call(
        kernel,
        name=name,
        out_shape=out_shape,
        in_specs=in_specs,
        out_specs=out_specs,
        scratch_shapes=list(scratch),
        compiler_params=pltpu.CompilerParams(vmem_limit_bytes=limit),
        cost_estimate=pl.CostEstimate(flops=flops, bytes_accessed=moved, transcendentals=0),
    )


def shape(dims, kind):
    return jax.ShapeDtypeStruct(dims, kind)


def features_kernel(*refs):
    sources, out, held, second_w, sems, more = refs[:7], refs[7], refs[8:14], refs[14], refs[15], refs[16]
    small = [pltpu.make_async_copy(sources[i], held[i], sems.at[i]) for i in range(6)]
    for copy in small:
        copy.start()
    length, take, wave, first_w, gain, shift = held
    taps_first, checkpoints, channels = first_w.shape
    slots, samples = wave.shape
    frames = out.shape[0] // slots
    copies = []
    for c, n in ((0, 1), (1, checkpoints - 1)):
        at = pl.ds(c, n)
        copies.append(pltpu.make_async_copy(sources[6].at[at], second_w.at[at], more.at[c]))
        copies[-1].start()
    for copy in small:
        copy.wait()
    lane = iota((frames, samples), 1)
    start = iota((frames, samples), 0) * 10
    columns = []
    for s in range(slots):
        row = jnp.broadcast_to(wave[s : s + 1, :], (frames, samples))
        columns.append(
            [
                jnp.sum(jnp.where(lane == start + o, row, 0.0), axis=1, keepdims=True)
                for o in range(taps_first + 10)
            ]
        )
    taps = [
        jnp.concatenate(
            [columns[s][5 * tap + k] for tap in range(3) for s in range(slots)], axis=0
        )
        for k in range(taps_first)
    ]

    def layer_one(c):
        total = taps[0] * first_w[0, c : c + 1, :]
        for k in range(1, taps_first):
            total = total + taps[k] * first_w[k, c : c + 1, :]
        return gelu(normalize(total, gain[c, 0:1, :], shift[c, 0:1, :])).astype(BF16)

    rows = slots * frames

    def layer_two(c, hidden):
        total = jnp.zeros((rows, channels), F32)
        for tap in range(3):
            total = total + jnp.dot(
                hidden[tap * rows : (tap + 1) * rows],
                second_w[c, tap * channels : (tap + 1) * channels, :],
                preferred_element_type=F32,
            )
        return total

    def finish(c, total):
        total = gelu(normalize(total, gain[c, 1:2, :], shift[c, 1:2, :]))
        if c == 0:
            spot = iota((rows, channels), 1)
            line = iota((rows, channels), 0)
            for s in range(slots):
                note = jnp.where(spot == 0, length[s].astype(F32), take[s].astype(F32))
                total = jnp.where(line == (s + 1) * frames - 1, note, total)
        out[:, c * channels : (c + 1) * channels] = total.astype(BF16)

    hidden = layer_one(0)
    held_back = None
    for c in range(checkpoints):
        if c < len(copies):
            copies[c].wait()
        total = layer_two(c, hidden)
        if c + 1 < checkpoints:
            hidden = layer_one(c + 1)
        if held_back is not None:
            finish(c - 1, held_back)
        held_back = total
    finish(checkpoints - 1, held_back)


def join_kernel(*refs):
    out = refs[-1]
    at = 0
    for ref in refs[2:-1]:
        out[at : at + ref.shape[0], :] = ref[...]
        at += ref.shape[0]


def norms_kernel(dec, norms, row):
    latents, feature = dec.shape
    channels = 512
    spot = iota((latents, LANES), 1)
    packed = jnp.zeros((latents, LANES), F32)
    total = jnp.zeros((latents, 1), F32)
    for c in range(feature // channels):
        block = dec[:, c * channels : (c + 1) * channels].astype(F32)
        norm = jnp.sqrt(jnp.sum(block * block, axis=1, keepdims=True) + 1e-06)
        total = total + norm
        packed = jnp.where(spot == c, norm, packed)
    norms[...] = packed
    row[...] = jnp.broadcast_to(total, (latents, LANES)).T[:8]


def encode_kernel(count, outer, inner, slots, frames, *refs):
    me_ref = refs[0]
    pieces = refs[1 : 1 + count]
    enc, bias, dec_hbm, weights_sum = refs[1 + count : 5 + count]
    send, inputs_out, latent_out, dec, sems = refs[5 + count :]
    part_rows = dec.shape[0] // DEC_PARTS
    fetches = []
    for i in range(DEC_PARTS):
        at = pl.ds(i * part_rows, part_rows)
        fetches.append(pltpu.make_async_copy(dec_hbm.at[at], dec.at[at], sems.at[i]))
        fetches[-1].start()
    me = me_ref[0]
    step = 2 * inner
    tokens, feature = inputs_out.shape
    rows = pieces[0].shape[0]
    group = max(GROUP_ROWS // rows, 1)
    width = group * rows
    held = width // frames
    shift_frames, shift_slots = log2(frames), log2(slots)

    def device_of(place):
        bits = (place & (outer - 1)) * step
        bits = bits + ((place >> log2(outer)) & (inner - 1)) * 2 + (place >> log2(outer * inner))
        return me ^ bits

    choose = (iota((held, width), 1) == iota((held, width), 0) * frames + frames - 1).astype(BF16)
    last = (iota((width, width), 0) == (iota((width, width), 1) | (frames - 1))).astype(BF16)
    ident = (iota((16, LANES), 0) == iota((16, LANES), 1)).astype(BF16)
    groups, takes, starts = [], [], []
    for g in range(0, len(pieces), group):
        parts = [piece[...] for piece in pieces[g : g + group]]
        groups.append(parts[0] if group == 1 else jnp.concatenate(parts, axis=0))
        notes = jnp.dot(choose, groups[-1][:, :LANES], preferred_element_type=F32)
        takes.append(notes[:, 1:2].astype(jnp.int32))
        slot = g * rows // frames + iota((held, 1), 0)
        starts.append(device_of(slot >> shift_slots) * ROWS_DEV)
    takes = jnp.concatenate(takes, axis=0)
    starts = jnp.concatenate(starts, axis=0)
    kinds = iota(takes.shape, 0) & (slots - 1)
    r = iota((tokens, 1), 0) >> log2(ROWS_DEV)
    holder = (
        ((r >> log2(inner)) & (outer - 1)) * step + (r & (inner - 1)) * 2 + (r >> log2(outer * inner))
    )
    token = (me ^ holder) * ROWS_DEV + (iota((tokens, 1), 0) & (ROWS_DEV - 1))
    lane = iota((1, width), 1)
    frame = lane & (frames - 1)
    total = jnp.zeros((tokens, feature), F32)
    for g, block in enumerate(groups):
        turned = lax.dot_general(
            ident, block[:, :LANES], (((1,), (1,)), ((), ())), preferred_element_type=F32
        )
        turned = jnp.dot(turned.astype(BF16), last, preferred_element_type=F32)
        size = turned[0:1, :].astype(jnp.int32)
        device = device_of((g * width + lane) >> (shift_frames + shift_slots))
        label = device * slots + ((lane >> shift_frames) & (slots - 1))
        match = takes == label
        begin = jnp.sum(jnp.where(match, starts, 0), axis=0, keepdims=True)
        second = jnp.sum(jnp.where(match, kinds, 0), axis=0, keepdims=True)
        target = begin + second * (ROWS_DEV - size) + frame
        target = jnp.where(frame < size, target, -1)
        pick = jnp.where(token == target, 1.0, 0.0).astype(BF16)
        total = total + jnp.dot(pick, block, preferred_element_type=F32)
    inputs = total.astype(BF16)
    inputs_out[...] = inputs
    latent = jnp.maximum(jnp.dot(inputs, enc[...], preferred_element_type=F32) + bias[...], 0.0)
    latent_out[...] = latent
    half = tokens // 2
    rounded = latent[half:].astype(BF16)
    middle = dec.shape[0] // 2
    for fetch in fetches[: DEC_PARTS // 2]:
        fetch.wait()
    part = jnp.dot(rounded[:, :middle], dec[:middle], preferred_element_type=F32)
    for fetch in fetches[DEC_PARTS // 2 :]:
        fetch.wait()
    part = part + jnp.dot(rounded[:, middle:], dec[middle:], preferred_element_type=F32)
    send[:, :feature] = part.astype(BF16)
    send[:, feature:] = lane_sums(latent[half:] * weights_sum[0:1, :]).astype(BF16)


def lane_sums(weighted):
    extra = weighted[:, :LANES]
    for q in range(1, weighted.shape[1] // LANES):
        extra = extra + weighted[:, q * LANES : (q + 1) * LANES]
    return extra


def own_kernel(inputs, latent, dec, weights_sum, dec_bias, own, shift):
    half, chunk = own.shape[0], shift.shape[0]
    feature = dec.shape[1]
    kept = latent[:half]
    own[:, :feature] = jnp.dot(kept.astype(BF16), dec[...], preferred_element_type=F32)
    own[:, feature:] = lane_sums(kept * weights_sum[0:1, :])
    shift[:, :feature] = dec_bias[...].reshape(1, feature) - inputs[:chunk].astype(F32)
    shift[:, feature:] = jnp.zeros((chunk, EXTRA), F32)


def turn_kernel(inputs, latent, norms, inputs_t, latent_t, scale):
    inputs_t[...] = inputs[...].astype(F32).T.astype(BF16)
    turned = latent[...].T
    latent_t[...] = (2.0 * turned).astype(BF16)
    activity = jnp.sum(turned, axis=1, keepdims=True)
    scale[...] = (sparsity * activity) / jnp.maximum(norms[...], 1e-30)


def sum_kernel(*refs):
    total = refs[1][...]
    for ref in refs[2:-1]:
        total = total + ref[...].astype(F32)
    refs[-1][...] = total.astype(BF16)


def gradients_kernel(count, inner, cells, *refs):
    pieces = refs[:count]
    dec, weights_sum, inputs_t, latent_t, latent, scale = refs[count : count + 6]
    enc_out, dec_out, enc_bias_out, dec_bias_out, loss_out, errors_out = refs[count + 6 : count + 12]
    enc_buf, dec_buf, sems = refs[count + 12 :]
    latents, feature = dec.shape
    channels = 512
    errors = jnp.concatenate([piece[:, :feature] for piece in pieces], axis=0)
    copies = []
    parts = 4
    size = latents // parts
    for i in range(parts):
        at = slice(i * size, (i + 1) * size)
        grad = jnp.dot(latent_t[at], errors, preferred_element_type=F32)
        for c in range(feature // channels):
            lanes = slice(c * channels, (c + 1) * channels)
            term = scale[at, c : c + 1] * dec[at, lanes].astype(F32)
            dec_buf[at, lanes] = (grad[:, lanes] + term).astype(BF16)
        copies.append(pltpu.make_async_copy(dec_buf.at[at], dec_out.at[at], sems.at[i]))
        copies[-1].start()
    upstream = lax.dot_general(
        errors, dec[...], (((1,), (1,)), ((), ())), preferred_element_type=F32
    )
    upstream = 2.0 * upstream + sparsity * weights_sum[0:1, :]
    through = jnp.where(latent[...] > 0.0, upstream, 0.0)
    enc_bias_out[...] = jnp.sum(through, axis=0, keepdims=True)
    through = through.astype(BF16)
    size = feature // parts
    for i in range(parts):
        at = slice(i * size, (i + 1) * size)
        grad = jnp.dot(inputs_t[at], through, preferred_element_type=F32)
        enc_buf[at] = grad.astype(BF16)
        copies.append(pltpu.make_async_copy(enc_buf.at[at], enc_out.at[at], sems.at[parts + i]))
        copies[-1].start()
    errors_out[...] = pieces[0][:ROWS_DEV, :feature]
    wide = [piece[...].astype(F32) for piece in pieces]
    plain = tree(wide)
    squares = tree([w[:, :feature] * w[:, :feature] for w in wide])
    plain = tree([plain[i * ROWS_DEV : (i + 1) * ROWS_DEV] for i in range(inner)])
    squares = tree([squares[i * ROWS_DEV : (i + 1) * ROWS_DEV] for i in range(inner)])
    dec_bias_out[...] = 2.0 * jnp.sum(plain[:, :feature], axis=0)
    loss = jnp.sum(squares) + sparsity * jnp.sum(plain[:, feature:])
    loss_out[0] = loss / cells
    for copy in copies:
        copy.wait()


def shards(
    waveforms,
    lengths,
    take_list,
    conv_first,
    conv_second,
    norm_gain,
    norm_shift,
    enc_weight,
    enc_bias,
    dec_weight,
    dec_bias,
):
    slots = take_list.shape[0]
    devices = lax.axis_size("utt")
    outer, inner = levels(devices)
    step = 2 * inner
    tokens = ROWS_DEV * devices
    position = lax.axis_index("utt").astype(jnp.int32).reshape(1)
    feature, latents = enc_weight.shape
    checkpoints, _, channels = conv_first.shape
    frames = (waveforms.shape[1] - 10) // 10
    wide = feature + EXTRA

    pinned = tokens <= PINNED_TOKENS
    call = functools.partial(launch, limit=PINNED_BYTES if pinned else VMEM_BYTES)

    def fast(dims, kind):
        return pltpu.VMEM(dims, kind) if pinned else shape(dims, kind)

    def near(value):
        return pltpu.with_memory_space_constraint(value, pltpu.VMEM) if pinned else value

    def far(value):
        return pltpu.with_memory_space_constraint(value, pltpu.HBM)

    kernels = conv_first.transpose(1, 0, 2)
    encoder = near(enc_weight)
    decoder = near(dec_weight)

    packed = call(
        features_kernel,
        "features",
        fast((slots * frames, feature), BF16),
        [pl.BlockSpec(memory_space=pl.ANY)] * 7,
        vmem(),
        [
            pltpu.SMEM(lengths.shape, jnp.int32),
            pltpu.SMEM(take_list.shape, jnp.int32),
            pltpu.VMEM(waveforms.shape, F32),
            pltpu.VMEM(kernels.shape, F32),
            pltpu.VMEM(norm_gain.shape, F32),
            pltpu.VMEM(norm_shift.shape, F32),
            pltpu.VMEM(conv_second.shape, BF16),
            pltpu.SemaphoreType.DMA((6,)),
            pltpu.SemaphoreType.DMA((checkpoints,)),
        ],
        flops=2 * slots * frames * feature * 3 * channels,
        moved=2 * conv_second.size,
    )(
        *[
            far(value)
            for value in (lengths, take_list, waveforms, kernels, norm_gain, norm_shift, conv_second)
        ]
    )

    norms, weights_sum = call(
        norms_kernel,
        "norms",
        (fast((latents, LANES), F32), fast((8, latents), F32)),
        [vmem()],
        (vmem(), vmem()),
        flops=4 * dec_weight.size,
        moved=2 * dec_weight.size,
    )(decoder)

    blocks = [packed] + [exchange(packed, step * k) for k in range(1, outer)]
    pieces = [
        call(
            join_kernel,
            "join",
            fast((outer * slots * frames, feature), BF16),
            [pl.BlockSpec(memory_space=pl.ANY)] * 2 + [vmem()] * outer,
            vmem(),
            moved=4 * outer * slots * frames * feature,
        )(near(norms), encoder, *[near(block) for block in blocks])
    ]
    bit = 2
    while bit < step:
        pieces = pieces + [exchange(piece, bit) for piece in pieces]
        bit *= 2
    pieces = pieces + [exchange(piece, 1) for piece in pieces]

    half = tokens // 2
    chunk = half // outer

    def encode(*refs):
        encode_kernel(len(pieces), outer, inner, slots, frames, *refs)

    send, inputs, latent, decoder = call(
        encode,
        "encode",
        (
            fast((half, wide), BF16),
            fast((tokens, feature), BF16),
            fast((tokens, latents), F32),
            fast(dec_weight.shape, BF16),
        ),
        [smem()] + [vmem()] * (len(pieces) + 2) + [pl.BlockSpec(memory_space=pl.ANY), vmem()],
        (vmem(),) * 4,
        [pltpu.SemaphoreType.DMA((DEC_PARTS,))],
        flops=3 * tokens * feature * latents,
        moved=4 * dec_weight.size,
    )(
        position,
        *[near(piece) for piece in pieces],
        encoder,
        enc_bias.reshape(1, latents),
        far(dec_weight),
        near(weights_sum),
    )
    received = exchange(send, 1)
    decoder = near(decoder)
    own, shift = call(
        own_kernel,
        "own",
        (fast((half, wide), F32), fast((chunk, wide), F32)),
        [vmem()] * 5,
        (vmem(),) * 2,
        flops=tokens * feature * latents,
        moved=2 * dec_weight.size,
    )(near(inputs), near(latent), decoder, near(weights_sum), dec_bias)

    inputs_t, latent_t, scale = call(
        turn_kernel,
        "turn",
        (fast((feature, tokens), BF16), fast((latents, tokens), BF16), fast((latents, LANES), F32)),
        [vmem()] * 3,
        (vmem(),) * 3,
        flops=2 * tokens * feature,
        moved=4 * tokens * feature,
    )(near(inputs), near(latent), near(norms))

    part = own + received.astype(F32)
    small = part.astype(BF16)
    blocks = [part[:chunk]]
    for k in range(1, outer):
        blocks.append(exchange(small[k * chunk : (k + 1) * chunk], step * k))
    total = call(
        sum_kernel,
        "sum",
        fast((chunk, wide), BF16),
        [pl.BlockSpec(memory_space=pl.ANY)] + [vmem()] * outer,
        vmem(),
        moved=8 * chunk * wide,
    )(near(scale), *[near(block) for block in blocks])
    bit = 2
    while bit < step:
        width = (bit // 2) * ROWS_DEV
        other = exchange(total, bit).astype(F32).reshape(-1, 2, width, wide)
        part = total.astype(F32) + other[:, ::-1].reshape(chunk, wide)
        total = part.astype(BF16)
        bit *= 2
    errors = (part + shift).astype(BF16)
    blocks = [errors] + [exchange(errors, step * k) for k in range(1, outer)]
    blocks += [exchange(block, 1) for block in blocks]

    def gradients(*refs):
        gradients_kernel(len(blocks), inner, float(tokens * feature), *refs)

    any_space = pl.BlockSpec(memory_space=pl.ANY)
    enc_grad, dec_grad, enc_bias_grad, dec_bias_grad, mean_loss, errors_own = call(
        gradients,
        "gradients",
        (
            shape((feature, latents), BF16),
            shape((latents, feature), BF16),
            shape((1, latents), F32),
            shape((feature,), F32),
            shape((1,), F32),
            shape((ROWS_DEV, feature), BF16),
        ),
        [vmem()] * (len(blocks) + 6),
        (any_space, any_space, vmem(), vmem(), smem(), vmem()),
        [
            pltpu.VMEM((feature, latents), BF16),
            pltpu.VMEM((latents, feature), BF16),
            pltpu.SemaphoreType.DMA((8,)),
        ],
        flops=6 * tokens * feature * latents,
        moved=8 * dec_weight.size,
    )(
        *[near(block) for block in blocks],
        decoder,
        near(weights_sum),
        near(inputs_t),
        near(latent_t),
        near(latent),
        near(scale),
    )
    return (
        enc_grad,
        dec_grad,
        enc_bias_grad.reshape(latents),
        dec_bias_grad,
        mean_loss,
        errors_own,
    )


def solution(mesh):
    return jax.shard_map(
        shards,
        mesh=mesh,
        in_specs=(
            P(("groups", "utt"), None),
            P(("groups", "utt")),
            P(("groups", "utt")),
            P(),
            P(),
            P(),
            P(),
            P(None, "utt"),
            P("utt"),
            P("utt", None),
            P(),
        ),
        out_specs=(
            P("groups", "utt"),
            P(("groups", "utt"), None),
            P(("groups", "utt")),
            P("groups"),
            P("groups"),
            P(("groups", "utt"), None),
        ),
        check_vma=False,
    )
```
